32 devices in a mesh: seq: 8 (over z, x), fsdp: 4 (over y, core).
Axes of the slice: x: 2, y: 2, z: 4, core: 2. Of those that a mesh axis runs over, the one named last changes fastest.
Arguments:
- tokens: bfloat16 [4, 2048, 1536], P('fsdp', 'seq'), may hold values from -6 to 6
- lengths: int32 [4], P('fsdp'), may hold values from 512 to 2048, as said below
- norm_gain: bfloat16 [1536], P('fsdp'), may hold values from 0.099609375 to 1.8984375
- in_weight: bfloat16 [1536, 6448], P('fsdp'), may hold values from -0.15625 to 0.15625
- conv_weight: bfloat16 [4, 3328], P(None, 'fsdp'), may hold values from -3 to 3
- conv_bias: bfloat16 [3328], P('fsdp'), may hold values from -0.5 to 0.5
- dt_bias: bfloat16 [48], P('fsdp'), may hold values from -4.5 to -3.5
- decay_log: bfloat16 [48], P('fsdp'), may hold values from -9 to 0
- skip_gain: bfloat16 [48], P('fsdp'), may hold values from 0.5 to 1.5
- gated_gain: bfloat16 [3072], P('fsdp'), may hold values from 0.099609375 to 1.8984375
- out_weight: bfloat16 [3072, 1536], P('fsdp'), may hold values from -0.109375 to 0.109375
- cotangent: bfloat16 [4, 2048, 1536], P('fsdp', 'seq'), may hold values from -6 to 6
Outputs:
- mixed: bfloat16 [4, 2048, 1536], P('fsdp', 'seq')
- input_grad: float32 [4, 2048, 1536], P('fsdp', 'seq')
- norm_gain_grad: float32 [1536], P('fsdp')
- in_weight_grad: float32 [1536, 6448], P('fsdp')
- conv_weight_grad: float32 [4, 3328], P(None, 'fsdp')
- conv_bias_grad: float32 [3328], P('fsdp')
- dt_bias_grad: float32 [48], P('fsdp')
- decay_log_grad: float32 [48], P('fsdp')
- skip_gain_grad: float32 [48], P('fsdp')
- gated_gain_grad: float32 [3072], P('fsdp')
- out_weight_grad: float32 [3072, 1536], P('fsdp')
The draws below stay inside these ranges and needn't reach their ends.
Inputs may be any that keep to these rules, and one draw needn't show every extreme that they name: `lengths`: each slot's valid positions come first; some slot has all 2048 valid.
All inputs are finite; a program needn't handle non-finite values.
Results may differ from the reference program's by a relative error of at most 0.012.
The reference program's roundings to bfloat16 on the way count: a program that leaves them out, or rounds other values in their place, can miss the bound.
Values may be sent and summed in bfloat16 or wider, within the bound.
No kernel may reach another device: no remote copies, remote signals or barrier semaphores. Data moves between devices by JAX's collectives and lax.ppermute only.
A program may use at most 256 MiB of HBM per device.

```python
import math
import jax
import jax.numpy as jnp
from jax import lax

D = 1536
CONV = 4
INNER = 3072
HEADS = 48
XBC = 3328
PROJ = 6448
LENGTH = 2048
SLOTS = 4


def draw_lengths(key, part):
    first_key, second_key = jax.random.split(jax.random.fold_in(key, 17))
    drawn = jax.random.randint(first_key, (SLOTS,), LENGTH // 4, LENGTH + 1)
    chosen = jax.random.randint(second_key, (), 0, SLOTS)
    return jnp.where(jnp.arange(SLOTS) == chosen, LENGTH, drawn).astype(jnp.int32)


def steps_of(rng, extent, cuts, low, high):
    def one(position, shards_of):
        heights = jax.random.uniform(jax.random.fold_in(jax.random.fold_in(rng, 6), position), (shards_of,), jnp.float32, low / len(cuts), high / len(cuts))
        return jnp.repeat(jnp.exp(heights), extent[position] // shards_of).reshape((-1,) + (1,) * (len(extent) - position - 1))

    loudness = one(*cuts[0])
    for cut in cuts[1:]:
        loudness = loudness * one(*cut)
    return loudness


def gaussian(own_key, dims, scale, limit, cuts=(), kind=jnp.bfloat16):
    gain = steps_of(own_key, dims, cuts, -0.22, 0.18) if cuts else 1.0
    array = jax.random.normal(own_key, dims, jnp.float32) * scale * gain
    return jnp.minimum(jnp.maximum(array, -limit), limit).astype(kind)


def setup_inputs(seed: int = 0) -> dict:
    streams_of = jax.random.split(jax.random.key(seed), 13)
    tokens = gaussian(streams_of[0], (SLOTS, LENGTH, D), 1.0, 6.0, ((0, 4), (1, 8)))
    lengths = draw_lengths(jax.random.fold_in(streams_of[12], 71), 0)
    norm_gain = jnp.clip(1.0 + 0.18 * jax.random.normal(streams_of[2], (D,), jnp.float32), 0.099609375, 1.8984375).astype(jnp.bfloat16)
    in_weight = gaussian(streams_of[3], (D, PROJ), D ** -0.5, 0.15625, ((0, 4),))
    conv_weight = gaussian(streams_of[4], (CONV, XBC), CONV ** -0.5, 3.0, ((1, 4),))
    conv_bias = jnp.clip(jax.random.uniform(streams_of[5], (XBC,), jnp.float32, -0.5, 0.5) * steps_of(streams_of[5], (XBC,), ((0, 4),), -0.4, 0.0), -0.5, 0.5).astype(jnp.bfloat16)
    dt_bias = jnp.clip(-4.5 + 1.0 * jax.random.uniform(streams_of[6], (HEADS,), jnp.float32) ** steps_of(streams_of[6], (HEADS,), ((0, 4),), -0.2, 0.2), -4.5, -3.5).astype(jnp.bfloat16)
    decay_log = jnp.clip(-9.0 + 9.0 * jax.random.uniform(streams_of[7], (HEADS,), jnp.float32) ** steps_of(streams_of[7], (HEADS,), ((0, 4),), -0.2, 0.2), -9.0, 0.0).astype(jnp.bfloat16)
    skip_gain = jnp.clip(0.5 + 1.0 * jax.random.uniform(streams_of[8], (HEADS,), jnp.float32) ** steps_of(streams_of[8], (HEADS,), ((0, 4),), -0.2, 0.2), 0.5, 1.5).astype(jnp.bfloat16)
    gated_gain = jnp.clip(1.0 + 0.18 * jax.random.normal(streams_of[9], (INNER,), jnp.float32), 0.099609375, 1.8984375).astype(jnp.bfloat16)
    out_weight = gaussian(streams_of[10], (INNER, D), INNER ** -0.5, 0.109375, ((0, 4),))
    cotangent = gaussian(streams_of[11], (SLOTS, LENGTH, D), 1.0, 6.0, ((0, 4), (1, 8)))
    return {"tokens": tokens, "lengths": lengths, "norm_gain": norm_gain, "in_weight": in_weight, "conv_weight": conv_weight, "conv_bias": conv_bias, "dt_bias": dt_bias, "decay_log": decay_log, "skip_gain": skip_gain, "gated_gain": gated_gain, "out_weight": out_weight, "cotangent": cotangent}


epsilon = 1e-05
highest = lax.Precision.HIGHEST

@jax.custom_vjp
def low(v):
    return lax.optimization_barrier(v.astype(jnp.bfloat16)).astype(jnp.float32)

@jax.custom_vjp
def low_back(v):
    return v

def low_keep(v):
    return (low(v), None)

def low_pass(kept, grad):
    return (grad,)

def back_keep(v):
    return (v, None)

def back_low(kept, grad):
    return (low(grad),)
low.defvjp(low_keep, low_pass)
low_back.defvjp(back_keep, back_low)

def ssd_block(values, b_rows, c_rows, step_size, rates):
    log_decay = jnp.cumsum(-step_size * rates, axis=0)
    count = values.shape[0]
    places = jnp.arange(count)
    lower = (places[:, None] >= places[None, :])[:, :, None]
    gaps = log_decay[:, None, :] - log_decay[None, :, :]
    weights = jnp.where(lower, jnp.exp(jnp.where(lower, gaps, 0.0)), 0.0)
    intersection = jnp.dot(c_rows, b_rows.T, precision=highest)
    mixing = weights * intersection[:, :, None] * step_size[None, :, :]
    local_out = jnp.einsum('tuh,uhp->thp', mixing, values, precision=highest)
    to_end = jnp.exp(log_decay[-1][None, :] - log_decay) * step_size
    local_state = jnp.einsum('qh,qhp,qn->hpn', to_end, values, b_rows, precision=highest)
    return (local_out, local_state, jnp.exp(log_decay[-1]), jnp.exp(log_decay))

def slot_forward(inputs, valid, params):
    norm_g, w_in, conv_w, conv_b, dt_b, decay_l, skip_g, gated_g, w_out = params
    count = inputs.shape[0]
    inner = w_out.shape[0]
    heads = dt_b.shape[0]
    head_size = inner // heads
    conv_width = conv_w.shape[1]
    state_width = (conv_width - inner) // 2
    taps = conv_w.shape[0]
    inv_rms = lax.rsqrt(lax.optimization_barrier(jnp.mean(inputs * inputs, axis=-1, keepdims=True)) + epsilon)
    normed = low(inputs * inv_rms * norm_g)
    projected = low_back(low(jnp.dot(normed, w_in, precision=highest)))
    gate_part = projected[:, :inner]
    conv_in = projected[:, inner:inner + conv_width]
    step_raw = projected[:, inner + conv_width:]
    extended = jnp.concatenate([jnp.zeros((taps - 1, conv_width), jnp.float32), conv_in], axis=0)
    summed = conv_b[None, :] + jnp.zeros((count, conv_width), jnp.float32)
    for offset in range(taps):
        summed = summed + extended[offset:offset + count] * conv_w[offset][None, :]
    activated = low(jax.nn.silu(summed))
    values = activated[:, :inner].reshape(count, heads, head_size)
    b_rows = activated[:, inner:inner + state_width]
    c_rows = activated[:, inner + state_width:]
    step_size = jax.nn.softplus(step_raw + dt_b)
    rates = jnp.exp(decay_l)
    block_len = math.gcd(256, count)
    blocks = count // block_len

    def advance(carried, pieces):
        vals, brow, crow, steps_b = pieces
        local_out, local_state, whole_decay, decay_in = ssd_block(vals, brow, crow, steps_b, rates)
        carried_out = decay_in[:, :, None] * jnp.einsum('qn,hpn->qhp', crow, carried, precision=highest)
        return (whole_decay[:, None, None] * carried + local_state, local_out + carried_out)
    final_state, heads_out = lax.scan(jax.checkpoint(advance), jnp.zeros((heads, head_size, state_width), jnp.float32), (values.reshape(blocks, block_len, heads, head_size), b_rows.reshape(blocks, block_len, state_width), c_rows.reshape(blocks, block_len, state_width), step_size.reshape(blocks, block_len, heads)))
    mixed_heads = heads_out.reshape(count, heads, head_size) + skip_g[None, :, None] * values
    gated = mixed_heads.reshape(count, inner) * jax.nn.silu(gate_part)
    inv_gated = lax.rsqrt(lax.optimization_barrier(jnp.mean(gated * gated, axis=-1, keepdims=True)) + epsilon)
    gated_out = low(gated * inv_gated * gated_g)
    branch = jnp.dot(gated_out, w_out, precision=highest)
    return valid[:, None] * (inputs + branch)

def reference(tokens, lengths, norm_gain, in_weight, conv_weight, conv_bias, dt_bias, decay_log, skip_gain, gated_gain, out_weight, cotangent):
    weights_all = tuple((item.astype(jnp.float32) for item in (norm_gain, in_weight, conv_weight, conv_bias, dt_bias, decay_log, skip_gain, gated_gain, out_weight)))
    inputs = tokens.astype(jnp.float32)
    valid = (jnp.arange(LENGTH)[None, :] < lengths[:, None]).astype(jnp.float32)

    def layer_all(inputs_all, *params):

        def per_slot(pieces):
            return slot_forward(pieces[0], pieces[1], params)
        return lax.map(jax.checkpoint(per_slot), (inputs_all, valid))
    result, pullback = jax.vjp(layer_all, inputs, *weights_all)
    gradients = pullback(cotangent.astype(jnp.float32))
    return (result.astype(jnp.bfloat16), gradients[0], gradients[1], gradients[2], gradients[3], gradients[4], gradients[5], gradients[6], gradients[7], gradients[8], gradients[9])
```

```python
import functools

import jax
import jax.numpy as jnp
from jax import lax
from jax.experimental import pallas as pl
from jax.experimental.pallas import tpu as pltpu
from jax.sharding import PartitionSpec as P

epsilon = 1e-05
bf16, f32 = jnp.bfloat16, jnp.float32
best = lax.Precision.HIGHEST
halo = 16
lanes = 128
head_size = 64


def dot(a, b, ca=1, cb=0, precision=None):
    return lax.dot_general(
        a, b, (((ca,), (cb,)), ((), ())), preferred_element_type=f32, precision=precision
    )


def sigmoid(v):
    return 1.0 / (1.0 + jnp.exp(-v))


def iota(shape, axis):
    return lax.broadcasted_iota(jnp.int32, shape, axis)


def spread(columns, pair):
    first, second = 2 * pair, 2 * pair + 1
    rows = columns.shape[0]
    return jnp.where(
        iota((rows, lanes), 1) < head_size,
        columns[:, first : first + 1],
        columns[:, second : second + 1],
    )


def of_heads(pair):
    return (iota((lanes, lanes), 1) == 2 * pair + iota((lanes, lanes), 0) // head_size).astype(f32)


def convolved(pc_ref, taps_ref, at):
    x = pc_ref[0, :, at : at + lanes].astype(f32)
    tapped = [pltpu.roll(x, 3 - k, 0)[halo:] for k in range(3)] + [x[halo:]]
    pre = taps_ref[4:5, at : at + lanes]
    for k in range(4):
        pre = pre + tapped[k] * taps_ref[k : k + 1, at : at + lanes]
    return tapped, pre


def forward_kernel(pc_ref, taps_ref, rate_ref, act_ref, y_ref, s_ref, lac_ref, dtc_ref, lar_ref, dtr_ref, *, channels, state):
    width = channels + 2 * state
    for at in range(0, width, lanes):
        _, pre = convolved(pc_ref, taps_ref, at)
        act_ref[0, :, at : at + lanes] = (pre * sigmoid(pre)).astype(bf16)
    seg = act_ref.shape[1]
    z = pc_ref[0, halo:, width : width + lanes].astype(f32) + rate_ref[0:1]
    dtc = jnp.maximum(z, 0.0) + jnp.log1p(jnp.exp(-jnp.abs(z)))
    lower = iota((seg, seg), 0) >= iota((seg, seg), 1)
    lac = dot(lower.astype(f32), -dtc * rate_ref[1:2], precision=best)
    rows = lar_ref.shape[1]
    lar, dtr = lac.T[:rows], dtc.T[:rows]
    lac_ref[0], dtc_ref[0], lar_ref[0], dtr_ref[0] = lac, dtc, lar, dtr
    b_rows = act_ref[0, :, channels : channels + state]
    c_rows = act_ref[0, :, channels + state : width]
    both = dot(c_rows, b_rows, 1, 1)
    to_end = jnp.exp(lac[seg - 1 : seg] - lac) * dtc
    for pair in range(channels // lanes):
        at = pair * lanes
        values = act_ref[0, :, at : at + lanes]
        parts = []
        for side in range(2):
            h = 2 * pair + side
            mix = jnp.where(lower, jnp.exp(lac[:, h : h + 1] - lar[h : h + 1]), 0.0) * both * dtr[h : h + 1]
            parts.append(dot(mix.astype(bf16), values[:, side * head_size : (side + 1) * head_size]))
        y_ref[0, :, at : at + lanes] = jnp.concatenate(parts, axis=1)
        weighted = (spread(to_end, pair) * values.astype(f32)).astype(bf16)
        s_ref[0, at : at + lanes] = dot(weighted, b_rows, 0, 0).astype(bf16)


def finish_kernel(y_ref, act_ref, lac_ref, sin_ref, gate_ref, bg_ref, vec_ref, y_out, stat_ref, *, channels, state):
    seg = y_ref.shape[1]
    c_rows = act_ref[0, :, channels + state : channels + 2 * state]
    decay = jnp.exp(lac_ref[0])
    first = jnp.zeros((seg, 1), f32)
    second = jnp.zeros((seg, 1), f32)
    for pair in range(channels // lanes):
        at = pair * lanes
        here = slice(at, at + lanes)
        carried = dot(c_rows, sin_ref[0, here], 1, 1)
        y = y_ref[0, :, here] + spread(decay, pair) * carried
        y_out[0, :, here] = y
        gate = gate_ref[0, :, here].astype(f32)
        heads = y + vec_ref[0:1, here] * act_ref[0, :, here].astype(f32)
        gated = heads * gate * sigmoid(gate)
        first = first + jnp.sum(gated * gated, axis=1, keepdims=True)
        second = second + jnp.sum(gated * bg_ref[0, :, here] * vec_ref[1:2, here], axis=1, keepdims=True)
    lane = iota((seg, lanes), 1)
    both = jnp.where(lane == 0, first, jnp.where(lane == 1, second, 0.0))
    stat_ref[0] = both.T[:8]


def norm_kernel(y_ref, act_ref, lac_ref, gate_ref, bg_ref, vec_ref, stat_ref, out_ref, dgate_ref, dy_ref, pos_ref, dsin_ref, dskip_ref, *, channels, state, inner):
    seg = y_ref.shape[1]
    stats = stat_ref[0].T
    inv = lax.rsqrt(stats[:, 0:1] * (1.0 / inner) + epsilon)
    lean = inv * inv * inv * (stats[:, 1:2] * (1.0 / inner))
    c_rows = act_ref[0, :, channels + state : channels + 2 * state]
    decay = jnp.exp(lac_ref[0])
    pos = jnp.zeros((seg, lanes), f32)

    @pl.when(pl.program_id(0) == 0)
    def _():
        dskip_ref[...] = jnp.zeros_like(dskip_ref)

    for pair in range(channels // lanes):
        at = pair * lanes
        here = slice(at, at + lanes)
        y = y_ref[0, :, here]
        values = act_ref[0, :, here].astype(f32)
        heads = y + vec_ref[0:1, here] * values
        gate = gate_ref[0, :, here].astype(f32)
        sg = sigmoid(gate)
        gated = heads * gate * sg
        gain = vec_ref[1:2, here]
        out_ref[0, :, here] = (gated * inv * gain).astype(bf16)
        dgated = inv * (bg_ref[0, :, here] * gain) - gated * lean
        dgate_ref[0, :, here] = (dgated * heads * (sg * (1.0 + gate * (1.0 - sg)))).astype(bf16)
        dy = dgated * gate * sg
        dy_ref[0, :, here] = dy
        pos = pos + dot(dy * y, of_heads(pair), precision=best)
        dsin_ref[0, here] = dot((spread(decay, pair) * dy).astype(bf16), c_rows, 0, 0).astype(bf16)
        dskip_ref[0:1, here] += jnp.sum(dy * values, axis=0, keepdims=True)
    pos_ref[0] = pos


def backward_kernel(act_ref, dy_ref, lac_ref, lar_ref, dtr_ref, sin_ref, r_ref, dbc_ref, *, channels, state):
    seg = dy_ref.shape[1]
    b_rows = act_ref[0, :, channels : channels + state]
    c_rows = act_ref[0, :, channels + state : channels + 2 * state]
    both = dot(c_rows, b_rows, 1, 1)
    lower = iota((seg, seg), 0) >= iota((seg, seg), 1)
    lac, lar, dtr = lac_ref[0], lar_ref[0], dtr_ref[0]
    decay = jnp.exp(lac)
    dboth = jnp.zeros((seg, seg), f32)
    dc = jnp.zeros((seg, state), f32)
    for pair in range(channels // lanes):
        at = pair * lanes
        here = slice(at, at + lanes)
        values = act_ref[0, :, here]
        dy = dy_ref[0, :, here]
        dyl = dy.astype(bf16)
        parts = []
        for side in range(2):
            h = 2 * pair + side
            own = slice(side * head_size, (side + 1) * head_size)
            weights = jnp.where(lower, jnp.exp(lac[:, h : h + 1] - lar[h : h + 1]), 0.0)
            parts.append(dot((weights * both).astype(bf16), dyl[:, own], 0, 0))
            dboth = dboth + dot(dyl[:, own], values[:, own], 1, 1) * (weights * dtr[h : h + 1])
        r_ref[0, :, here] = jnp.concatenate(parts, axis=1)
        dc = dc + dot((spread(decay, pair) * dy).astype(bf16), sin_ref[0, here])
    dlow = dboth.astype(bf16)
    dbc_ref[0, :, :state] = dot(dlow, c_rows, 0, 0)
    dbc_ref[0, :, state:] = dc + dot(dlow, b_rows)


def carry_kernel(pc_ref, taps_ref, rate_ref, act_ref, dy_ref, r_ref, pos_ref, lac_ref, dtc_ref, g_ref, sin_ref, s_ref, dbc_ref, vec_ref, dpre_ref, first_ref, dstep_ref, dbc_out, dtaps_ref, drate_ref, *, channels, state):
    seg = dy_ref.shape[1]
    width = channels + 2 * state
    b_rows = act_ref[0, :, channels : channels + state]
    lac, dtc = lac_ref[0], dtc_ref[0]
    last = lac[seg - 1 : seg]
    to_last = jnp.exp(last - lac)
    neg = jnp.zeros((seg, lanes), f32)
    db = jnp.zeros((seg, state), f32)
    through = jnp.zeros((1, lanes), f32)
    local = jnp.zeros((1, lanes), f32)

    @pl.when(pl.program_id(0) == 0)
    def _():
        dtaps_ref[...] = jnp.zeros_like(dtaps_ref)
        drate_ref[...] = jnp.zeros_like(drate_ref)

    for pair in range(channels // lanes):
        at = pair * lanes
        here = slice(at, at + lanes)
        grad = g_ref[0, here]
        values = act_ref[0, :, here].astype(f32)
        reach = spread(to_last, pair)
        step = spread(dtc, pair)
        r = r_ref[0, :, here] + reach * dot(b_rows, grad, 1, 1)
        owners = of_heads(pair)
        neg = neg + dot(values * r, owners, precision=best)
        db = db + dot((reach * step * values).astype(bf16), grad)
        wide = grad.astype(f32)
        through = through + jnp.sum(dot(wide * sin_ref[0, here].astype(f32), owners, 0, 0, best), axis=0, keepdims=True)
        local = local + jnp.sum(dot(wide * s_ref[0, here].astype(f32), owners, 0, 0, best), axis=0, keepdims=True)
        tapped, pre = convolved(pc_ref, taps_ref, at)
        sg = sigmoid(pre)
        dpre = (step * r + vec_ref[0:1, here] * dy_ref[0, :, here]) * (sg * (1.0 + pre * (1.0 - sg)))
        dpre_ref[0, :, here] = dpre
        for k in range(4):
            dtaps_ref[k : k + 1, here] += jnp.sum(dpre * tapped[k], axis=0, keepdims=True)
        dtaps_ref[4:5, here] += jnp.sum(dpre, axis=0, keepdims=True)
    first_ref[0] = dpre_ref[0, :8]
    dbc_out[0, :, :state] = dbc_ref[0, :, :state] + db
    dbc_out[0, :, state:] = dbc_ref[0, :, state:]
    seed = jnp.exp(last) * through + local
    upper = (iota((seg, seg), 0) <= iota((seg, seg), 1)).astype(f32)
    q = dot(upper, pos_ref[0] - dtc * neg, precision=best) + seed
    rates = rate_ref[1:2]
    z = pc_ref[0, halo:, width : width + lanes].astype(f32) + rate_ref[0:1]
    draw = (neg - rates * q) * sigmoid(z)
    dstep_ref[0] = draw.astype(bf16)
    drate_ref[0:1] += jnp.sum(draw, axis=0, keepdims=True)
    drate_ref[1:2] += jnp.sum(q * (-dtc * rates), axis=0, keepdims=True)


def returned_kernel(dpre_ref, next_ref, taps_ref, out_ref):
    seg = dpre_ref.shape[1]
    for at in range(0, dpre_ref.shape[2], lanes):
        here = slice(at, at + lanes)
        x = jnp.concatenate([dpre_ref[0, :, here], next_ref[0, :, here]], axis=0)
        total = x[:seg] * taps_ref[3:4, here]
        for k in range(3):
            by = 3 - k
            total = total + pltpu.roll(x, seg + 8 - by, 0)[:seg] * taps_ref[k : k + 1, here]
        out_ref[0, :, here] = total.astype(bf16)


def call(kernel, slots, ins, outs, name, flops=0, **statics):
    def spec(shape, per):
        if per:
            return pl.BlockSpec((1,) + tuple(shape[1:]), lambda s: (s,) + (0,) * (len(shape) - 1))
        return pl.BlockSpec(tuple(shape), lambda s: (0,) * len(shape))

    moved = sum(a.size * a.dtype.itemsize for a, _ in ins)
    for shape, dtype, _ in outs:
        size = 1
        for d in shape:
            size *= d
        moved += size * jnp.dtype(dtype).itemsize
    return pl.pallas_call(
        functools.partial(kernel, **statics),
        grid=(slots,),
        in_specs=[spec(a.shape, per) for a, per in ins],
        out_specs=[spec(shape, per) for shape, _, per in outs],
        out_shape=[jax.ShapeDtypeStruct(shape, dtype) for shape, dtype, _ in outs],
        compiler_params=pltpu.CompilerParams(vmem_limit_bytes=40 << 20),
        cost_estimate=pl.CostEstimate(flops=flops, bytes_accessed=moved, transcendentals=0),
        name=name,
    )(*[a for a, _ in ins])


def swap(value, axis, by):
    count = lax.axis_size(axis)
    return lax.ppermute(value, axis, [(i, i ^ by) for i in range(count)])


def all_slots(value, axis):
    count = lax.axis_size(axis)
    pieces, by = {0: value}, count // 2
    while by:
        for j in list(pieces):
            pieces[j ^ by] = swap(pieces[j], axis, by)
        by //= 2
    return jnp.concatenate([pieces[j] for j in range(count)], axis=0)


def to_owner(parts, axis):
    count = lax.axis_size(axis)
    parts, by = list(parts), 1
    left = list(range(count))
    while by < count:
        keep = [j for j in left if not j & by]
        new = {}
        for j in keep:
            new[j] = parts[j] + swap(parts[j ^ by].astype(bf16), axis, by).astype(f32)
        parts = [new.get(j) for j in range(count)]
        left = keep
        by *= 2
    return parts[0]


def over_owners(value, axis):
    count, by = lax.axis_size(axis), 1
    while by < count:
        other = swap(value, axis, by)
        value = value + jnp.stack([other[j ^ by] for j in range(count)])
        by *= 2
    return value


def exchange(value, axis):
    return lax.all_to_all(value, axis, 0, 0)


def per_device(tokens, lengths, norm_gain, in_weight, conv_weight, conv_bias, dt_bias, decay_log, skip_gain, gated_gain, out_weight, cotangent):
    nf, nq = lax.axis_size("fsdp"), lax.axis_size("seq")
    me, place = lax.axis_index("fsdp"), lax.axis_index("seq")
    _, seg, width = tokens.shape
    rows = in_weight.shape[0]
    channels = out_weight.shape[0]
    inner = channels * nf
    heads = dt_bias.shape[0]
    conv_own = conv_weight.shape[1]
    state = (conv_own * nf - inner) // 2
    share = 2 * state // nf
    slots = nf

    small = jnp.concatenate([conv_weight, conv_bias[None]], axis=0)
    small = jnp.pad(small, ((0, 3), (0, 0)))
    norm_all = lax.all_gather(norm_gain, "fsdp", axis=0, tiled=True).astype(f32)
    taps_all = lax.all_gather(small, "fsdp", axis=1, tiled=True).astype(f32)
    taps = jnp.concatenate([lax.dynamic_slice_in_dim(taps_all, me * channels, channels, 1), taps_all[:, inner:]], axis=1)
    taps_share = lax.dynamic_slice_in_dim(taps_all, inner + me * share, share, 1)
    rate = jnp.stack([dt_bias.astype(f32), jnp.exp(decay_log.astype(f32))])
    rate = jnp.pad(rate, ((0, 6), (0, lanes - heads)))
    vec = jnp.stack([jnp.repeat(skip_gain.astype(f32), head_size), gated_gain.astype(f32)])
    vec = jnp.pad(vec, ((0, 6), (0, 0)))

    w_value = in_weight[:, inner : 2 * inner].reshape(rows, nf, channels)
    w_rows = jnp.broadcast_to(in_weight[:, 2 * inner : 2 * inner + 2 * state][:, None], (rows, nf, 2 * state))
    w_step = jnp.pad(in_weight[:, 2 * inner + 2 * state :].reshape(rows, nf, heads), ((0, 0), (0, 0), (0, lanes - heads)))
    w_conv = jnp.concatenate([w_value, w_rows, w_step], axis=2).transpose(1, 0, 2)
    w_conv = exchange(w_conv, "fsdp").reshape(width, -1)

    inputs = tokens[0].astype(f32)
    inv = lax.rsqrt(jnp.mean(inputs * inputs, axis=-1, keepdims=True) + epsilon)
    normed_own = (inputs * inv * norm_all).astype(bf16)
    before = lax.ppermute(normed_own[seg - halo :], "seq", [(i, i + 1) for i in range(nq - 1)])
    normed = all_slots(jnp.concatenate([before, normed_own], axis=0)[None], "fsdp")

    valid = (place * seg + jnp.arange(seg) < lengths[0]).astype(f32)[:, None]
    upstream = valid * cotangent[0].astype(f32)
    w_gate = in_weight[:, :inner].reshape(rows, nf, channels).transpose(1, 0, 2)
    w_gate, later, _ = lax.optimization_barrier((w_gate, upstream.astype(bf16), w_conv))
    w_gate = exchange(w_gate, "fsdp").reshape(width, channels)
    back_branch = all_slots(later[None], "fsdp")

    def project(x, w):
        return lax.dot_general(x, w, (((2,), (0,)), ((), ())), preferred_element_type=f32)

    pc = project(normed, w_conv).astype(bf16)
    main = normed[:, halo:]
    cw = channels + 2 * state
    raw = pc[:, halo:, cw:].astype(f32) + rate[0]
    total = jnp.sum(jax.nn.softplus(raw), axis=1)[:, :heads] * -rate[1, :heads]
    piece = slots * channels // nq
    whole = jnp.repeat(jnp.exp(total).reshape(-1), head_size).reshape(nq, piece)
    whole = exchange(whole, "seq")[..., None]

    tall = 16
    statics = dict(channels=channels, state=state)
    act, y_local, s_local, lac, dtc, lar, dtr = call(
        forward_kernel,
        slots,
        [(pc, True), (taps, False), (rate, False)],
        [
            ((slots, seg, cw), bf16, True),
            ((slots, seg, channels), f32, True),
            ((slots, channels, state), bf16, True),
            ((slots, seg, lanes), f32, True),
            ((slots, seg, lanes), f32, True),
            ((slots, tall, seg), f32, True),
            ((slots, tall, seg), f32, True),
        ],
        "forward",
        flops=2 * slots * seg * seg * channels,
        **statics,
    )
    everything = exchange(s_local.reshape(nq, piece, state), "seq").astype(f32)
    carried, reached = jnp.zeros((piece, state), f32), []
    for i in range(nq):
        reached.append(carried.astype(bf16))
        carried = whole[i] * carried + everything[i]
    s_in = exchange(jnp.stack(reached), "seq").reshape(slots, channels, state)

    gate = project(main, w_gate).astype(bf16)
    bg = lax.dot_general(back_branch, out_weight, (((2,), (1,)), ((), ())), preferred_element_type=f32)
    y, stats = call(
        finish_kernel,
        slots,
        [(y_local, True), (act, True), (lac, True), (s_in, True), (gate, True), (bg, True), (vec, False)],
        [((slots, seg, channels), f32, True), ((slots, 8, seg), f32, True)],
        "finish",
        **statics,
    )
    stats = over_owners(stats, "fsdp")
    gated_out, dgate, dy, pos, dsin, dskip = call(
        norm_kernel,
        slots,
        [(y, True), (act, True), (lac, True), (gate, True), (bg, True), (vec, False), (stats, True)],
        [
            ((slots, seg, channels), bf16, True),
            ((slots, seg, channels), bf16, True),
            ((slots, seg, channels), f32, True),
            ((slots, seg, lanes), f32, True),
            ((slots, channels, state), bf16, True),
            ((8, channels), f32, False),
        ],
        "norm",
        inner=inner,
        **statics,
    )
    everything = exchange(dsin.reshape(nq, piece, state), "seq").astype(f32)
    carried, reached = jnp.zeros((piece, state), f32), [None] * nq
    for i in reversed(range(nq)):
        reached[i] = carried.astype(bf16)
        carried = whole[i] * carried + everything[i]
    g_end = exchange(jnp.stack(reached), "seq").reshape(slots, channels, state)

    r_local, dbc = call(
        backward_kernel,
        slots,
        [(act, True), (dy, True), (lac, True), (lar, True), (dtr, True), (s_in, True)],
        [((slots, seg, channels), f32, True), ((slots, seg, 2 * state), f32, True)],
        "backward",
        flops=4 * slots * seg * seg * channels,
        **statics,
    )
    dpre, first, dstep, dbc, dtaps, drate = call(
        carry_kernel,
        slots,
        [
            (pc, True), (taps, False), (rate, False), (act, True), (dy, True), (r_local, True), (pos, True),
            (lac, True), (dtc, True), (g_end, True), (s_in, True), (s_local, True), (dbc, True), (vec, False),
        ],
        [
            ((slots, seg, channels), f32, True),
            ((slots, 8, channels), f32, True),
            ((slots, seg, lanes), bf16, True),
            ((slots, seg, 2 * state), f32, True),
            ((8, channels), f32, False),
            ((8, lanes), f32, False),
        ],
        "carry",
        **statics,
    )
    behind = [(i, i - 1) for i in range(1, nq)]
    after = lax.ppermute(first, "seq", behind)
    (dvalue,) = call(
        returned_kernel,
        slots,
        [(dpre, True), (after, True), (taps[:, :channels], False)],
        [((slots, seg, channels), bf16, True)],
        "returned",
    )

    mine = dbc.astype(bf16).reshape(slots, seg, nf, share)
    d_act = None
    for j in range(nf):
        part = lax.dynamic_index_in_dim(mine, me ^ j, 2, False)
        part = swap(part, "fsdp", j) if j else part
        part = jnp.stack([part[m ^ j] for m in range(slots)]).astype(f32)
        d_act = part if d_act is None else d_act + part
    xs = lax.dynamic_slice_in_dim(pc, channels + me * share, share, 2)[:, halo - 3 :].astype(f32)
    tapped = [xs[:, k : k + seg] for k in range(4)]
    pre = taps_share[4] + sum(tapped[k] * taps_share[k] for k in range(4))
    sg = sigmoid(pre)
    dpre_s = d_act * (sg * (1.0 + pre * (1.0 - sg)))
    dtaps_s = jnp.stack([jnp.sum(dpre_s * t, axis=(0, 1)) for t in tapped] + [jnp.sum(dpre_s, axis=(0, 1))])
    after_s = lax.ppermute(dpre_s[:, :3], "seq", behind)
    longer = jnp.concatenate([dpre_s, after_s], axis=1)
    dshare = sum(longer[:, 3 - k : 3 - k + seg] * taps_share[k] for k in range(4)).astype(bf16)
    dlast = jnp.concatenate([dshare, dstep[..., :heads]], axis=2)

    def grad_of(x, dz):
        return lax.dot_general(x, dz, (((0, 1), (0, 1)), ((), ())), preferred_element_type=f32)

    per = channels // rows
    block = jnp.concatenate(
        [
            dtaps[:5].T.reshape(per, rows, 5).transpose(1, 0, 2).reshape(rows, 5 * per),
            jnp.pad(dtaps_s.T, ((0, rows - share), (0, 0))),
            jnp.pad(
                jnp.stack([drate[0, :heads], drate[1, :heads], jnp.sum(dskip[0].reshape(heads, head_size), axis=1)], axis=1),
                ((0, rows - heads), (0, 0)),
            ),
        ],
        axis=1,
    )
    extra = block.shape[1]
    block = jnp.pad(block, ((0, 0), (0, lanes - share - heads - extra)))
    gw_last = jnp.concatenate([grad_of(main, dlast), jnp.tile(block, (nf, 1))], axis=1)

    def summed(g):
        g = g.astype(bf16).reshape(nf, nq, rows // nq, -1).transpose(1, 0, 2, 3).reshape(width, -1)
        g = lax.psum_scatter(g, "seq", scatter_dimension=0, tiled=True).reshape(nf, rows // nq, -1)
        g = exchange(g, "fsdp")
        g = lax.all_gather(g, "seq", axis=1)
        return g.reshape(nf, rows, -1)

    g_out = grad_of(gated_out, back_branch).astype(bf16)
    g_out = lax.psum_scatter(g_out, "seq", scatter_dimension=0, tiled=True)
    g_out = lax.all_gather(g_out, "seq", axis=0, tiled=True).astype(f32)
    s_gate = summed(grad_of(main, dgate)).astype(f32)
    s_value = summed(grad_of(main, dvalue)).astype(f32)
    s_last = summed(gw_last).astype(f32)

    def spread_columns(s):
        return s.transpose(1, 0, 2).reshape(rows, -1)

    g_in = jnp.concatenate(
        [
            spread_columns(s_gate),
            spread_columns(s_value),
            spread_columns(s_last[..., :share]),
            spread_columns(s_last[..., share : share + heads]),
        ],
        axis=1,
    )
    got = s_last[..., share + heads : share + heads + extra]
    tap_grads = jnp.concatenate(
        [
            got[..., : 5 * per].reshape(nf, rows, per, 5).transpose(0, 2, 1, 3).reshape(inner, 5),
            got[:, :share, 5 * per : 5 * per + 5].reshape(2 * state, 5),
        ],
        axis=0,
    )
    tap_grads = lax.dynamic_slice_in_dim(tap_grads, me * conv_own, conv_own, 0).T
    head_grads = lax.dynamic_index_in_dim(got, me, 0, False)[:heads, 5 * per + 5 :]

    norm_grad = jnp.sum(g_in * in_weight.astype(f32), axis=1) / norm_gain.astype(f32)
    gated_grad = jnp.sum(g_out * out_weight.astype(f32), axis=1) / gated_gain.astype(f32)

    branch = project(gated_out, out_weight)
    branch = to_owner([branch[j] for j in range(slots)], "fsdp")
    mixed = (valid * (inputs + branch)).astype(bf16)

    w_share = lax.dynamic_slice_in_dim(w_conv, channels + me * share, share, 1)
    w_last = jnp.concatenate([w_share, w_conv[:, cw : cw + heads]], axis=1)

    def back(dz, w):
        return lax.dot_general(dz, w, (((2,), (1,)), ((), ())), preferred_element_type=f32)

    bn = back(dgate, w_gate) + back(dvalue, w_conv[:, :channels]) + back(dlast, w_last)
    bn = to_owner([bn[j] for j in range(slots)], "fsdp") * norm_all
    lean = jnp.mean(bn * inputs, axis=-1, keepdims=True)
    input_grad = upstream + inv * bn - inputs * (inv * inv * inv) * lean
    return (
        mixed[None],
        input_grad[None],
        norm_grad,
        g_in,
        tap_grads[:4],
        tap_grads[4],
        head_grads[:, 0],
        head_grads[:, 1],
        head_grads[:, 2],
        gated_grad,
        g_out,
    )


def solution(mesh):
    whole, rows = P("fsdp", "seq", None), P("fsdp", None)
    one, columns = P("fsdp"), P(None, "fsdp")
    return jax.shard_map(
        per_device,
        mesh=mesh,
        in_specs=(whole, one, one, rows, columns, one, one, one, one, one, rows, whole),
        out_specs=(whole, whole, one, rows, columns, one, one, one, one, one, rows),
        check_vma=False,
    )
```

```python
import functools

import jax
import jax.numpy as jnp
from jax import lax
from jax.experimental import pallas as pl
from jax.experimental.pallas import tpu as pltpu
from jax.sharding import PartitionSpec as P

epsilon = 1e-05
bf16, f32 = jnp.bfloat16, jnp.float32
best = lax.Precision.HIGHEST
halo = 16
lanes = 128
head_size = 64


def dot(a, b, ca=1, cb=0, precision=None):
    return lax.dot_general(
        a, b, (((ca,), (cb,)), ((), ())), preferred_element_type=f32, precision=precision
    )


def sigmoid(v):
    return 1.0 / (1.0 + jnp.exp(-v))


def iota(shape, axis):
    return lax.broadcasted_iota(jnp.int32, shape, axis)


def spread(columns, pair):
    first, second = 2 * pair, 2 * pair + 1
    rows = columns.shape[0]
    return jnp.where(
        iota((rows, lanes), 1) < head_size,
        columns[:, first : first + 1],
        columns[:, second : second + 1],
    )


def per_head(total, products, pair):
    rows = products.shape[0]
    lane = iota((rows, lanes), 1)
    low = jnp.sum(jnp.where(lane < head_size, products, 0.0), axis=1, keepdims=True)
    high = jnp.sum(jnp.where(lane < head_size, 0.0, products), axis=1, keepdims=True)
    return total + jnp.where(lane == 2 * pair, low, jnp.where(lane == 2 * pair + 1, high, 0.0))


def in_heads(products, pair):
    rows = jnp.sum(products, axis=1, keepdims=True)
    low, high = jnp.sum(rows[:head_size]), jnp.sum(rows[head_size:])
    lane = iota((1, lanes), 1)
    return jnp.where(lane == 2 * pair, low, jnp.where(lane == 2 * pair + 1, high, 0.0))


def convolved(pc_ref, taps_ref, at):
    x = pc_ref[0, :, at : at + lanes].astype(f32)
    tapped = [pltpu.roll(x, 3 - k, 0)[halo:] for k in range(3)] + [x[halo:]]
    pre = taps_ref[4:5, at : at + lanes]
    for k in range(4):
        pre = pre + tapped[k] * taps_ref[k : k + 1, at : at + lanes]
    return tapped, pre


def pieces_out(ids_ref, out_ref, whole, rows):
    count = out_ref.shape[0]
    for p in range(count):
        out_ref[p ^ (ids_ref[0] % count), :rows] = whole[p * rows : (p + 1) * rows]


def pieces_in(ids_ref, ref, rows):
    count = ref.shape[0]
    return jnp.concatenate([ref[p ^ (ids_ref[0] % count), :rows] for p in range(count)], axis=0)


def normalize_kernel(main_ref, small_ref, gain_ref, out_ref):
    for ref, at in ((small_ref, 0), (main_ref, halo)):
        x = ref[0].astype(f32)
        inv = lax.rsqrt(jnp.mean(x * x, axis=1, keepdims=True) + epsilon)
        out_ref[0, at : at + x.shape[0]] = (x * inv * gain_ref[...]).astype(bf16)


def of_rows(row, ids_ref, rows, count):
    head = ((ids_ref[0] % count) * rows + iota((rows, lanes), 0)) // head_size
    return jnp.sum(jnp.where(iota((rows, lanes), 1) == head, row, 0.0), axis=1, keepdims=True)


def chain_kernel(ids_ref, *refs, rows, count):
    n = (len(refs) - 3) // 1
    ins, out_ref, decay_ref, hold = refs[:n], refs[n], refs[n + 1], refs[n + 2]
    for j in range(n):
        hold[ids_ref[0] ^ j] = ins[j][...]
    carried = jnp.zeros((rows, lanes), f32)
    for i in range(n):
        out_ref[ids_ref[0] ^ i] = carried.astype(bf16)
        row = hold[i, rows : rows + 1].astype(f32) + hold[i, rows + 1 : rows + 2].astype(f32)
        decay_ref[i] = jnp.broadcast_to(row, (8, lanes))
        carried = of_rows(row, ids_ref, rows, count) * carried + hold[i, :rows].astype(f32)


def back_chain_kernel(ids_ref, *refs, rows, count):
    n = len(refs) - 3
    ins, decay_ref, out_ref, hold = refs[:n], refs[n], refs[n + 1], refs[n + 2]
    for j in range(n):
        hold[ids_ref[0] ^ j] = ins[j][...]
    carried = jnp.zeros((rows, lanes), f32)
    for i in reversed(range(n)):
        out_ref[ids_ref[0] ^ i] = carried.astype(bf16)
        carried = of_rows(decay_ref[i, :1], ids_ref, rows, count) * carried + hold[i].astype(f32)


def order_kernel(ids_ref, *refs):
    for j in range(len(refs) - 1):
        refs[-1][ids_ref[0] ^ j] = refs[j][...]


def forward_kernel(ids_ref, pc_ref, taps_ref, rate_ref, act_ref, y_ref, s_ref, lac_ref, dtc_ref, lar_ref, dtr_ref, *, channels, state, rows):
    width = channels + 2 * state
    for at in range(0, width, lanes):
        _, pre = convolved(pc_ref, taps_ref, at)
        act_ref[0, :, at : at + lanes] = (pre * sigmoid(pre)).astype(bf16)
    seg = act_ref.shape[1]
    z = pc_ref[0, halo:, width : width + lanes].astype(f32) + rate_ref[0:1]
    dtc = jnp.maximum(z, 0.0) + jnp.log1p(jnp.exp(-jnp.abs(z)))
    lower = iota((seg, seg), 0) >= iota((seg, seg), 1)
    lac = dot(lower.astype(f32), -dtc * rate_ref[1:2], precision=best)
    tall = lar_ref.shape[1]
    lar, dtr = lac.T[:tall], dtc.T[:tall]
    lac_ref[0], dtc_ref[0], lar_ref[0], dtr_ref[0] = lac, dtc, lar, dtr
    b_rows = act_ref[0, :, channels : channels + state]
    c_rows = act_ref[0, :, channels + state : width]
    both = dot(c_rows, b_rows, 1, 1)
    to_end = jnp.exp(lac[seg - 1 : seg] - lac) * dtc
    states = []
    for pair in range(channels // lanes):
        at = pair * lanes
        values = act_ref[0, :, at : at + lanes]
        parts = []
        for side in range(2):
            h = 2 * pair + side
            mix = jnp.where(lower, jnp.exp(lac[:, h : h + 1] - lar[h : h + 1]), 0.0) * both * dtr[h : h + 1]
            parts.append(dot(mix.astype(bf16), values[:, side * head_size : (side + 1) * head_size]))
        y_ref[0, :, at : at + lanes] = jnp.concatenate(parts, axis=1)
        weighted = (spread(to_end, pair) * values.astype(f32)).astype(bf16)
        states.append(dot(weighted, b_rows, 0, 0).astype(bf16))
    pieces_out(ids_ref, s_ref, jnp.concatenate(states, axis=0), rows)
    whole = jnp.exp(lac[seg - 1 : seg])
    high = whole.astype(bf16).astype(f32)
    row = iota((16, lanes), 0)
    tail = jnp.where(row == 0, high, jnp.where(row == 1, whole - high, 0.0)).astype(bf16)
    for p in range(s_ref.shape[0]):
        s_ref[p, rows:] = tail


def finish_kernel(y_ref, act_ref, lac_ref, sin_ref, gate_ref, bg_ref, vec_ref, y_out, stat_ref, *, channels, state):
    seg = y_ref.shape[1]
    c_rows = act_ref[0, :, channels + state : channels + 2 * state]
    decay = jnp.exp(lac_ref[0])
    first = jnp.zeros((seg, 1), f32)
    second = jnp.zeros((seg, 1), f32)
    for pair in range(channels // lanes):
        at = pair * lanes
        here = slice(at, at + lanes)
        carried = dot(c_rows, sin_ref[0, here], 1, 1)
        y = y_ref[0, :, here] + spread(decay, pair) * carried
        y_out[0, :, here] = y
        gate = gate_ref[0, :, here].astype(f32)
        heads = y + vec_ref[0:1, here] * act_ref[0, :, here].astype(f32)
        gated = heads * gate * sigmoid(gate)
        first = first + jnp.sum(gated * gated, axis=1, keepdims=True)
        second = second + jnp.sum(gated * bg_ref[0, :, here] * vec_ref[1:2, here], axis=1, keepdims=True)
    lane = iota((seg, lanes), 1)
    both = jnp.where(lane == 0, first, jnp.where(lane == 1, second, 0.0))
    stat_ref[0] = both.T[:8]


def norm_kernel(ids_ref, y_ref, act_ref, lac_ref, gate_ref, bg_ref, vec_ref, *refs, channels, state, inner, rows):
    stat_refs, (out_ref, dgate_ref, dy_ref, pos_ref, dsin_ref, dskip_ref) = refs[:-6], refs[-6:]
    seg = y_ref.shape[1]
    stats = sum(ref[0] for ref in stat_refs).T
    states = []
    inv = lax.rsqrt(stats[:, 0:1] * (1.0 / inner) + epsilon)
    lean = inv * inv * inv * (stats[:, 1:2] * (1.0 / inner))
    c_rows = act_ref[0, :, channels + state : channels + 2 * state]
    decay = jnp.exp(lac_ref[0])
    pos = jnp.zeros((seg, lanes), f32)

    @pl.when(pl.program_id(0) == 0)
    def _():
        dskip_ref[...] = jnp.zeros_like(dskip_ref)

    for pair in range(channels // lanes):
        at = pair * lanes
        here = slice(at, at + lanes)
        y = y_ref[0, :, here]
        values = act_ref[0, :, here].astype(f32)
        heads = y + vec_ref[0:1, here] * values
        gate = gate_ref[0, :, here].astype(f32)
        sg = sigmoid(gate)
        gated = heads * gate * sg
        gain = vec_ref[1:2, here]
        out_ref[0, :, here] = (gated * inv * gain).astype(bf16)
        dgated = inv * (bg_ref[0, :, here] * gain) - gated * lean
        dgate_ref[0, :, here] = (dgated * heads * (sg * (1.0 + gate * (1.0 - sg)))).astype(bf16)
        dy = dgated * gate * sg
        dy_ref[0, :, here] = dy
        pos = per_head(pos, dy * y, pair)
        states.append(dot((spread(decay, pair) * dy).astype(bf16), c_rows, 0, 0).astype(bf16))
        dskip_ref[0:1, here] += jnp.sum(dy * values, axis=0, keepdims=True)
    pos_ref[0] = pos
    pieces_out(ids_ref, dsin_ref, jnp.concatenate(states, axis=0), rows)


def backward_kernel(act_ref, dy_ref, lac_ref, lar_ref, dtr_ref, sin_ref, r_ref, dbc_ref, *, channels, state):
    seg = dy_ref.shape[1]
    b_rows = act_ref[0, :, channels : channels + state]
    c_rows = act_ref[0, :, channels + state : channels + 2 * state]
    both = dot(c_rows, b_rows, 1, 1)
    lower = iota((seg, seg), 0) >= iota((seg, seg), 1)
    lac, lar, dtr = lac_ref[0], lar_ref[0], dtr_ref[0]
    decay = jnp.exp(lac)
    dboth = jnp.zeros((seg, seg), f32)
    dc = jnp.zeros((seg, state), f32)
    for pair in range(channels // lanes):
        at = pair * lanes
        here = slice(at, at + lanes)
        values = act_ref[0, :, here]
        dy = dy_ref[0, :, here]
        dyl = dy.astype(bf16)
        parts = []
        for side in range(2):
            h = 2 * pair + side
            own = slice(side * head_size, (side + 1) * head_size)
            weights = jnp.where(lower, jnp.exp(lac[:, h : h + 1] - lar[h : h + 1]), 0.0)
            parts.append(dot((weights * both).astype(bf16), dyl[:, own], 0, 0))
            dboth = dboth + dot(dyl[:, own], values[:, own], 1, 1) * (weights * dtr[h : h + 1])
        r_ref[0, :, here] = jnp.concatenate(parts, axis=1)
        dc = dc + dot((spread(decay, pair) * dy).astype(bf16), sin_ref[0, here])
    dlow = dboth.astype(bf16)
    dbc_ref[0, :, :state] = dot(dlow, c_rows, 0, 0)
    dbc_ref[0, :, state:] = dc + dot(dlow, b_rows)


def carry_kernel(ids_ref, pc_ref, taps_ref, rate_ref, act_ref, dy_ref, r_ref, pos_ref, lac_ref, dtc_ref, g_ref, sin_ref, s_ref, dbc_ref, vec_ref, dpre_ref, first_ref, dstep_ref, dbc_out, dtaps_ref, drate_ref, *, channels, state, rows):
    seg = dy_ref.shape[1]
    width = channels + 2 * state
    b_rows = act_ref[0, :, channels : channels + state]
    lac, dtc = lac_ref[0], dtc_ref[0]
    last = lac[seg - 1 : seg]
    to_last = jnp.exp(last - lac)
    neg = jnp.zeros((seg, lanes), f32)
    db = jnp.zeros((seg, state), f32)
    through = jnp.zeros((1, lanes), f32)
    local = jnp.zeros((1, lanes), f32)
    states = pieces_in(ids_ref, s_ref, rows)

    @pl.when(pl.program_id(0) == 0)
    def _():
        dtaps_ref[...] = jnp.zeros_like(dtaps_ref)
        drate_ref[...] = jnp.zeros_like(drate_ref)

    for pair in range(channels // lanes):
        at = pair * lanes
        here = slice(at, at + lanes)
        grad = g_ref[0, here]
        values = act_ref[0, :, here].astype(f32)
        reach = spread(to_last, pair)
        step = spread(dtc, pair)
        r = r_ref[0, :, here] + reach * dot(b_rows, grad, 1, 1)
        neg = per_head(neg, values * r, pair)
        db = db + dot((reach * step * values).astype(bf16), grad)
        wide = grad.astype(f32)
        through = through + in_heads(wide * sin_ref[0, here].astype(f32), pair)
        local = local + in_heads(wide * states[here].astype(f32), pair)
        tapped, pre = convolved(pc_ref, taps_ref, at)
        sg = sigmoid(pre)
        dpre = (step * r + vec_ref[0:1, here] * dy_ref[0, :, here]) * (sg * (1.0 + pre * (1.0 - sg)))
        dpre_ref[0, :, here] = dpre
        for k in range(4):
            dtaps_ref[k : k + 1, here] += jnp.sum(dpre * tapped[k], axis=0, keepdims=True)
        dtaps_ref[4:5, here] += jnp.sum(dpre, axis=0, keepdims=True)
    first_ref[0] = dpre_ref[0, :8]
    dbc_out[0, :, :state] = dbc_ref[0, :, :state] + db
    dbc_out[0, :, state:] = dbc_ref[0, :, state:]
    seed = jnp.exp(last) * through + local
    upper = (iota((seg, seg), 0) <= iota((seg, seg), 1)).astype(f32)
    q = dot(upper, pos_ref[0] - dtc * neg, precision=best) + seed
    rates = rate_ref[1:2]
    z = pc_ref[0, halo:, width : width + lanes].astype(f32) + rate_ref[0:1]
    draw = (neg - rates * q) * sigmoid(z)
    dstep_ref[0] = draw.astype(bf16)
    drate_ref[0:1] += jnp.sum(draw, axis=0, keepdims=True)
    drate_ref[1:2] += jnp.sum(q * (-dtc * rates), axis=0, keepdims=True)


def returned_kernel(dpre_ref, next_ref, taps_ref, out_ref):
    seg = dpre_ref.shape[1]
    for at in range(0, dpre_ref.shape[2], lanes):
        here = slice(at, at + lanes)
        x = jnp.concatenate([dpre_ref[0, :, here], next_ref[0, :, here]], axis=0)
        total = x[:seg] * taps_ref[3:4, here]
        for k in range(3):
            by = 3 - k
            total = total + pltpu.roll(x, seg + 8 - by, 0)[:seg] * taps_ref[k : k + 1, here]
        out_ref[0, :, here] = total.astype(bf16)


def call(kernel, grid, ins, outs, name, ids=None, flops=0, scratch=(), **statics):
    def spec(shape, index):
        if index == "rows":
            return pl.BlockSpec((shape[0], shape[1] // grid, shape[2]), lambda s, *i: (0, s, 0))
        if index is None:
            return pl.BlockSpec(tuple(shape), lambda s, *i: (0,) * len(shape))
        block, at = index
        return pl.BlockSpec((block,) + tuple(shape[1:]), lambda s, *i: (at(s, *i),) + (0,) * (len(shape) - 1))

    moved = sum(a.size * a.dtype.itemsize for a, _ in ins)
    for shape, dtype, _ in outs:
        size = 1
        for d in shape:
            size *= d
        moved += size * jnp.dtype(dtype).itemsize
    return pl.pallas_call(
        functools.partial(kernel, **statics),
        grid_spec=pltpu.PrefetchScalarGridSpec(
            num_scalar_prefetch=0 if ids is None else 1,
            grid=(grid,),
            in_specs=[spec(a.shape, index) for a, index in ins],
            out_specs=[spec(shape, index) for shape, _, index in outs],
            scratch_shapes=list(scratch),
        ),
        out_shape=[jax.ShapeDtypeStruct(shape, dtype) for shape, dtype, _ in outs],
        compiler_params=pltpu.CompilerParams(vmem_limit_bytes=24 << 20),
        cost_estimate=pl.CostEstimate(flops=flops, bytes_accessed=moved, transcendentals=0),
        name=name,
    )(*([] if ids is None else [ids]), *[a for a, _ in ins])


each = (1, lambda s, *i: s)


def swap(value, axis, by):
    count = lax.axis_size(axis)
    return lax.ppermute(value, axis, [(i, i ^ by) for i in range(count)])


def all_slots(value, axis):
    count = lax.axis_size(axis)
    pieces, by = {0: value}, count // 2
    while by:
        for j in list(pieces):
            pieces[j ^ by] = swap(pieces[j], axis, by)
        by //= 2
    return jnp.concatenate([pieces[j] for j in range(count)], axis=0)


def to_owner(parts, axis):
    count = lax.axis_size(axis)
    parts, by = list(parts), 1
    left = list(range(count))
    while by < count:
        keep = [j for j in left if not j & by]
        new = {}
        for j in keep:
            new[j] = parts[j] + swap(parts[j ^ by].astype(bf16), axis, by).astype(f32)
        parts = [new.get(j) for j in range(count)]
        left = keep
        by *= 2
    return parts[0]


def scatter_sum(value, axis, at):
    count, place, by = lax.axis_size(axis), lax.axis_index(axis), 1
    while by < count:
        shape = value.shape
        value = value.reshape(shape[:at] + (shape[at] // 2, 2) + shape[at + 1 :])
        bit = (place // by) % 2
        keep = lax.dynamic_index_in_dim(value, bit, at + 1, False)
        give = lax.dynamic_index_in_dim(value, 1 - bit, at + 1, False)
        value = (keep.astype(f32) + swap(give, axis, by).astype(f32)).astype(bf16)
        by *= 2
    return jnp.squeeze(value, at)


def gathered(piece, axis):
    value, by = piece[None], lax.axis_size(axis) // 2
    while by:
        value = jnp.concatenate([value, swap(value, axis, by)], axis=0)
        by //= 2
    return value


def reversed_bits(j, count):
    out, by = 0, 1
    while by < count:
        out = out * 2 + (j // by) % 2
        by *= 2
    return out


def traded(value, axis):
    count, me = lax.axis_size(axis), lax.axis_index(axis)
    parts = [lax.dynamic_index_in_dim(value, me ^ j, 0, False) for j in range(count)]
    return jnp.stack([swap(part, axis, j) if j else part for j, part in enumerate(parts)])


def sent(value, axis):
    return [swap(value[j], axis, j) if j else value[0] for j in range(lax.axis_size(axis))]


def in_order(parts, index):
    stacked = jnp.stack(parts)
    return jnp.concatenate([lax.dynamic_index_in_dim(stacked, index ^ a, 0) for a in range(len(parts))])


def rows_in_order(parts, index):
    total = sum(part.shape[0] for part, _ in parts)
    out = jnp.zeros((total,) + parts[0][0].shape[1:], parts[0][0].dtype)
    for part, start in parts:
        out = lax.dynamic_update_slice_in_dim(out, part, start, 0)
    return out


def assemble_kernel(ids_ref, *refs, parts, share, heads, inner):
    bufs, (last_ref, weight_ref, out_ref, tail_ref, sum_ref) = refs[: len(parts)], refs[len(parts) :]
    owners = last_ref.shape[1]
    rows = out_ref.shape[0]
    total = jnp.zeros((rows, 1), f32)

    def put(at, value):
        size = value.shape[1]
        out_ref[:, at : at + size] = value
        return jnp.sum(value * weight_ref[:, at : at + size].astype(f32), axis=1, keepdims=True)

    for a in range(owners):
        for ref, (start, step) in zip(bufs, parts, strict=True):
            total = total + put(start + a * step, ref[0, ids_ref[1] ^ a].astype(f32))
    lane = iota((rows, lanes), 1)
    lasts = [last_ref[0, ids_ref[1] ^ a].astype(f32) for a in range(owners)]
    for a in range(owners):
        tail_ref[a] = lasts[a]
    group = lanes // share
    for block in range(owners // group):
        value = jnp.zeros((rows, lanes), f32)
        for b in range(group):
            moved = lasts[block * group + b]
            moved = pltpu.roll(moved, b * share, 1) if b else moved
            value = jnp.where(lane // share == b, moved, value)
        total = total + put(2 * inner + block * lanes, value)
    value = jnp.zeros((rows, lanes), f32)
    for a in range(owners):
        moved = pltpu.roll(lasts[a], (a * heads - share) % lanes, 1)
        value = jnp.where(lane // heads == a, moved, value)
    total = total + put(2 * inner + owners * share, value[:, : owners * heads])
    sum_ref[...] = total


def rows_kernel(ids_ref, *refs, parts):
    bufs, (weight_ref, out_ref, sum_ref) = refs[: len(parts)], refs[len(parts) :]
    total = jnp.zeros((out_ref.shape[0], 1), f32)
    for ref, (start, size) in zip(bufs, parts, strict=True):
        value = ref[0].astype(f32)
        out_ref[:, start : start + size] = value
        total = total + jnp.sum(value * weight_ref[:, start : start + size].astype(f32), axis=1, keepdims=True)
    sum_ref[...] = total


def per_device(tokens, lengths, norm_gain, in_weight, conv_weight, conv_bias, dt_bias, decay_log, skip_gain, gated_gain, out_weight, cotangent):
    nf, nq = lax.axis_size("fsdp"), lax.axis_size("seq")
    me, place = lax.axis_index("fsdp"), lax.axis_index("seq")
    _, seg, width = tokens.shape
    rows = in_weight.shape[0]
    channels = out_weight.shape[0]
    inner = channels * nf
    heads = dt_bias.shape[0]
    conv_own = conv_weight.shape[1]
    state = (conv_own * nf - inner) // 2
    share = 2 * state // nf
    slots = nf

    ids = jnp.stack([place, me]).astype(jnp.int32)
    per_slot = nq // slots
    piece = channels // per_slot

    x_main = all_slots(tokens, "fsdp")
    before = lax.ppermute(tokens[0, seg - 3 :], "seq", [(i, i + 1) for i in range(nq - 1)])

    def padded(rows_):
        return jnp.pad(rows_, ((0, 0), (0, width - rows_.shape[1])))

    small = jnp.concatenate(
        [padded(conv_weight), padded(conv_bias[None]), padded(norm_gain[None]), jnp.zeros((7, width), bf16), before], axis=0
    )
    x_small = all_slots(small[None], "fsdp")
    listed = [x_small[j] for j in range(nf)]
    norm_all = in_order([part[5, :rows] for part in listed], me).astype(f32).reshape(1, width)
    taps_all = in_order([part[:5, :conv_own] for part in listed], me).astype(f32)
    taps_all = taps_all.reshape(nf, 5, conv_own).transpose(1, 0, 2).reshape(5, -1)
    taps_all = jnp.pad(taps_all, ((0, 3), (0, 0)))
    taps = jnp.concatenate([lax.dynamic_slice_in_dim(taps_all, me * channels, channels, 1), taps_all[:, inner:]], axis=1)
    taps_share = lax.dynamic_slice_in_dim(taps_all, inner + me * share, share, 1)
    rate = jnp.stack([dt_bias.astype(f32), jnp.exp(decay_log.astype(f32))])
    rate = jnp.pad(rate, ((0, 6), (0, lanes - heads)))
    vec = jnp.stack([jnp.repeat(skip_gain.astype(f32), head_size), gated_gain.astype(f32)])
    vec = jnp.pad(vec, ((0, 6), (0, 0)))

    half, side = rows // 2, place % 2
    gives = [lax.dynamic_slice_in_dim(in_weight, inner + (me ^ j) * channels, channels, 1) for j in range(nf)]
    got = [(gives[0], me * rows)]
    for j in range(nf - 1, 0, -1):
        start = (me ^ j) * rows
        if j == 1:
            got.append((swap(gives[j], "fsdp", j), start))
        else:
            mine = swap(lax.dynamic_slice_in_dim(gives[j], side * half, half, 0), "fsdp", j)
            got.append((mine, start + side * half))
            got.append((swap(mine, "seq", 1), start + (1 - side) * half))
    w_value = rows_in_order(got, me)
    rest = in_weight[:, 2 * inner :]
    kept = rest.shape[1]
    rest = all_slots(jnp.pad(rest, ((0, 0), (0, -kept % lanes)))[None], "fsdp")
    rest = in_order([rest[j] for j in range(nf)], me).reshape(width, -1)
    w_rows = rest[:, : 2 * state]
    w_step = jnp.pad(lax.dynamic_slice_in_dim(rest, 2 * state + me * heads, heads, 1), ((0, 0), (0, lanes - heads)))
    w_conv = jnp.concatenate([w_value, w_rows, w_step], axis=1)

    (normed,) = call(
        normalize_kernel,
        slots,
        [(x_main, each), (x_small, each), (norm_all, None)],
        [((slots, halo + seg, width), bf16, each)],
        "normalize",
    )
    inputs = tokens[0].astype(f32)
    inv = lax.rsqrt(jnp.mean(inputs * inputs, axis=-1, keepdims=True) + epsilon)
    valid = (place * seg + jnp.arange(seg) < lengths[0]).astype(f32)[:, None]
    upstream = valid * cotangent[0].astype(f32)

    gives = [lax.dynamic_slice_in_dim(in_weight, (me ^ j) * channels, channels, 1) for j in range(nf)]
    gives, later, _ = lax.optimization_barrier((gives, upstream.astype(bf16), got[-2][0]))
    w_gate = rows_in_order([(swap(g, "fsdp", j) if j else g, (me ^ j) * rows) for j, g in enumerate(gives)], me)
    back_branch = all_slots(later[None], "fsdp")

    def project(x, w):
        return lax.dot_general(x, w, (((2,), (0,)), ((), ())), preferred_element_type=f32)

    pc = project(normed, w_conv).astype(bf16)
    main = normed[:, halo:]
    cw = channels + 2 * state
    tall = 16
    statics = dict(channels=channels, state=state)
    turned = (per_slot, lambda s, i: s ^ (i[0] // per_slot))
    act, y_local, s_local, lac, dtc, lar, dtr = call(
        forward_kernel,
        slots,
        [(pc, each), (taps, None), (rate, None)],
        [
            ((slots, seg, cw), bf16, each),
            ((slots, seg, channels), f32, each),
            ((nq, piece + 16, state), bf16, turned),
            ((slots, seg, lanes), f32, each),
            ((slots, seg, lanes), f32, each),
            ((slots, tall, seg), f32, each),
            ((slots, tall, seg), f32, each),
        ],
        "forward",
        ids=ids,
        flops=2 * slots * seg * seg * channels,
        rows=piece,
        **statics,
    )

    def ordered(parts):
        (out,) = call(order_kernel, 1, [(p, None) for p in parts], [((nq, piece, state), bf16, None)], "order", ids=ids)
        return out.reshape(slots, channels, state)

    came = sent(s_local, "seq")
    reached, decays = call(
        chain_kernel,
        1,
        [(part, None) for part in came],
        [((nq, piece, state), bf16, None), ((nq, 8, lanes), f32, None)],
        "chain",
        ids=ids,
        scratch=[pltpu.VMEM((nq, piece + 16, state), bf16)],
        rows=piece,
        count=per_slot,
    )
    s_in = ordered(sent(reached, "seq"))

    gate = project(main, w_gate).astype(bf16)
    bg = lax.dot_general(back_branch, out_weight, (((2,), (1,)), ((), ())), preferred_element_type=f32)
    y, stats = call(
        finish_kernel,
        slots,
        [(y_local, each), (act, each), (lac, each), (s_in, each), (gate, each), (bg, each), (vec, None)],
        [((slots, seg, channels), f32, each), ((slots, 8, seg), f32, each)],
        "finish",
        **statics,
    )
    shares = [(swap(stats, "fsdp", j) if j else stats, (1, lambda s, i, j=j: s ^ j)) for j in range(nf)]
    gated_out, dgate, dy, pos, dsin, dskip = call(
        norm_kernel,
        slots,
        [(y, each), (act, each), (lac, each), (gate, each), (bg, each), (vec, None)] + shares,
        [
            ((slots, seg, channels), bf16, each),
            ((slots, seg, channels), bf16, each),
            ((slots, seg, channels), f32, each),
            ((slots, seg, lanes), f32, each),
            ((nq, piece, state), bf16, turned),
            ((8, channels), f32, None),
        ],
        "norm",
        ids=ids,
        inner=inner,
        rows=piece,
        **statics,
    )
    came = sent(dsin, "seq")
    (reached,) = call(
        back_chain_kernel,
        1,
        [(part, None) for part in came] + [(decays, None)],
        [((nq, piece, state), bf16, None)],
        "back_chain",
        ids=ids,
        scratch=[pltpu.VMEM((nq, piece, state), bf16)],
        rows=piece,
        count=per_slot,
    )
    g_end = ordered(sent(reached, "seq"))

    r_local, dbc = call(
        backward_kernel,
        slots,
        [(act, each), (dy, each), (lac, each), (lar, each), (dtr, each), (s_in, each)],
        [((slots, seg, channels), f32, each), ((slots, seg, 2 * state), f32, each)],
        "backward",
        flops=4 * slots * seg * seg * channels,
        **statics,
    )
    dpre, first, dstep, dbc, dtaps, drate = call(
        carry_kernel,
        slots,
        [
            (pc, each), (taps, None), (rate, None), (act, each), (dy, each), (r_local, each), (pos, each), (lac, each),
            (dtc, each), (g_end, each), (s_in, each), (s_local, turned), (dbc, each), (vec, None),
        ],
        [
            ((slots, seg, channels), f32, each),
            ((slots, 8, channels), f32, each),
            ((slots, seg, lanes), bf16, each),
            ((slots, seg, 2 * state), f32, each),
            ((8, channels), f32, None),
            ((8, lanes), f32, None),
        ],
        "carry",
        ids=ids,
        rows=piece,
        **statics,
    )
    behind = [(i, i - 1) for i in range(1, nq)]
    after = lax.ppermute(first, "seq", behind)
    (dvalue,) = call(
        returned_kernel,
        slots,
        [(dpre, each), (after, each), (taps[:, :channels], None)],
        [((slots, seg, channels), bf16, each)],
        "returned",
    )

    mine = dbc.astype(bf16).reshape(slots, seg, nf, share)
    d_act = None
    for j in range(nf):
        part = lax.dynamic_index_in_dim(mine, me ^ j, 2, False)
        part = swap(part, "fsdp", j) if j else part
        part = jnp.stack([part[m ^ j] for m in range(slots)]).astype(f32)
        d_act = part if d_act is None else d_act + part
    xs = lax.dynamic_slice_in_dim(pc, channels + me * share, share, 2)[:, halo - 3 :].astype(f32)
    tapped = [xs[:, k : k + seg] for k in range(4)]
    pre = taps_share[4] + sum(tapped[k] * taps_share[k] for k in range(4))
    sg = sigmoid(pre)
    dpre_s = d_act * (sg * (1.0 + pre * (1.0 - sg)))
    dtaps_s = jnp.stack([jnp.sum(dpre_s * t, axis=(0, 1)) for t in tapped] + [jnp.sum(dpre_s, axis=(0, 1))])
    after_s = lax.ppermute(dpre_s[:, :3], "seq", behind)
    longer = jnp.concatenate([dpre_s, after_s], axis=1)
    dshare = sum(longer[:, 3 - k : 3 - k + seg] * taps_share[k] for k in range(4)).astype(bf16)
    dlast = jnp.concatenate([dshare, dstep[..., :heads]], axis=2)

    def grad_of(x, dz):
        return lax.dot_general(x, dz, (((0, 1), (0, 1)), ((), ())), preferred_element_type=f32)

    per = channels // rows
    block = jnp.concatenate(
        [
            dtaps[:5].T.reshape(per, rows, 5).transpose(1, 0, 2).reshape(rows, 5 * per),
            jnp.pad(dtaps_s.T, ((0, rows - share), (0, 0))),
            jnp.pad(
                jnp.stack([drate[0, :heads], drate[1, :heads], jnp.sum(dskip[0].reshape(heads, head_size), axis=1)], axis=1),
                ((0, rows - heads), (0, 0)),
            ),
        ],
        axis=1,
    )
    extra = block.shape[1]
    block = jnp.pad(block, ((0, 0), (0, lanes - share - heads - extra)))
    gw_last = jnp.concatenate([grad_of(main, dlast), jnp.tile(block, (nf, 1))], axis=1)

    unit = rows // nq

    def summed(g):
        g = scatter_sum(g.astype(bf16).reshape(nf, nq, unit, -1), "seq", 1)
        return gathered(traded(g, "fsdp"), "seq")

    def cut(value):
        size = value.shape[-1] // 2
        return [value] if size % lanes else [value[..., :size], value[..., size:]]

    out_parts = [
        gathered(scatter_sum(grad_of(gated_out, part).astype(bf16).reshape(nq, channels // nq, -1), "seq", 0), "seq")
        for part in cut(back_branch)
    ]
    starts, bufs = [], []
    for base, whole in ((0, dgate), (inner, dvalue)):
        for part in cut(whole):
            starts.append((base, channels))
            base += part.shape[-1]
            bufs.append(summed(grad_of(main, part)))
    s_last = summed(gw_last)

    by_place = (1, lambda s, i: reversed_bits(i[0] ^ s, nq))
    place_of = jnp.stack([reversed_bits(place ^ q, nq) for q in range(nq)])
    if unit % 16 == 0:
        g_in, tail, norm_sum = call(
            assemble_kernel,
            nq,
            [(buf, by_place) for buf in bufs] + [(s_last, by_place), (in_weight, (unit, lambda s, i: s))],
            [
                (in_weight.shape, f32, (unit, lambda s, i: s)),
                ((nf, rows, lanes), f32, "rows"),
                ((rows, 1), f32, (unit, lambda s, i: s)),
            ],
            "assemble",
            ids=ids,
            parts=starts,
            share=share,
            heads=heads,
            inner=inner,
        )
        norm_sum = norm_sum[:, 0]
    else:
        order = me ^ jnp.arange(nf)

        def natural(buf):
            return buf[place_of][:, order].astype(f32).transpose(1, 0, 2, 3).reshape(nf, rows, -1)

        def side_by_side(value):
            return value.transpose(1, 0, 2).reshape(rows, -1)

        count = len(bufs) // 2
        joined = [side_by_side(jnp.concatenate([natural(b) for b in bs], axis=2)) for bs in (bufs[:count], bufs[count:])]
        tail = natural(s_last)
        joined += [side_by_side(tail[..., :share]), side_by_side(tail[..., share : share + heads])]
        g_in = jnp.concatenate(joined, axis=1)
        norm_sum = jnp.sum(g_in * in_weight.astype(f32), axis=1)
    out_unit = channels // nq
    if out_unit % 16 == 0:
        sizes = [part.shape[-1] for part in out_parts]
        g_out, gated_sum = call(
            rows_kernel,
            nq,
            [(part, by_place) for part in out_parts] + [(out_weight, (out_unit, lambda s, i: s))],
            [(out_weight.shape, f32, (out_unit, lambda s, i: s)), ((channels, 1), f32, (out_unit, lambda s, i: s))],
            "rows",
            ids=ids,
            parts=[(sum(sizes[:i]), size) for i, size in enumerate(sizes)],
        )
        gated_sum = gated_sum[:, 0]
    else:
        g_out = jnp.concatenate([part[place_of].astype(f32).reshape(channels, -1) for part in out_parts], axis=1)
        gated_sum = jnp.sum(g_out * out_weight.astype(f32), axis=1)

    norm_grad = norm_sum / norm_gain.astype(f32)
    gated_grad = gated_sum / gated_gain.astype(f32)

    got = tail[..., share + heads : share + heads + extra]
    tap_grads = jnp.concatenate(
        [
            got[..., : 5 * per].reshape(nf, rows, per, 5).transpose(0, 2, 1, 3).reshape(inner, 5),
            got[:, :share, 5 * per : 5 * per + 5].reshape(2 * state, 5),
        ],
        axis=0,
    )
    tap_grads = lax.dynamic_slice_in_dim(tap_grads, me * conv_own, conv_own, 0).T
    head_grads = lax.dynamic_index_in_dim(got, me, 0, False)[:heads, 5 * per + 5 :]

    branch = project(gated_out, out_weight)
    branch = to_owner([branch[j] for j in range(slots)], "fsdp")
    mixed = (valid * (inputs + branch)).astype(bf16)

    w_share = lax.dynamic_slice_in_dim(w_conv, channels + me * share, share, 1)
    w_last = jnp.concatenate([w_share, w_conv[:, cw : cw + heads]], axis=1)

    def back(dz, w):
        return lax.dot_general(dz, w, (((2,), (1,)), ((), ())), preferred_element_type=f32)

    bn = back(dgate, w_gate) + back(dvalue, w_conv[:, :channels]) + back(dlast, w_last)
    bn = to_owner([bn[j] for j in range(slots)], "fsdp") * norm_all
    lean = jnp.mean(bn * inputs, axis=-1, keepdims=True)
    input_grad = upstream + inv * bn - inputs * (inv * inv * inv) * lean
    return (
        mixed[None],
        input_grad[None],
        norm_grad,
        g_in,
        tap_grads[:4],
        tap_grads[4],
        head_grads[:, 0],
        head_grads[:, 1],
        head_grads[:, 2],
        gated_grad,
        g_out,
    )


def solution(mesh):
    whole, rows = P("fsdp", "seq", None), P("fsdp", None)
    one, columns = P("fsdp"), P(None, "fsdp")
    return jax.shard_map(
        per_device,
        mesh=mesh,
        in_specs=(whole, one, one, rows, columns, one, one, one, one, one, rows, whole),
        out_specs=(whole, whole, one, rows, columns, one, one, one, one, one, rows),
        check_vma=False,
    )
```

```python
import functools

import jax
import jax.numpy as jnp
from jax import lax
from jax.experimental import pallas as pl
from jax.experimental.pallas import tpu as pltpu
from jax.sharding import PartitionSpec as P

epsilon = 1e-05
bf16, f32 = jnp.bfloat16, jnp.float32
best = lax.Precision.HIGHEST
halo = 16
lanes = 128
head_size = 64


def dot(a, b, ca=1, cb=0, precision=None):
    return lax.dot_general(
        a, b, (((ca,), (cb,)), ((), ())), preferred_element_type=f32, precision=precision
    )


def sigmoid(v):
    return 1.0 / (1.0 + jnp.exp(-v))


def iota(shape, axis):
    return lax.broadcasted_iota(jnp.int32, shape, axis)


def spread(columns, pair):
    first, second = 2 * pair, 2 * pair + 1
    rows = columns.shape[0]
    return jnp.where(
        iota((rows, lanes), 1) < head_size,
        columns[:, first : first + 1],
        columns[:, second : second + 1],
    )


def per_head(total, products, pair):
    rows = products.shape[0]
    lane = iota((rows, lanes), 1)
    low = jnp.sum(jnp.where(lane < head_size, products, 0.0), axis=1, keepdims=True)
    high = jnp.sum(jnp.where(lane < head_size, 0.0, products), axis=1, keepdims=True)
    return total + jnp.where(lane == 2 * pair, low, jnp.where(lane == 2 * pair + 1, high, 0.0))


def in_heads(products, pair):
    rows = jnp.sum(products, axis=1, keepdims=True)
    low, high = jnp.sum(rows[:head_size]), jnp.sum(rows[head_size:])
    lane = iota((1, lanes), 1)
    return jnp.where(lane == 2 * pair, low, jnp.where(lane == 2 * pair + 1, high, 0.0))


def convolved(pc_ref, taps_ref, at):
    x = pc_ref[0, :, at : at + lanes].astype(f32)
    tapped = [pltpu.roll(x, 3 - k, 0)[halo:] for k in range(3)] + [x[halo:]]
    pre = taps_ref[4:5, at : at + lanes]
    for k in range(4):
        pre = pre + tapped[k] * taps_ref[k : k + 1, at : at + lanes]
    return tapped, pre


def pieces_out(out_ref, whole, rows):
    for p in range(out_ref.shape[0]):
        out_ref[p, :rows] = whole[p * rows : (p + 1) * rows]


def pieces_in(ref, rows):
    return jnp.concatenate([ref[p, :rows] for p in range(ref.shape[0])], axis=0)


def block_of(index, size):
    return pl.ds(pl.multiple_of(index * size, size), size)


def columns_of(ref, index, size):
    if size % lanes == 0:
        return ref[:, block_of(index, size)]
    value = ref[:, :size]
    for a in range(1, ref.shape[1] // size):
        value = jnp.where(index == a, ref[:, a * size : (a + 1) * size], value)
    return value


def normalize_kernel(ids_ref, main_ref, small_ref, gain_ref, out_ref, *, owners):
    size = out_ref.shape[2] // owners
    for ref, at in ((small_ref, 0), (main_ref, halo)):
        x = ref[0].astype(f32)
        inv = lax.rsqrt(jnp.mean(x * x, axis=1, keepdims=True) + epsilon)
        for j in range(owners):
            own = ids_ref[1] ^ j
            part = columns_of(ref.at[0], own, size).astype(f32) * inv * columns_of(gain_ref, own, size)
            out_ref[0, at : at + x.shape[0], j * size : (j + 1) * size] = part.astype(bf16)


def weight_kernel(ids_ref, *refs, owners, state, heads):
    rest_ref, out_ref = refs[-2:]
    size = rest_ref.shape[2]
    channels = out_ref.shape[0] - 2 * state - lanes
    n = 0
    for j in range(owners):
        own = slice(j * size, (j + 1) * size)
        if j < 2:
            out_ref[:channels, own] = refs[n][...]
            n += 1
        else:
            half = channels // 2
            for side in range(2):
                out_ref[block_of((ids_ref[0] % 2) ^ side, half), own] = refs[n][...]
                n += 1
        out_ref[channels : channels + 2 * state, own] = rest_ref[j, : 2 * state]
        rows = owners * heads
        pick = iota((lanes, rows), 1) == ids_ref[1] * heads + iota((lanes, rows), 0)
        pick = jnp.where(iota((lanes, rows), 0) < heads, pick.astype(f32), 0.0).astype(bf16)
        out_ref[channels + 2 * state :, own] = dot(pick, rest_ref[j, 2 * state : 2 * state + rows]).astype(bf16)


def input_kernel(ids_ref, bn_ref, gain_ref, tokens_ref, cot_ref, valid_ref, out_ref, *, owners):
    x = tokens_ref[...].astype(f32)
    width = x.shape[1]
    size = width // owners
    inv = lax.rsqrt(jnp.mean(x * x, axis=1, keepdims=True) + epsilon)
    lean = jnp.zeros_like(inv)
    for a in range(owners):
        here = slice(a * size, (a + 1) * size)
        bn = columns_of(bn_ref, ids_ref[1] ^ a, size) * gain_ref[:, here]
        lean = lean + jnp.sum(bn * x[:, here], axis=1, keepdims=True)
    lean = lean * (inv * inv * inv) * (1.0 / width)
    for a in range(owners):
        here = slice(a * size, (a + 1) * size)
        bn = columns_of(bn_ref, ids_ref[1] ^ a, size) * gain_ref[:, here]
        out_ref[:, here] = valid_ref[...] * cot_ref[:, here].astype(f32) + inv * bn - x[:, here] * lean


def of_rows(row, ids_ref, rows, count):
    head = ((ids_ref[0] % count) * rows + iota((rows, lanes), 0)) // head_size
    return jnp.sum(jnp.where(iota((rows, lanes), 1) == head, row, 0.0), axis=1, keepdims=True)


def chain_kernel(ids_ref, in_ref, out_ref, *, rows, count):
    carried = jnp.zeros((rows, lanes), f32)
    for i in range(in_ref.shape[0]):
        out_ref[i] = carried.astype(bf16)
        row = in_ref[i, rows : rows + 1].astype(f32) + in_ref[i, rows + 1 : rows + 2].astype(f32)
        carried = of_rows(row, ids_ref, rows, count) * carried + in_ref[i, :rows].astype(f32)


def back_chain_kernel(ids_ref, in_ref, decay_ref, out_ref, *, rows, count):
    carried = jnp.zeros((rows, lanes), f32)
    for i in reversed(range(in_ref.shape[0])):
        out_ref[i] = carried.astype(bf16)
        row = decay_ref[i, rows : rows + 1].astype(f32) + decay_ref[i, rows + 1 : rows + 2].astype(f32)
        carried = of_rows(row, ids_ref, rows, count) * carried + in_ref[i].astype(f32)


def forward_kernel(pc_ref, taps_ref, rate_ref, act_ref, y_ref, s_ref, lac_ref, dtc_ref, lar_ref, dtr_ref, *, channels, state, rows):
    width = channels + 2 * state
    for at in range(0, width, lanes):
        _, pre = convolved(pc_ref, taps_ref, at)
        act_ref[0, :, at : at + lanes] = (pre * sigmoid(pre)).astype(bf16)
    seg = act_ref.shape[1]
    z = pc_ref[0, halo:, width : width + lanes].astype(f32) + rate_ref[0:1]
    dtc = jnp.maximum(z, 0.0) + jnp.log1p(jnp.exp(-jnp.abs(z)))
    lower = iota((seg, seg), 0) >= iota((seg, seg), 1)
    lac = dot(lower.astype(f32), -dtc * rate_ref[1:2], precision=best)
    tall = lar_ref.shape[1]
    lar, dtr = lac.T[:tall], dtc.T[:tall]
    lac_ref[0], dtc_ref[0], lar_ref[0], dtr_ref[0] = lac, dtc, lar, dtr
    b_rows = act_ref[0, :, channels : channels + state]
    c_rows = act_ref[0, :, channels + state : width]
    both = dot(c_rows, b_rows, 1, 1)
    to_end = jnp.exp(lac[seg - 1 : seg] - lac) * dtc
    states = []
    for pair in range(channels // lanes):
        at = pair * lanes
        values = act_ref[0, :, at : at + lanes]
        parts = []
        for side in range(2):
            h = 2 * pair + side
            mix = jnp.where(lower, jnp.exp(lac[:, h : h + 1] - lar[h : h + 1]), 0.0) * both * dtr[h : h + 1]
            parts.append(dot(mix.astype(bf16), values[:, side * head_size : (side + 1) * head_size]))
        y_ref[0, :, at : at + lanes] = jnp.concatenate(parts, axis=1)
        weighted = (spread(to_end, pair) * values.astype(f32)).astype(bf16)
        states.append(dot(weighted, b_rows, 0, 0).astype(bf16))
    pieces_out(s_ref, jnp.concatenate(states, axis=0), rows)
    whole = jnp.exp(lac[seg - 1 : seg])
    high = whole.astype(bf16).astype(f32)
    row = iota((16, lanes), 0)
    tail = jnp.where(row == 0, high, jnp.where(row == 1, whole - high, 0.0)).astype(bf16)
    for p in range(s_ref.shape[0]):
        s_ref[p, rows:] = tail


def finish_kernel(y_ref, act_ref, lac_ref, sin_ref, gate_ref, bg_ref, vec_ref, y_out, stat_ref, *, channels, state):
    seg = y_ref.shape[1]
    c_rows = act_ref[0, :, channels + state : channels + 2 * state]
    decay = jnp.exp(lac_ref[0])
    first = jnp.zeros((seg, 1), f32)
    second = jnp.zeros((seg, 1), f32)
    for pair in range(channels // lanes):
        at = pair * lanes
        here = slice(at, at + lanes)
        carried = dot(c_rows, sin_ref[0, here], 1, 1)
        y = y_ref[0, :, here] + spread(decay, pair) * carried
        y_out[0, :, here] = y
        gate = gate_ref[0, :, here].astype(f32)
        heads = y + vec_ref[0:1, here] * act_ref[0, :, here].astype(f32)
        gated = heads * gate * sigmoid(gate)
        first = first + jnp.sum(gated * gated, axis=1, keepdims=True)
        second = second + jnp.sum(gated * bg_ref[0, :, here] * vec_ref[1:2, here], axis=1, keepdims=True)
    lane = iota((seg, lanes), 1)
    both = jnp.where(lane == 0, first, jnp.where(lane == 1, second, 0.0))
    stat_ref[0] = both.T[:8]


def norm_kernel(y_ref, act_ref, lac_ref, gate_ref, bg_ref, vec_ref, *refs, channels, state, inner, rows):
    stat_refs, (out_ref, dgate_ref, dy_ref, pos_ref, dsin_ref, dskip_ref) = refs[:-6], refs[-6:]
    seg = y_ref.shape[1]
    stats = sum(ref[0] for ref in stat_refs).T
    states = []
    inv = lax.rsqrt(stats[:, 0:1] * (1.0 / inner) + epsilon)
    lean = inv * inv * inv * (stats[:, 1:2] * (1.0 / inner))
    c_rows = act_ref[0, :, channels + state : channels + 2 * state]
    decay = jnp.exp(lac_ref[0])
    pos = jnp.zeros((seg, lanes), f32)

    @pl.when(pl.program_id(0) == 0)
    def _():
        dskip_ref[...] = jnp.zeros_like(dskip_ref)

    for pair in range(channels // lanes):
        at = pair * lanes
        here = slice(at, at + lanes)
        y = y_ref[0, :, here]
        values = act_ref[0, :, here].astype(f32)
        heads = y + vec_ref[0:1, here] * values
        gate = gate_ref[0, :, here].astype(f32)
        sg = sigmoid(gate)
        gated = heads * gate * sg
        gain = vec_ref[1:2, here]
        out_ref[0, :, here] = (gated * inv * gain).astype(bf16)
        dgated = inv * (bg_ref[0, :, here] * gain) - gated * lean
        dgate_ref[0, :, here] = (dgated * heads * (sg * (1.0 + gate * (1.0 - sg)))).astype(bf16)
        dy = dgated * gate * sg
        dy_ref[0, :, here] = dy
        pos = per_head(pos, dy * y, pair)
        states.append(dot((spread(decay, pair) * dy).astype(bf16), c_rows, 0, 0).astype(bf16))
        dskip_ref[0:1, here] += jnp.sum(dy * values, axis=0, keepdims=True)
    pos_ref[0] = pos
    pieces_out(dsin_ref, jnp.concatenate(states, axis=0), rows)


def backward_kernel(act_ref, dy_ref, lac_ref, lar_ref, dtr_ref, sin_ref, r_ref, dbc_ref, *, channels, state):
    seg = dy_ref.shape[1]
    b_rows = act_ref[0, :, channels : channels + state]
    c_rows = act_ref[0, :, channels + state : channels + 2 * state]
    both = dot(c_rows, b_rows, 1, 1)
    lower = iota((seg, seg), 0) >= iota((seg, seg), 1)
    lac, lar, dtr = lac_ref[0], lar_ref[0], dtr_ref[0]
    decay = jnp.exp(lac)
    dboth = jnp.zeros((seg, seg), f32)
    dc = jnp.zeros((seg, state), f32)
    for pair in range(channels // lanes):
        at = pair * lanes
        here = slice(at, at + lanes)
        values = act_ref[0, :, here]
        dy = dy_ref[0, :, here]
        dyl = dy.astype(bf16)
        parts = []
        for side in range(2):
            h = 2 * pair + side
            own = slice(side * head_size, (side + 1) * head_size)
            weights = jnp.where(lower, jnp.exp(lac[:, h : h + 1] - lar[h : h + 1]), 0.0)
            parts.append(dot((weights * both).astype(bf16), dyl[:, own], 0, 0))
            dboth = dboth + dot(dyl[:, own], values[:, own], 1, 1) * (weights * dtr[h : h + 1])
        r_ref[0, :, here] = jnp.concatenate(parts, axis=1)
        dc = dc + dot((spread(decay, pair) * dy).astype(bf16), sin_ref[0, here])
    dlow = dboth.astype(bf16)
    dbc_ref[0, :, :state] = dot(dlow, c_rows, 0, 0)
    dbc_ref[0, :, state:] = dc + dot(dlow, b_rows)


def rows_grad_kernel(ids_ref, act_ref, lac_ref, dtc_ref, g_ref, dbc_ref, *refs, channels, state):
    out_refs, hold = refs[:-1], refs[-1]
    seg = act_ref.shape[1]
    lac, dtc = lac_ref[0], dtc_ref[0]
    weights = jnp.exp(lac[seg - 1 : seg] - lac) * dtc
    db = dbc_ref[0, :, :state]
    for pair in range(channels // lanes):
        here = slice(pair * lanes, (pair + 1) * lanes)
        db = db + dot((spread(weights, pair) * act_ref[0, :, here].astype(f32)).astype(bf16), g_ref[0, here])
    hold[:state] = db.T
    hold[state:] = dbc_ref[0, :, state:].T
    share = out_refs[0].shape[1]
    for j, out_ref in enumerate(out_refs):
        out_ref[0] = hold[block_of(ids_ref[1] ^ j, share)].astype(bf16)


def share_kernel(ids_ref, pc_ref, taps_ref, *refs, channels, state):
    parts, (dpre_ref, first_ref, dtaps_ref, hold) = refs[:-4], refs[-4:]
    seg = pc_ref.shape[1] - halo
    share = parts[0].shape[1]
    own = block_of(ids_ref[1], share)
    hold[...] = pc_ref[0, :, channels : channels + 2 * state].astype(f32)[halo:].T
    x = hold[own]
    hold[:, :halo] = pc_ref[0, :halo, channels : channels + 2 * state].astype(f32).T
    edge = hold[own, :halo]
    lane = iota((share, seg), 1)
    tapped = []
    for k in range(3):
        value = pltpu.roll(x, 3 - k, 1)
        for t in range(3 - k):
            value = jnp.where(lane == t, edge[:, halo - 3 + k + t : halo - 2 + k + t], value)
        tapped.append(value)
    tapped.append(x)
    pre = taps_ref[:, 4:5] + sum(tapped[k] * taps_ref[:, k : k + 1] for k in range(4))
    sg = sigmoid(pre)
    dpre = sum(ref[0].astype(f32) for ref in parts) * (sg * (1.0 + pre * (1.0 - sg)))

    @pl.when(pl.program_id(0) == 0)
    def _():
        dtaps_ref[...] = jnp.zeros_like(dtaps_ref)

    lane = iota((share, lanes), 1)
    total = jnp.zeros((share, lanes), f32)
    for k in range(5):
        column = jnp.sum(dpre * tapped[k] if k < 4 else dpre, axis=1, keepdims=True)
        total = jnp.where(lane == k, column, total)
    dtaps_ref[...] += total
    rows = jnp.concatenate([dpre, jnp.zeros((lanes - share, seg), f32)], axis=0).T
    dpre_ref[0] = rows
    first_ref[0] = rows[:8]


def carry_kernel(pc_ref, taps_ref, rate_ref, act_ref, dy_ref, r_ref, pos_ref, lac_ref, dtc_ref, g_ref, sin_ref, s_ref, vec_ref, dpre_ref, first_ref, dstep_ref, dtaps_ref, drate_ref, *, channels, state, rows):
    seg = dy_ref.shape[1]
    width = channels + 2 * state
    b_rows = act_ref[0, :, channels : channels + state]
    lac, dtc = lac_ref[0], dtc_ref[0]
    last = lac[seg - 1 : seg]
    to_last = jnp.exp(last - lac)
    neg = jnp.zeros((seg, lanes), f32)
    through = jnp.zeros((1, lanes), f32)
    local = jnp.zeros((1, lanes), f32)
    states = pieces_in(s_ref, rows)

    @pl.when(pl.program_id(0) == 0)
    def _():
        dtaps_ref[...] = jnp.zeros_like(dtaps_ref)
        drate_ref[...] = jnp.zeros_like(drate_ref)

    for pair in range(channels // lanes):
        at = pair * lanes
        here = slice(at, at + lanes)
        grad = g_ref[0, here]
        values = act_ref[0, :, here].astype(f32)
        r = r_ref[0, :, here] + spread(to_last, pair) * dot(b_rows, grad, 1, 1)
        neg = per_head(neg, values * r, pair)
        wide = grad.astype(f32)
        through = through + in_heads(wide * sin_ref[0, here].astype(f32), pair)
        local = local + in_heads(wide * states[here].astype(f32), pair)
        tapped, pre = convolved(pc_ref, taps_ref, at)
        sg = sigmoid(pre)
        dpre = (spread(dtc, pair) * r + vec_ref[0:1, here] * dy_ref[0, :, here]) * (sg * (1.0 + pre * (1.0 - sg)))
        dpre_ref[0, :, here] = dpre
        for k in range(4):
            dtaps_ref[k : k + 1, here] += jnp.sum(dpre * tapped[k], axis=0, keepdims=True)
        dtaps_ref[4:5, here] += jnp.sum(dpre, axis=0, keepdims=True)
    first_ref[0] = dpre_ref[0, :8]
    seed = jnp.exp(last) * through + local
    upper = (iota((seg, seg), 0) <= iota((seg, seg), 1)).astype(f32)
    q = dot(upper, pos_ref[0] - dtc * neg, precision=best) + seed
    rates = rate_ref[1:2]
    z = pc_ref[0, halo:, width : width + lanes].astype(f32) + rate_ref[0:1]
    draw = (neg - rates * q) * sigmoid(z)
    dstep_ref[0] = draw.astype(bf16)
    drate_ref[0:1] += jnp.sum(draw, axis=0, keepdims=True)
    drate_ref[1:2] += jnp.sum(q * (-dtc * rates), axis=0, keepdims=True)


def returned_kernel(dpre_ref, dshare_ref, next_ref, taps_ref, dstep_ref, out_ref, *, share, heads):
    seg, width = dpre_ref.shape[1:]
    for at in range(0, width + lanes, lanes):
        here = slice(at, at + lanes)
        own = dpre_ref[0, :, here] if at < width else dshare_ref[0]
        x = jnp.concatenate([own, next_ref[0, :, here]], axis=0)
        total = x[:seg] * taps_ref[3:4, here]
        for k in range(3):
            by = 3 - k
            total = total + pltpu.roll(x, seg + 8 - by, 0)[:seg] * taps_ref[k : k + 1, here]
        if at == width:
            step = pltpu.roll(dstep_ref[0].astype(f32), share, 1)
            lane = iota((seg, lanes), 1)
            total = jnp.where(lane < share, total, jnp.where(lane < share + heads, step, 0.0))
        out_ref[0, :, here] = total.astype(bf16)


def call(kernel, grid, ins, outs, name, ids=None, flops=0, scratch=(), far=False, **statics):
    def spec(shape, index):
        if index is None:
            return pl.BlockSpec(tuple(shape), lambda s, *i: (0,) * len(shape))
        block, at = index
        return pl.BlockSpec((block,) + tuple(shape[1:]), lambda s, *i: (at(s, *i),) + (0,) * (len(shape) - 1))

    moved = sum(a.size * a.dtype.itemsize for a, _ in ins)
    for shape, dtype, _ in outs:
        size = 1
        for d in shape:
            size *= d
        moved += size * jnp.dtype(dtype).itemsize
    return pl.pallas_call(
        functools.partial(kernel, **statics),
        grid_spec=pltpu.PrefetchScalarGridSpec(
            num_scalar_prefetch=0 if ids is None else 1,
            grid=(grid,),
            in_specs=[spec(a.shape, index) for a, index in ins],
            out_specs=[spec(shape, index) for shape, _, index in outs],
            scratch_shapes=list(scratch),
        ),
        out_shape=[(pltpu.HBM if far else jax.ShapeDtypeStruct)(shape, dtype) for shape, dtype, _ in outs],
        compiler_params=pltpu.CompilerParams(vmem_limit_bytes=24 << 20),
        cost_estimate=pl.CostEstimate(flops=flops, bytes_accessed=moved, transcendentals=0),
        name=name,
    )(*([] if ids is None else [ids]), *[pltpu.with_memory_space_constraint(a, pltpu.HBM) if far else a for a, _ in ins])


each = (1, lambda s, *i: s)


def swap(value, axis, by):
    count = lax.axis_size(axis)
    return lax.ppermute(value, axis, [(i, i ^ by) for i in range(count)])


def all_slots(value, axis, first=None):
    count = lax.axis_size(axis)
    by = count // 2
    offsets = [0]
    while by:
        value = jnp.concatenate([value, swap(value, axis, by)], axis=0)
        if first is not None:
            value, first = tied(value, first), None
        offsets += [j ^ by for j in offsets]
        by //= 2
    size = value.shape[0] // count
    where = [offsets.index(j) for j in range(count)]
    return jnp.concatenate([value[i * size : (i + 1) * size] for i in where], axis=0)


def blocks_turned(value, by, owners):
    size = value.shape[-1] // owners
    return jnp.concatenate([value[..., (j ^ by) * size : ((j ^ by) + 1) * size] for j in range(owners)], axis=-1)


def to_owner(value, axis, turn=False):
    count = lax.axis_size(axis)
    by = 1
    while by < count:
        value = value.reshape((value.shape[0] // 2, 2) + value.shape[1:])
        other = swap(value[:, 1].astype(bf16), axis, by).astype(f32)
        value = value[:, 0] + (blocks_turned(other, by, count) if turn else other)
        by *= 2
    return value[0]


def halved(value, axis, by):
    value = value.reshape((value.shape[0] // 2, 2) + value.shape[1:])
    bit = (lax.axis_index(axis) // by) % 2
    keep = lax.dynamic_index_in_dim(value, bit, 1, False)
    give = lax.dynamic_index_in_dim(value, 1 - bit, 1, False)
    return (keep.astype(f32) + swap(give, axis, by).astype(f32)).astype(bf16)


def halved_from(value, axis, by):
    while value.shape[0] > 1:
        value = halved(value, axis, by)
        by *= 2
    return value[0]


def tied(value, *others):
    return lax.optimization_barrier((value, others))[0]


def gather_step(value, axis, by):
    return jnp.concatenate([value, swap(value, axis, by)], axis=0)


def gathered(value, axis, by):
    while by:
        value = gather_step(value, axis, by)
        by //= 2
    return value


def reversed_bits(j, count):
    out, by = 0, 1
    while by < count:
        out = out * 2 + (j // by) % 2
        by *= 2
    return out


def traded(value, axis):
    count = lax.axis_size(axis)
    size = value.shape[-1] // count
    parts = [value[:, j * size : (j + 1) * size] for j in range(count)]
    return jnp.stack([swap(part, axis, j) if j else part for j, part in enumerate(parts)])


def exchange(value, axis):
    return lax.all_to_all(value, axis, 0, 0)


def in_order(parts, index):
    stacked = jnp.stack(parts)
    return jnp.concatenate([lax.dynamic_index_in_dim(stacked, index ^ a, 0) for a in range(len(parts))])


def assemble_kernel(ids_ref, gate_ref, *refs, share, heads):
    conv_refs, (weight_ref, out_ref, tail_ref, sum_ref) = refs[:-4], refs[-4:]
    step = pl.program_id(0)
    count, owners = gate_ref.shape[:2]
    channels = out_ref.shape[0]

    def place_of(q):
        return reversed_bits(ids_ref[0] ^ q, count)

    @pl.when(step == 0)
    def _():
        sum_ref[...] = jnp.zeros_like(sum_ref)

    def put(at, value):
        size = value.shape[0]
        out_ref[at : at + size] = value
        sum_ref[0:1] += jnp.sum(value * weight_ref[at : at + size].astype(f32), axis=0, keepdims=True)

    def parts():
        at = 0
        for ref in conv_refs:
            for q in range(count):
                yield at, ref, q
                at += ref.shape[2]

    @pl.when(step < owners)
    def _():
        rows = gate_ref.shape[2]
        for q in range(count):
            put(q * rows, gate_ref[place_of(q), ids_ref[1] ^ step].astype(f32))

    @pl.when(step // owners == 1)
    def _():
        for at, ref, q in parts():
            size = min(ref.shape[2], channels - at)
            if size > 0:
                put(at, ref[place_of(q), ids_ref[1] ^ (step % owners), :size].astype(f32))

    @pl.when(step == 2 * owners)
    def _():
        for a in range(owners):
            found = []
            for at, ref, q in parts():
                skip = max(0, channels - at)
                if skip < ref.shape[2]:
                    found.append(ref[place_of(q), ids_ref[1] ^ a].astype(f32)[skip:])
            value = jnp.concatenate(found, axis=0)
            tail_ref[a] = value
            put(a * share, value[:share])
            put(owners * share + a * heads, value[share : share + heads])


def rows_kernel(ids_ref, *refs, parts):
    bufs, (weight_ref, out_ref, sum_ref) = refs[: len(parts)], refs[len(parts) :]
    total = jnp.zeros((out_ref.shape[0], 1), f32)
    for ref, (start, size) in zip(bufs, parts, strict=True):
        value = ref[0].astype(f32)
        out_ref[:, start : start + size] = value
        total = total + jnp.sum(value * weight_ref[:, start : start + size].astype(f32), axis=1, keepdims=True)
    sum_ref[...] = total


def per_device(tokens, lengths, norm_gain, in_weight, conv_weight, conv_bias, dt_bias, decay_log, skip_gain, gated_gain, out_weight, cotangent):
    nf, nq = lax.axis_size("fsdp"), lax.axis_size("seq")
    me, place = lax.axis_index("fsdp"), lax.axis_index("seq")
    _, seg, width = tokens.shape
    rows = in_weight.shape[0]
    channels = out_weight.shape[0]
    inner = channels * nf
    heads = dt_bias.shape[0]
    conv_own = conv_weight.shape[1]
    state = (conv_own * nf - inner) // 2
    share = 2 * state // nf
    slots = nf

    ids = jnp.stack([place, me]).astype(jnp.int32)
    per_slot = nq // slots
    piece = channels // per_slot

    weight = in_weight.T
    half, side = channels // 2, place % 2
    got = []
    for j in range(nf):
        start = inner + (me ^ j) * channels
        if j < 2:
            give = lax.dynamic_slice_in_dim(weight, start, channels, 0)
            got.append(swap(give, "fsdp", j) if j else give)
        else:
            mine = swap(lax.dynamic_slice_in_dim(weight, start + side * half, half, 0), "fsdp", j)
            got += [mine, swap(mine, "seq", 1)]
    own_tokens = tied(tokens, got[2::2])
    x_main = all_slots(own_tokens, "fsdp", got[3::2])
    before = lax.ppermute(tokens[0, seg - 3 :], "seq", [(i, i + 1) for i in range(nq - 1)])

    def padded(rows_):
        return jnp.pad(rows_, ((0, 0), (0, width - rows_.shape[1])))

    small = jnp.concatenate(
        [padded(conv_weight), padded(conv_bias[None]), padded(norm_gain[None]), jnp.zeros((7, width), bf16), before], axis=0
    )
    x_small = all_slots(small[None], "fsdp")
    listed = [x_small[j] for j in range(nf)]
    norm_all = in_order([part[5, :rows] for part in listed], me).astype(f32).reshape(1, width)
    taps_all = in_order([part[:5, :conv_own] for part in listed], me).astype(f32)
    taps_all = taps_all.reshape(nf, 5, conv_own).transpose(1, 0, 2).reshape(5, -1)
    taps_all = jnp.pad(taps_all, ((0, 3), (0, 0)))
    taps = jnp.concatenate([lax.dynamic_slice_in_dim(taps_all, me * channels, channels, 1), taps_all[:, inner:]], axis=1)
    taps_share = lax.dynamic_slice_in_dim(taps_all, inner + me * share, share, 1)
    rate = jnp.stack([dt_bias.astype(f32), jnp.exp(decay_log.astype(f32))])
    rate = jnp.pad(rate, ((0, 6), (0, lanes - heads)))
    vec = jnp.stack([jnp.repeat(skip_gain.astype(f32), head_size), gated_gain.astype(f32)])
    vec = jnp.pad(vec, ((0, 6), (0, 0)))

    rest = all_slots(weight[2 * inner :][None], "fsdp")
    cw = channels + 2 * state
    (w_conv,) = call(
        weight_kernel,
        1,
        [(part, None) for part in got] + [(rest, None)],
        [((cw + lanes, width), bf16, None)],
        "weights",
        ids=ids,
        owners=nf,
        state=state,
        heads=heads,
    )

    (normed,) = call(
        normalize_kernel,
        slots,
        [(x_main, each), (x_small, each), (norm_all, None)],
        [((slots, halo + seg, width), bf16, each)],
        "normalize",
        ids=ids,
        owners=nf,
    )
    inputs = tokens[0].astype(f32)
    valid = (place * seg + jnp.arange(seg) < lengths[0]).astype(f32)[:, None]
    upstream = valid * cotangent[0].astype(f32)

    gives = [lax.dynamic_slice_in_dim(weight, (me ^ j) * channels, channels, 0) for j in range(nf)]
    gives, later = tied((gives, upstream.astype(bf16)), got[-1])
    w_gate = jnp.concatenate([swap(g, "fsdp", j) if j else g for j, g in enumerate(gives)], axis=1)
    back_branch = all_slots(later[None], "fsdp")

    def project(x, w):
        return lax.dot_general(x, w, (((2,), (1,)), ((), ())), preferred_element_type=f32)

    pc = project(normed, w_conv).astype(bf16)
    main = normed[:, halo:]
    tall = 16
    statics = dict(channels=channels, state=state)
    turned = (per_slot, lambda s, *i: s)
    act, y_local, s_local, lac, dtc, lar, dtr = call(
        forward_kernel,
        slots,
        [(pc, each), (taps, None), (rate, None)],
        [
            ((slots, seg, cw), bf16, each),
            ((slots, seg, channels), f32, each),
            ((nq, piece + 16, state), bf16, turned),
            ((slots, seg, lanes), f32, each),
            ((slots, seg, lanes), f32, each),
            ((slots, tall, seg), f32, each),
            ((slots, tall, seg), f32, each),
        ],
        "forward",
        far=True,
        flops=2 * slots * seg * seg * channels,
        rows=piece,
        **statics,
    )

    came = exchange(s_local, "seq")
    (reached,) = call(
        chain_kernel, 1, [(came, None)], [((nq, piece, state), bf16, None)], "chain", ids=ids, rows=piece, count=per_slot
    )
    s_in = exchange(reached, "seq").reshape(slots, channels, state)

    gate = project(main, w_gate).astype(bf16)
    bg = lax.dot_general(back_branch, out_weight, (((2,), (1,)), ((), ())), preferred_element_type=f32)
    y, stats = call(
        finish_kernel,
        slots,
        [(y_local, each), (act, each), (lac, each), (s_in, each), (gate, each), (bg, each), (vec, None)],
        [((slots, seg, channels), f32, each), ((slots, 8, seg), f32, each)],
        "finish",
        far=True,
        **statics,
    )
    shares = [(swap(stats, "fsdp", j) if j else stats, (1, lambda s, j=j: s ^ j)) for j in range(nf)]
    gated_out, dgate, dy, pos, dsin, dskip = call(
        norm_kernel,
        slots,
        [(y, each), (act, each), (lac, each), (gate, each), (bg, each), (vec, None)] + shares,
        [
            ((slots, seg, channels), bf16, each),
            ((slots, seg, channels), bf16, each),
            ((slots, seg, channels), f32, each),
            ((slots, seg, lanes), f32, each),
            ((nq, piece, state), bf16, turned),
            ((8, channels), f32, None),
        ],
        "norm",
        far=True,
        inner=inner,
        rows=piece,
        **statics,
    )

    def grad_of(dz, x):
        return lax.dot_general(dz, x, (((0, 1), (0, 1)), ((), ())), preferred_element_type=f32).astype(bf16)

    def cut(value):
        size = value.shape[-1] // 2
        return [value] if size // nq % 8 else [value[..., :size], value[..., size:]]

    def pieces(g):
        return g.reshape((nq, g.shape[0] // nq) + g.shape[1:])

    back_came = exchange(dsin, "seq")
    out_sum = lax.psum_scatter(pieces(grad_of(gated_out, back_branch)), "seq", scatter_dimension=0)
    gate_sum = halved(pieces(grad_of(dgate, main)), "seq", 1)
    back_came, gate_sum = lax.optimization_barrier((back_came, gate_sum))
    gate_sum = halved(gate_sum, "seq", 2)
    (reached,) = call(
        back_chain_kernel,
        1,
        [(back_came, None), (came, None)],
        [((nq, piece, state), bf16, None)],
        "back_chain",
        ids=ids,
        rows=piece,
        count=per_slot,
    )
    g_end = exchange(reached, "seq").reshape(slots, channels, state)
    g_end, gate_sum = lax.optimization_barrier((g_end, gate_sum))
    gate_sum = halved_from(gate_sum, "seq", 4)

    r_local, dbc = call(
        backward_kernel,
        slots,
        [(act, each), (dy, each), (lac, each), (lar, each), (dtr, each), (s_in, each)],
        [((slots, seg, channels), f32, each), ((slots, seg, 2 * state), f32, each)],
        "backward",
        far=True,
        flops=4 * slots * seg * seg * channels,
        **statics,
    )
    d_shares = call(
        rows_grad_kernel,
        slots,
        [(act, each), (lac, each), (dtc, each), (g_end, each), (dbc, each)],
        [((slots, share, seg), bf16, each)] * nf,
        "rows_grad",
        ids=ids,
        scratch=[pltpu.VMEM((2 * state, seg), f32)],
        **statics,
    )
    d_shares = [(swap(d, "fsdp", j) if j else d, (1, lambda s, i, j=j: s ^ j)) for j, d in enumerate(d_shares)]
    r_local, gate_sum = lax.optimization_barrier((r_local, gate_sum))
    gate_sum = traded(gate_sum, "fsdp")
    dpre, first, dstep, dtaps, drate = call(
        carry_kernel,
        slots,
        [
            (pc, each), (taps, None), (rate, None), (act, each), (dy, each), (r_local, each), (pos, each), (lac, each),
            (dtc, each), (g_end, each), (s_in, each), (s_local, turned), (vec, None),
        ],
        [
            ((slots, seg, channels), f32, each),
            ((slots, 8, channels), f32, each),
            ((slots, seg, lanes), bf16, each),
            ((8, channels), f32, None),
            ((8, lanes), f32, None),
        ],
        "carry",
        far=True,
        rows=piece,
        **statics,
    )
    dstep, gate_sum = lax.optimization_barrier((dstep, gate_sum))
    pc_later, dpre = lax.optimization_barrier((pc, dpre))
    gate_sum = gather_step(gate_sum[None], "seq", nq // 2)
    dpre_share, first_share, dtaps_share = call(
        share_kernel,
        slots,
        [(pc_later, each), (taps_share.T, None)] + d_shares,
        [((slots, seg, lanes), f32, each), ((slots, 8, lanes), f32, each), ((share, lanes), f32, None)],
        "share",
        ids=ids,
        scratch=[pltpu.VMEM((2 * state, seg), f32)],
        **statics,
    )
    behind = [(i, i - 1) for i in range(1, nq)]
    after = lax.ppermute(jnp.concatenate([first, first_share], axis=2), "seq", behind)
    after, gate_sum = lax.optimization_barrier((after, gate_sum))
    gate_sum = gather_step(gate_sum, "seq", nq // 4)
    taps_back = jnp.concatenate([taps[:, :channels], jnp.pad(taps_share, ((0, 0), (0, lanes - share)))], axis=1)
    (dconv,) = call(
        returned_kernel,
        slots,
        [(dpre, each), (dpre_share, each), (after, each), (taps_back, None), (dstep, each)],
        [((slots, seg, channels + lanes), bf16, each)],
        "returned",
        share=share,
        heads=heads,
    )

    dconv, gate_sum = lax.optimization_barrier((dconv, gate_sum))
    gate_bufs = [gathered(gate_sum, "seq", nq // 8)]

    per = channels // rows
    head_rows = jnp.stack([drate[0, :heads], drate[1, :heads], jnp.sum(dskip[0].reshape(heads, head_size), axis=1)])
    block = jnp.concatenate(
        [
            dtaps[:5].reshape(5 * per, rows),
            jnp.pad(dtaps_share[:, :5].T, ((0, 0), (0, rows - share))),
            jnp.pad(head_rows, ((0, 0), (0, rows - heads))),
        ],
        axis=0,
    )
    extra = block.shape[0]
    block = jnp.tile(block, (1, nf)).astype(bf16)
    conv_grads = [grad_of(part, main) for part in cut(dconv)]
    spare = channels + share + heads - sum(g.shape[0] for g in conv_grads[:-1])
    conv_grads[-1] = lax.dynamic_update_slice_in_dim(conv_grads[-1], block, spare, 0)

    def shared(g):
        return gathered(traded(g, "fsdp")[None], "seq", nq // 2)

    out_unit = channels // nq
    out_parts = [lax.all_gather(out_sum, "seq")]
    conv_sums = [halved_from(pieces(g), "seq", 1) for g in conv_grads]
    conv_sums, out_parts = lax.optimization_barrier((conv_sums, out_parts))
    conv_bufs = [shared(g) for g in conv_sums]
    place_of = jnp.stack([reversed_bits(place ^ q, nq) for q in range(nq)])
    if all(buf.shape[2] % 8 == 0 for buf in gate_bufs + conv_bufs):
        g_in, tail, norm_sum = call(
            assemble_kernel,
            2 * nf + 1,
            [(buf, None) for buf in gate_bufs + conv_bufs] + [(weight, (channels, lambda s, i: s))],
            [
                (weight.shape, f32, (channels, lambda s, i: s)),
                ((nf, lanes, rows), f32, None),
                ((8, rows), f32, None),
            ],
            "assemble",
            ids=ids,
            share=share,
            heads=heads,
        )
        norm_sum = norm_sum[0]
    else:
        order = me ^ jnp.arange(nf)

        def natural(bufs):
            bufs = [buf[place_of][:, order].astype(f32).transpose(1, 0, 2, 3).reshape(nf, -1, rows) for buf in bufs]
            return jnp.concatenate(bufs, axis=1)

        gate_all, conv_all = natural(gate_bufs), natural(conv_bufs)
        tail = conv_all[:, channels:]
        joined = [gate_all.reshape(inner, rows), conv_all[:, :channels].reshape(inner, rows)]
        joined += [tail[:, :share].reshape(nf * share, rows), tail[:, share : share + heads].reshape(nf * heads, rows)]
        g_in = jnp.concatenate(joined, axis=0)
        norm_sum = jnp.sum(g_in * weight.astype(f32), axis=0)
    if out_unit % 16 == 0:
        sizes = [part.shape[-1] for part in out_parts]
        g_out, gated_sum = call(
            rows_kernel,
            nq,
            [(part, (1, lambda s, i: s)) for part in out_parts] + [(out_weight, (out_unit, lambda s, i: s))],
            [(out_weight.shape, f32, (out_unit, lambda s, i: s)), ((channels, 1), f32, (out_unit, lambda s, i: s))],
            "rows",
            ids=ids,
            parts=[(sum(sizes[:i]), size) for i, size in enumerate(sizes)],
        )
        gated_sum = gated_sum[:, 0]
    else:
        g_out = jnp.concatenate([part.astype(f32).reshape(channels, -1) for part in out_parts], axis=1)
        gated_sum = jnp.sum(g_out * out_weight.astype(f32), axis=1)

    norm_grad = norm_sum / norm_gain.astype(f32)
    gated_grad = gated_sum / gated_gain.astype(f32)

    got = tail[:, share + heads : share + heads + extra]
    tap_grads = jnp.concatenate(
        [
            got[:, : 5 * per].reshape(nf, 5, channels).transpose(1, 0, 2).reshape(5, inner),
            got[:, 5 * per : 5 * per + 5, :share].transpose(1, 0, 2).reshape(5, 2 * state),
        ],
        axis=1,
    )
    tap_grads = lax.dynamic_slice_in_dim(tap_grads, me * conv_own, conv_own, 1)
    head_grads = lax.dynamic_index_in_dim(got, me, 0, False)[5 * per + 5 :, :heads]

    branch = lax.dot_general(gated_out, out_weight, (((2,), (0,)), ((), ())), preferred_element_type=f32)
    branch = to_owner(branch, "fsdp")
    mixed = (valid * (inputs + branch)).astype(bf16)

    w_share = lax.dynamic_slice_in_dim(w_conv, channels + me * share, share, 0)
    w_last = jnp.concatenate([w_share, w_conv[cw : cw + lanes - share]], axis=0)

    def back(dz, w):
        return lax.dot_general(dz, w, (((2,), (0,)), ((), ())), preferred_element_type=f32)

    bn = back(dgate, w_gate) + back(dconv[..., :channels], w_conv[:channels]) + back(dconv[..., channels:], w_last)
    bn = to_owner(bn, "fsdp", turn=True)
    (input_grad,) = call(
        input_kernel,
        1,
        [(bn, None), (norm_all, None), (tokens[0], None), (cotangent[0], None), (valid, None)],
        [((seg, width), f32, None)],
        "input",
        ids=ids,
        owners=nf,
    )
    return (
        mixed[None],
        input_grad[None],
        norm_grad,
        g_in.T,
        tap_grads[:4],
        tap_grads[4],
        head_grads[0],
        head_grads[1],
        head_grads[2],
        gated_grad,
        g_out,
    )


def solution(mesh):
    whole, rows = P("fsdp", "seq", None), P("fsdp", None)
    one, columns = P("fsdp"), P(None, "fsdp")
    return jax.shard_map(
        per_device,
        mesh=mesh,
        in_specs=(whole, one, one, rows, columns, one, one, one, one, one, rows, whole),
        out_specs=(whole, whole, one, rows, columns, one, one, one, one, one, rows),
        check_vma=False,
    )
```

```python
import functools

import jax
import jax.numpy as jnp
from jax import lax
from jax.experimental import pallas as pl
from jax.experimental.pallas import tpu as pltpu
from jax.sharding import PartitionSpec as P

epsilon = 1e-05
bf16, f32 = jnp.bfloat16, jnp.float32
best = lax.Precision.HIGHEST
halo = 16
lanes = 128
head_size = 64


def dot(a, b, ca=1, cb=0, precision=None):
    return lax.dot_general(
        a, b, (((ca,), (cb,)), ((), ())), preferred_element_type=f32, precision=precision
    )


def sigmoid(v):
    return 1.0 / (1.0 + jnp.exp(-v))


def iota(shape, axis):
    return lax.broadcasted_iota(jnp.int32, shape, axis)


def spread(columns, pair):
    first, second = 2 * pair, 2 * pair + 1
    rows = columns.shape[0]
    return jnp.where(
        iota((rows, lanes), 1) < head_size,
        columns[:, first : first + 1],
        columns[:, second : second + 1],
    )


def per_head(total, products, pair):
    rows = products.shape[0]
    lane = iota((rows, lanes), 1)
    low = jnp.sum(jnp.where(lane < head_size, products, 0.0), axis=1, keepdims=True)
    high = jnp.sum(jnp.where(lane < head_size, 0.0, products), axis=1, keepdims=True)
    return total + jnp.where(lane == 2 * pair, low, jnp.where(lane == 2 * pair + 1, high, 0.0))


def in_heads(products, pair):
    rows = jnp.sum(products, axis=1, keepdims=True)
    low, high = jnp.sum(rows[:head_size]), jnp.sum(rows[head_size:])
    lane = iota((1, lanes), 1)
    return jnp.where(lane == 2 * pair, low, jnp.where(lane == 2 * pair + 1, high, 0.0))


def convolved(pc_ref, taps_ref, at):
    x = pc_ref[0, :, at : at + lanes].astype(f32)
    tapped = [pltpu.roll(x, 3 - k, 0)[halo:] for k in range(3)] + [x[halo:]]
    pre = taps_ref[4:5, at : at + lanes]
    for k in range(4):
        pre = pre + tapped[k] * taps_ref[k : k + 1, at : at + lanes]
    return tapped, pre


def pieces_out(out_ref, whole, rows):
    for p in range(out_ref.shape[0]):
        out_ref[p, :rows] = whole[p * rows : (p + 1) * rows]


def pieces_in(ref, rows):
    return jnp.concatenate([ref[p, :rows] for p in range(ref.shape[0])], axis=0)


def block_of(index, size):
    return pl.ds(pl.multiple_of(index * size, size), size)


def columns_of(ref, index, size):
    if size % lanes == 0:
        return ref[:, block_of(index, size)]
    value = ref[:, :size]
    for a in range(1, ref.shape[1] // size):
        value = jnp.where(index == a, ref[:, a * size : (a + 1) * size], value)
    return value


def normalize_kernel(ids_ref, main_ref, small_ref, gain_ref, out_ref, *, owners):
    size = out_ref.shape[2] // owners
    for ref, at in ((small_ref, 0), (main_ref, halo)):
        x = ref[0].astype(f32)
        inv = lax.rsqrt(jnp.mean(x * x, axis=1, keepdims=True) + epsilon)
        for j in range(owners):
            own = ids_ref[1] ^ j
            part = columns_of(ref.at[0], own, size).astype(f32) * inv * columns_of(gain_ref, own, size)
            out_ref[0, at : at + x.shape[0], j * size : (j + 1) * size] = part.astype(bf16)


def weight_kernel(ids_ref, *refs, owners, state, heads):
    rest_ref, out_ref = refs[-2:]
    size = rest_ref.shape[2]
    channels = out_ref.shape[0] - 2 * state - lanes
    n = 0
    for j in range(owners):
        own = slice(j * size, (j + 1) * size)
        if j < 2:
            out_ref[:channels, own] = refs[n][...]
            n += 1
        else:
            half = channels // 2
            for side in range(2):
                out_ref[block_of((ids_ref[0] % 2) ^ side, half), own] = refs[n][...]
                n += 1
        out_ref[channels : channels + 2 * state, own] = rest_ref[j, : 2 * state]
        rows = owners * heads
        pick = iota((lanes, rows), 1) == ids_ref[1] * heads + iota((lanes, rows), 0)
        pick = jnp.where(iota((lanes, rows), 0) < heads, pick.astype(f32), 0.0).astype(bf16)
        out_ref[channels + 2 * state :, own] = dot(pick, rest_ref[j, 2 * state : 2 * state + rows]).astype(bf16)


def input_kernel(ids_ref, bn_ref, gain_ref, tokens_ref, cot_ref, valid_ref, out_ref, *, owners):
    x = tokens_ref[...].astype(f32)
    width = x.shape[1]
    size = width // owners
    inv = lax.rsqrt(jnp.mean(x * x, axis=1, keepdims=True) + epsilon)
    lean = jnp.zeros_like(inv)
    for a in range(owners):
        here = slice(a * size, (a + 1) * size)
        bn = columns_of(bn_ref, ids_ref[1] ^ a, size) * gain_ref[:, here]
        lean = lean + jnp.sum(bn * x[:, here], axis=1, keepdims=True)
    lean = lean * (inv * inv * inv) * (1.0 / width)
    for a in range(owners):
        here = slice(a * size, (a + 1) * size)
        bn = columns_of(bn_ref, ids_ref[1] ^ a, size) * gain_ref[:, here]
        out_ref[:, here] = valid_ref[...] * cot_ref[:, here].astype(f32) + inv * bn - x[:, here] * lean


def of_rows(row, ids_ref, rows, count):
    head = ((ids_ref[0] % count) * rows + iota((rows, lanes), 0)) // head_size
    return jnp.sum(jnp.where(iota((rows, lanes), 1) == head, row, 0.0), axis=1, keepdims=True)


def chain_kernel(ids_ref, in_ref, out_ref, *, rows, count):
    carried = jnp.zeros((rows, lanes), f32)
    for i in range(in_ref.shape[0]):
        out_ref[i] = carried.astype(bf16)
        row = in_ref[i, rows : rows + 1].astype(f32) + in_ref[i, rows + 1 : rows + 2].astype(f32)
        carried = of_rows(row, ids_ref, rows, count) * carried + in_ref[i, :rows].astype(f32)


def back_chain_kernel(ids_ref, in_ref, decay_ref, out_ref, *, rows, count):
    carried = jnp.zeros((rows, lanes), f32)
    for i in reversed(range(in_ref.shape[0])):
        out_ref[i] = carried.astype(bf16)
        row = decay_ref[i, rows : rows + 1].astype(f32) + decay_ref[i, rows + 1 : rows + 2].astype(f32)
        carried = of_rows(row, ids_ref, rows, count) * carried + in_ref[i].astype(f32)


def forward_kernel(pc_ref, taps_ref, rate_ref, act_ref, y_ref, s_ref, lac_ref, dtc_ref, lar_ref, dtr_ref, *, channels, state, rows):
    width = channels + 2 * state
    for at in range(0, width, lanes):
        _, pre = convolved(pc_ref, taps_ref, at)
        act_ref[0, :, at : at + lanes] = (pre * sigmoid(pre)).astype(bf16)
    seg = act_ref.shape[1]
    z = pc_ref[0, halo:, width : width + lanes].astype(f32) + rate_ref[0:1]
    dtc = jnp.maximum(z, 0.0) + jnp.log1p(jnp.exp(-jnp.abs(z)))
    lower = iota((seg, seg), 0) >= iota((seg, seg), 1)
    lac = dot(lower.astype(f32), -dtc * rate_ref[1:2], precision=best)
    tall = lar_ref.shape[1]
    lar, dtr = lac.T[:tall], dtc.T[:tall]
    lac_ref[0], dtc_ref[0], lar_ref[0], dtr_ref[0] = lac, dtc, lar, dtr
    b_rows = act_ref[0, :, channels : channels + state]
    c_rows = act_ref[0, :, channels + state : width]
    both = dot(c_rows, b_rows, 1, 1)
    to_end = jnp.exp(lac[seg - 1 : seg] - lac) * dtc
    states = []
    for pair in range(channels // lanes):
        at = pair * lanes
        values = act_ref[0, :, at : at + lanes]
        parts = []
        for side in range(2):
            h = 2 * pair + side
            mix = jnp.where(lower, jnp.exp(lac[:, h : h + 1] - lar[h : h + 1]), 0.0) * both * dtr[h : h + 1]
            parts.append(dot(mix.astype(bf16), values[:, side * head_size : (side + 1) * head_size]))
        y_ref[0, :, at : at + lanes] = jnp.concatenate(parts, axis=1)
        weighted = (spread(to_end, pair) * values.astype(f32)).astype(bf16)
        states.append(dot(weighted, b_rows, 0, 0).astype(bf16))
    pieces_out(s_ref, jnp.concatenate(states, axis=0), rows)
    whole = jnp.exp(lac[seg - 1 : seg])
    high = whole.astype(bf16).astype(f32)
    row = iota((16, lanes), 0)
    tail = jnp.where(row == 0, high, jnp.where(row == 1, whole - high, 0.0)).astype(bf16)
    for p in range(s_ref.shape[0]):
        s_ref[p, rows:] = tail


def finish_kernel(y_ref, act_ref, lac_ref, sin_ref, gate_ref, bg_ref, vec_ref, y_out, stat_ref, *, channels, state):
    seg = y_ref.shape[1]
    c_rows = act_ref[0, :, channels + state : channels + 2 * state]
    decay = jnp.exp(lac_ref[0])
    first = jnp.zeros((seg, 1), f32)
    second = jnp.zeros((seg, 1), f32)
    for pair in range(channels // lanes):
        at = pair * lanes
        here = slice(at, at + lanes)
        carried = dot(c_rows, sin_ref[0, here], 1, 1)
        y = y_ref[0, :, here] + spread(decay, pair) * carried
        y_out[0, :, here] = y
        gate = gate_ref[0, :, here].astype(f32)
        heads = y + vec_ref[0:1, here] * act_ref[0, :, here].astype(f32)
        gated = heads * gate * sigmoid(gate)
        first = first + jnp.sum(gated * gated, axis=1, keepdims=True)
        second = second + jnp.sum(gated * bg_ref[0, :, here] * vec_ref[1:2, here], axis=1, keepdims=True)
    lane = iota((seg, lanes), 1)
    both = jnp.where(lane == 0, first, jnp.where(lane == 1, second, 0.0))
    stat_ref[0] = both.T[:8]


def norm_kernel(y_ref, act_ref, lac_ref, gate_ref, bg_ref, vec_ref, *refs, channels, state, inner, rows):
    stat_refs, (out_ref, dgate_ref, dy_ref, pos_ref, dsin_ref, dskip_ref) = refs[:-6], refs[-6:]
    seg = y_ref.shape[1]
    stats = sum(ref[0] for ref in stat_refs).T
    states = []
    inv = lax.rsqrt(stats[:, 0:1] * (1.0 / inner) + epsilon)
    lean = inv * inv * inv * (stats[:, 1:2] * (1.0 / inner))
    c_rows = act_ref[0, :, channels + state : channels + 2 * state]
    decay = jnp.exp(lac_ref[0])
    pos = jnp.zeros((seg, lanes), f32)

    @pl.when(pl.program_id(0) == 0)
    def _():
        dskip_ref[...] = jnp.zeros_like(dskip_ref)

    for pair in range(channels // lanes):
        at = pair * lanes
        here = slice(at, at + lanes)
        y = y_ref[0, :, here]
        values = act_ref[0, :, here].astype(f32)
        heads = y + vec_ref[0:1, here] * values
        gate = gate_ref[0, :, here].astype(f32)
        sg = sigmoid(gate)
        gated = heads * gate * sg
        gain = vec_ref[1:2, here]
        out_ref[0, :, here] = (gated * inv * gain).astype(bf16)
        dgated = inv * (bg_ref[0, :, here] * gain) - gated * lean
        dgate_ref[0, :, here] = (dgated * heads * (sg * (1.0 + gate * (1.0 - sg)))).astype(bf16)
        dy = dgated * gate * sg
        dy_ref[0, :, here] = dy
        pos = per_head(pos, dy * y, pair)
        states.append(dot((spread(decay, pair) * dy).astype(bf16), c_rows, 0, 0).astype(bf16))
        dskip_ref[0:1, here] += jnp.sum(dy * values, axis=0, keepdims=True)
    pos_ref[0] = pos
    pieces_out(dsin_ref, jnp.concatenate(states, axis=0), rows)


def backward_kernel(act_ref, dy_ref, lac_ref, lar_ref, dtr_ref, sin_ref, r_ref, dbc_ref, *, channels, state):
    seg = dy_ref.shape[1]
    b_rows = act_ref[0, :, channels : channels + state]
    c_rows = act_ref[0, :, channels + state : channels + 2 * state]
    both = dot(c_rows, b_rows, 1, 1)
    lower = iota((seg, seg), 0) >= iota((seg, seg), 1)
    lac, lar, dtr = lac_ref[0], lar_ref[0], dtr_ref[0]
    decay = jnp.exp(lac)
    dboth = jnp.zeros((seg, seg), f32)
    dc = jnp.zeros((seg, state), f32)
    for pair in range(channels // lanes):
        at = pair * lanes
        here = slice(at, at + lanes)
        values = act_ref[0, :, here]
        dy = dy_ref[0, :, here]
        dyl = dy.astype(bf16)
        parts = []
        for side in range(2):
            h = 2 * pair + side
            own = slice(side * head_size, (side + 1) * head_size)
            weights = jnp.where(lower, jnp.exp(lac[:, h : h + 1] - lar[h : h + 1]), 0.0)
            parts.append(dot((weights * both).astype(bf16), dyl[:, own], 0, 0))
            dboth = dboth + dot(dyl[:, own], values[:, own], 1, 1) * (weights * dtr[h : h + 1])
        r_ref[0, :, here] = jnp.concatenate(parts, axis=1)
        dc = dc + dot((spread(decay, pair) * dy).astype(bf16), sin_ref[0, here])
    dlow = dboth.astype(bf16)
    dbc_ref[0, :, :state] = dot(dlow, c_rows, 0, 0)
    dbc_ref[0, :, state:] = dc + dot(dlow, b_rows)


def rows_grad_kernel(ids_ref, act_ref, lac_ref, dtc_ref, g_ref, dbc_ref, *refs, channels, state):
    out_refs, hold = refs[:-1], refs[-1]
    seg = act_ref.shape[1]
    lac, dtc = lac_ref[0], dtc_ref[0]
    weights = jnp.exp(lac[seg - 1 : seg] - lac) * dtc
    db = dbc_ref[0, :, :state]
    for pair in range(channels // lanes):
        here = slice(pair * lanes, (pair + 1) * lanes)
        db = db + dot((spread(weights, pair) * act_ref[0, :, here].astype(f32)).astype(bf16), g_ref[0, here])
    hold[:state] = db.T
    hold[state:] = dbc_ref[0, :, state:].T
    share = out_refs[0].shape[1]
    for j, out_ref in enumerate(out_refs):
        out_ref[0] = hold[block_of(ids_ref[1] ^ j, share)].astype(bf16)


def share_kernel(ids_ref, pc_ref, taps_ref, *refs, channels, state):
    parts, (dpre_ref, first_ref, dtaps_ref, hold) = refs[:-4], refs[-4:]
    seg = pc_ref.shape[1] - halo
    share = parts[0].shape[1]
    own = block_of(ids_ref[1], share)
    hold[...] = pc_ref[0, :, channels : channels + 2 * state].astype(f32)[halo:].T
    x = hold[own]
    hold[:, :halo] = pc_ref[0, :halo, channels : channels + 2 * state].astype(f32).T
    edge = hold[own, :halo]
    lane = iota((share, seg), 1)
    tapped = []
    for k in range(3):
        value = pltpu.roll(x, 3 - k, 1)
        for t in range(3 - k):
            value = jnp.where(lane == t, edge[:, halo - 3 + k + t : halo - 2 + k + t], value)
        tapped.append(value)
    tapped.append(x)
    pre = taps_ref[:, 4:5] + sum(tapped[k] * taps_ref[:, k : k + 1] for k in range(4))
    sg = sigmoid(pre)
    dpre = sum(ref[0].astype(f32) for ref in parts) * (sg * (1.0 + pre * (1.0 - sg)))

    @pl.when(pl.program_id(0) == 0)
    def _():
        dtaps_ref[...] = jnp.zeros_like(dtaps_ref)

    lane = iota((share, lanes), 1)
    total = jnp.zeros((share, lanes), f32)
    for k in range(5):
        column = jnp.sum(dpre * tapped[k] if k < 4 else dpre, axis=1, keepdims=True)
        total = jnp.where(lane == k, column, total)
    dtaps_ref[...] += total
    rows = jnp.concatenate([dpre, jnp.zeros((lanes - share, seg), f32)], axis=0).T
    dpre_ref[0] = rows
    first_ref[0] = rows[:8]


def carry_kernel(pc_ref, taps_ref, rate_ref, act_ref, dy_ref, r_ref, pos_ref, lac_ref, dtc_ref, g_ref, sin_ref, s_ref, vec_ref, dpre_ref, first_ref, dstep_ref, dtaps_ref, drate_ref, *, channels, state, rows):
    seg = dy_ref.shape[1]
    width = channels + 2 * state
    b_rows = act_ref[0, :, channels : channels + state]
    lac, dtc = lac_ref[0], dtc_ref[0]
    last = lac[seg - 1 : seg]
    to_last = jnp.exp(last - lac)
    neg = jnp.zeros((seg, lanes), f32)
    through = jnp.zeros((1, lanes), f32)
    local = jnp.zeros((1, lanes), f32)
    states = pieces_in(s_ref, rows)

    @pl.when(pl.program_id(0) == 0)
    def _():
        dtaps_ref[...] = jnp.zeros_like(dtaps_ref)
        drate_ref[...] = jnp.zeros_like(drate_ref)

    for pair in range(channels // lanes):
        at = pair * lanes
        here = slice(at, at + lanes)
        grad = g_ref[0, here]
        values = act_ref[0, :, here].astype(f32)
        r = r_ref[0, :, here] + spread(to_last, pair) * dot(b_rows, grad, 1, 1)
        neg = per_head(neg, values * r, pair)
        wide = grad.astype(f32)
        through = through + in_heads(wide * sin_ref[0, here].astype(f32), pair)
        local = local + in_heads(wide * states[here].astype(f32), pair)
        tapped, pre = convolved(pc_ref, taps_ref, at)
        sg = sigmoid(pre)
        dpre = (spread(dtc, pair) * r + vec_ref[0:1, here] * dy_ref[0, :, here]) * (sg * (1.0 + pre * (1.0 - sg)))
        dpre_ref[0, :, here] = dpre
        for k in range(4):
            dtaps_ref[k : k + 1, here] += jnp.sum(dpre * tapped[k], axis=0, keepdims=True)
        dtaps_ref[4:5, here] += jnp.sum(dpre, axis=0, keepdims=True)
    first_ref[0] = dpre_ref[0, :8]
    seed = jnp.exp(last) * through + local
    upper = (iota((seg, seg), 0) <= iota((seg, seg), 1)).astype(f32)
    q = dot(upper, pos_ref[0] - dtc * neg, precision=best) + seed
    rates = rate_ref[1:2]
    z = pc_ref[0, halo:, width : width + lanes].astype(f32) + rate_ref[0:1]
    draw = (neg - rates * q) * sigmoid(z)
    dstep_ref[0] = draw.astype(bf16)
    drate_ref[0:1] += jnp.sum(draw, axis=0, keepdims=True)
    drate_ref[1:2] += jnp.sum(q * (-dtc * rates), axis=0, keepdims=True)


def returned_kernel(dpre_ref, dshare_ref, next_ref, taps_ref, dstep_ref, out_ref, *, share, heads):
    seg, width = dpre_ref.shape[1:]
    for at in range(0, width + lanes, lanes):
        here = slice(at, at + lanes)
        own = dpre_ref[0, :, here] if at < width else dshare_ref[0]
        x = jnp.concatenate([own, next_ref[0, :, here]], axis=0)
        total = x[:seg] * taps_ref[3:4, here]
        for k in range(3):
            by = 3 - k
            total = total + pltpu.roll(x, seg + 8 - by, 0)[:seg] * taps_ref[k : k + 1, here]
        if at == width:
            step = pltpu.roll(dstep_ref[0].astype(f32), share, 1)
            lane = iota((seg, lanes), 1)
            total = jnp.where(lane < share, total, jnp.where(lane < share + heads, step, 0.0))
        out_ref[0, :, here] = total.astype(bf16)


def call(kernel, grid, ins, outs, name, ids=None, flops=0, scratch=(), far=False, **statics):
    def spec(shape, index):
        if index is None:
            return pl.BlockSpec(tuple(shape), lambda s, *i: (0,) * len(shape))
        block, at = index
        return pl.BlockSpec((block,) + tuple(shape[1:]), lambda s, *i: (at(s, *i),) + (0,) * (len(shape) - 1))

    moved = sum(a.size * a.dtype.itemsize for a, _ in ins)
    for shape, dtype, _ in outs:
        size = 1
        for d in shape:
            size *= d
        moved += size * jnp.dtype(dtype).itemsize
    return pl.pallas_call(
        functools.partial(kernel, **statics),
        grid_spec=pltpu.PrefetchScalarGridSpec(
            num_scalar_prefetch=0 if ids is None else 1,
            grid=(grid,),
            in_specs=[spec(a.shape, index) for a, index in ins],
            out_specs=[spec(shape, index) for shape, _, index in outs],
            scratch_shapes=list(scratch),
        ),
        out_shape=[(pltpu.HBM if far else jax.ShapeDtypeStruct)(shape, dtype) for shape, dtype, _ in outs],
        compiler_params=pltpu.CompilerParams(vmem_limit_bytes=24 << 20),
        cost_estimate=pl.CostEstimate(flops=flops, bytes_accessed=moved, transcendentals=0),
        name=name,
    )(*([] if ids is None else [ids]), *[pltpu.with_memory_space_constraint(a, pltpu.HBM) if far else a for a, _ in ins])


each = (1, lambda s, *i: s)


def swap(value, axis, by):
    count = lax.axis_size(axis)
    return lax.ppermute(value, axis, [(i, i ^ by) for i in range(count)])


def all_slots(value, axis, first=None):
    count = lax.axis_size(axis)
    by = count // 2
    offsets = [0]
    while by:
        value = jnp.concatenate([value, swap(value, axis, by)], axis=0)
        if first is not None:
            value, first = tied(value, first), None
        offsets += [j ^ by for j in offsets]
        by //= 2
    size = value.shape[0] // count
    where = [offsets.index(j) for j in range(count)]
    return jnp.concatenate([value[i * size : (i + 1) * size] for i in where], axis=0)


def blocks_turned(value, by, owners):
    size = value.shape[-1] // owners
    return jnp.concatenate([value[..., (j ^ by) * size : ((j ^ by) + 1) * size] for j in range(owners)], axis=-1)


def to_owner(value, axis, turn=False, first=None):
    count = lax.axis_size(axis)
    by = 1
    while by < count:
        value = value.reshape((value.shape[0] // 2, 2) + value.shape[1:])
        other = swap(value[:, 1].astype(bf16), axis, by).astype(f32)
        value = value[:, 0] + (blocks_turned(other, by, count) if turn else other)
        if first is not None:
            value, first = tied(value, first), None
        by *= 2
    return value[0]


def halved_start(value, axis, by):
    value = value.reshape((value.shape[0] // 2, 2) + value.shape[1:])
    bit = (lax.axis_index(axis) // by) % 2
    keep = lax.dynamic_index_in_dim(value, bit, 1, False)
    give = lax.dynamic_index_in_dim(value, 1 - bit, 1, False)
    return keep, swap(give, axis, by)


def halved_end(pair, *others):
    keep, came = tied(pair, others) if others else pair
    return (keep.astype(f32) + came.astype(f32)).astype(bf16)


def halved_from(value, axis, by):
    while value.shape[0] > 1:
        value = halved_end(halved_start(value, axis, by))
        by *= 2
    return value[0]


def tied(value, *others):
    return lax.optimization_barrier((value, others))[0]


def gather_step(value, axis, by, *others):
    came = swap(value, axis, by)
    return jnp.concatenate([value, tied(came, others) if others else came], axis=0)


def gathered(value, axis, by):
    while by:
        value = gather_step(value, axis, by)
        by //= 2
    return value


def reversed_bits(j, count):
    out, by = 0, 1
    while by < count:
        out = out * 2 + (j // by) % 2
        by *= 2
    return out


def traded(value, axis):
    count = lax.axis_size(axis)
    size = value.shape[-1] // count
    parts = [value[:, j * size : (j + 1) * size] for j in range(count)]
    return jnp.stack([swap(part, axis, j) if j else part for j, part in enumerate(parts)])


def exchange(value, axis):
    return lax.all_to_all(value, axis, 0, 0)


def in_order(parts, index):
    stacked = jnp.stack(parts)
    return jnp.concatenate([lax.dynamic_index_in_dim(stacked, index ^ a, 0) for a in range(len(parts))])


def assemble_kernel(ids_ref, gate_ref, *refs, share, heads):
    conv_refs, (weight_ref, out_ref, tail_ref, sum_ref) = refs[:-4], refs[-4:]
    step = pl.program_id(0)
    count, owners = gate_ref.shape[:2]
    channels = out_ref.shape[0]

    def place_of(q):
        return reversed_bits(ids_ref[0] ^ q, count)

    @pl.when(step == 0)
    def _():
        sum_ref[...] = jnp.zeros_like(sum_ref)

    def put(at, value):
        size = value.shape[0]
        out_ref[at : at + size] = value
        sum_ref[0:1] += jnp.sum(value * weight_ref[at : at + size].astype(f32), axis=0, keepdims=True)

    def parts():
        at = 0
        for ref in conv_refs:
            for q in range(count):
                yield at, ref, q
                at += ref.shape[2]

    @pl.when(step < owners)
    def _():
        rows = gate_ref.shape[2]
        for q in range(count):
            put(q * rows, gate_ref[place_of(q), ids_ref[1] ^ step].astype(f32))

    @pl.when(step // owners == 1)
    def _():
        for at, ref, q in parts():
            size = min(ref.shape[2], channels - at)
            if size > 0:
                put(at, ref[place_of(q), ids_ref[1] ^ (step % owners), :size].astype(f32))

    @pl.when(step == 2 * owners)
    def _():
        for a in range(owners):
            found = []
            for at, ref, q in parts():
                skip = max(0, channels - at)
                if skip < ref.shape[2]:
                    found.append(ref[place_of(q), ids_ref[1] ^ a].astype(f32)[skip:])
            value = jnp.concatenate(found, axis=0)
            tail_ref[a] = value
            put(a * share, value[:share])
            put(owners * share + a * heads, value[share : share + heads])


def rows_kernel(ids_ref, *refs, parts):
    bufs, (weight_ref, out_ref, sum_ref) = refs[: len(parts)], refs[len(parts) :]
    total = jnp.zeros((out_ref.shape[0], 1), f32)
    for ref, (start, size) in zip(bufs, parts, strict=True):
        value = ref[0].astype(f32)
        out_ref[:, start : start + size] = value
        total = total + jnp.sum(value * weight_ref[:, start : start + size].astype(f32), axis=1, keepdims=True)
    sum_ref[...] = total


def per_device(tokens, lengths, norm_gain, in_weight, conv_weight, conv_bias, dt_bias, decay_log, skip_gain, gated_gain, out_weight, cotangent):
    nf, nq = lax.axis_size("fsdp"), lax.axis_size("seq")
    me, place = lax.axis_index("fsdp"), lax.axis_index("seq")
    _, seg, width = tokens.shape
    rows = in_weight.shape[0]
    channels = out_weight.shape[0]
    inner = channels * nf
    heads = dt_bias.shape[0]
    conv_own = conv_weight.shape[1]
    state = (conv_own * nf - inner) // 2
    share = 2 * state // nf
    slots = nf

    ids = jnp.stack([place, me]).astype(jnp.int32)
    per_slot = nq // slots
    piece = channels // per_slot

    weight = in_weight.T
    half, side = channels // 2, place % 2
    got = []
    for j in range(nf):
        start = inner + (me ^ j) * channels
        if j < 2:
            give = lax.dynamic_slice_in_dim(weight, start, channels, 0)
            got.append(swap(give, "fsdp", j) if j else give)
        else:
            mine = swap(lax.dynamic_slice_in_dim(weight, start + side * half, half, 0), "fsdp", j)
            got += [mine, swap(mine, "seq", 1)]
    own_tokens = tied(tokens, got[2::2])
    x_main = all_slots(own_tokens, "fsdp", got[3::2])
    before = lax.ppermute(tokens[0, seg - 3 :], "seq", [(i, i + 1) for i in range(nq - 1)])

    def padded(rows_):
        return jnp.pad(rows_, ((0, 0), (0, width - rows_.shape[1])))

    small = jnp.concatenate(
        [padded(conv_weight), padded(conv_bias[None]), padded(norm_gain[None]), jnp.zeros((7, width), bf16), before], axis=0
    )
    x_small = all_slots(small[None], "fsdp")
    listed = [x_small[j] for j in range(nf)]
    norm_all = in_order([part[5, :rows] for part in listed], me).astype(f32).reshape(1, width)
    taps_all = in_order([part[:5, :conv_own] for part in listed], me).astype(f32)
    taps_all = taps_all.reshape(nf, 5, conv_own).transpose(1, 0, 2).reshape(5, -1)
    taps_all = jnp.pad(taps_all, ((0, 3), (0, 0)))
    taps = jnp.concatenate([lax.dynamic_slice_in_dim(taps_all, me * channels, channels, 1), taps_all[:, inner:]], axis=1)
    taps_share = lax.dynamic_slice_in_dim(taps_all, inner + me * share, share, 1)
    rate = jnp.stack([dt_bias.astype(f32), jnp.exp(decay_log.astype(f32))])
    rate = jnp.pad(rate, ((0, 6), (0, lanes - heads)))
    vec = jnp.stack([jnp.repeat(skip_gain.astype(f32), head_size), gated_gain.astype(f32)])
    vec = jnp.pad(vec, ((0, 6), (0, 0)))

    rest = all_slots(weight[2 * inner :][None], "fsdp")
    cw = channels + 2 * state
    (w_conv,) = call(
        weight_kernel,
        1,
        [(part, None) for part in got] + [(rest, None)],
        [((cw + lanes, width), bf16, None)],
        "weights",
        ids=ids,
        owners=nf,
        state=state,
        heads=heads,
    )

    (normed,) = call(
        normalize_kernel,
        slots,
        [(x_main, each), (x_small, each), (norm_all, None)],
        [((slots, halo + seg, width), bf16, each)],
        "normalize",
        ids=ids,
        owners=nf,
    )
    inputs = tokens[0].astype(f32)
    valid = (place * seg + jnp.arange(seg) < lengths[0]).astype(f32)[:, None]
    upstream = valid * cotangent[0].astype(f32)

    gives = [lax.dynamic_slice_in_dim(weight, (me ^ j) * channels, channels, 0) for j in range(nf)]
    gives, later = tied((gives, upstream.astype(bf16)), got[-1])
    w_gate = jnp.concatenate([swap(g, "fsdp", j) if j else g for j, g in enumerate(gives)], axis=1)
    back_branch = all_slots(later[None], "fsdp")

    def project(x, w):
        return lax.dot_general(x, w, (((2,), (1,)), ((), ())), preferred_element_type=f32)

    pc = project(normed, w_conv).astype(bf16)
    main = normed[:, halo:]
    tall = 16
    statics = dict(channels=channels, state=state)
    turned = (per_slot, lambda s, *i: s)
    act, y_local, s_local, lac, dtc, lar, dtr = call(
        forward_kernel,
        slots,
        [(pc, each), (taps, None), (rate, None)],
        [
            ((slots, seg, cw), bf16, each),
            ((slots, seg, channels), f32, each),
            ((nq, piece + 16, state), bf16, turned),
            ((slots, seg, lanes), f32, each),
            ((slots, seg, lanes), f32, each),
            ((slots, tall, seg), f32, each),
            ((slots, tall, seg), f32, each),
        ],
        "forward",
        far=True,
        flops=2 * slots * seg * seg * channels,
        rows=piece,
        **statics,
    )

    came = exchange(s_local, "seq")
    (reached,) = call(
        chain_kernel, 1, [(came, None)], [((nq, piece, state), bf16, None)], "chain", ids=ids, rows=piece, count=per_slot
    )
    s_in = exchange(reached, "seq").reshape(slots, channels, state)

    gate = project(main, w_gate).astype(bf16)
    bg = lax.dot_general(back_branch, out_weight, (((2,), (1,)), ((), ())), preferred_element_type=f32)
    y, stats = call(
        finish_kernel,
        slots,
        [(y_local, each), (act, each), (lac, each), (s_in, each), (gate, each), (bg, each), (vec, None)],
        [((slots, seg, channels), f32, each), ((slots, 8, seg), f32, each)],
        "finish",
        far=True,
        **statics,
    )
    shares = [(swap(stats, "fsdp", j) if j else stats, (1, lambda s, j=j: s ^ j)) for j in range(nf)]
    gated_out, dgate, dy, pos, dsin, dskip = call(
        norm_kernel,
        slots,
        [(y, each), (act, each), (lac, each), (gate, each), (bg, each), (vec, None)] + shares,
        [
            ((slots, seg, channels), bf16, each),
            ((slots, seg, channels), bf16, each),
            ((slots, seg, channels), f32, each),
            ((slots, seg, lanes), f32, each),
            ((nq, piece, state), bf16, turned),
            ((8, channels), f32, None),
        ],
        "norm",
        far=True,
        inner=inner,
        rows=piece,
        **statics,
    )

    def grad_of(dz, x):
        return lax.dot_general(dz, x, (((0, 1), (0, 1)), ((), ())), preferred_element_type=f32).astype(bf16)

    def cut(value):
        size = value.shape[-1] // 2
        return [value] if size // nq % 8 else [value[..., :size], value[..., size:]]

    def pieces(g):
        return g.reshape((nq, g.shape[0] // nq) + g.shape[1:])

    barrier = lax.optimization_barrier
    gate_grad, out_grad = grad_of(dgate, main), grad_of(gated_out, back_branch)
    back_came = exchange(tied(dsin, gate_grad), "seq")
    gate_step = halved_start(pieces(gate_grad), "seq", 1)
    out_step = halved_start(pieces(out_grad), "seq", 1)
    branch = lax.dot_general(gated_out, out_weight, (((2,), (0,)), ((), ())), preferred_element_type=f32)
    branch = to_owner(branch, "fsdp")
    (reached,) = call(
        back_chain_kernel,
        1,
        [(back_came, None), (came, None)],
        [((nq, piece, state), bf16, None)],
        "back_chain",
        ids=ids,
        rows=piece,
        count=per_slot,
    )
    g_end = exchange(reached, "seq").reshape(slots, channels, state)
    gate_sum = halved_end(gate_step, reached)
    dy_later, gate_sum = barrier((dy, gate_sum))
    gate_step = halved_start(gate_sum, "seq", 2)

    r_local, dbc = call(
        backward_kernel,
        slots,
        [(act, each), (dy_later, each), (lac, each), (lar, each), (dtr, each), (s_in, each)],
        [((slots, seg, channels), f32, each), ((slots, seg, 2 * state), f32, each)],
        "backward",
        far=True,
        flops=4 * slots * seg * seg * channels,
        **statics,
    )
    gate_sum = halved_end(gate_step, dbc)
    dbc, gate_sum = barrier((dbc, gate_sum))
    gate_step = halved_start(gate_sum, "seq", 4)
    d_shares = call(
        rows_grad_kernel,
        slots,
        [(act, each), (lac, each), (dtc, each), (g_end, each), (dbc, each)],
        [((slots, share, seg), bf16, each)] * nf,
        "rows_grad",
        ids=ids,
        scratch=[pltpu.VMEM((2 * state, seg), f32)],
        **statics,
    )
    out_sum = halved_end(out_step, d_shares[0])
    r_local, out_sum, own_share = barrier((r_local, out_sum, d_shares[0]))
    out_step = halved_start(out_sum, "seq", 2)
    d_shares = [own_share] + [swap(d, "fsdp", j) for j, d in enumerate(d_shares) if j]
    dpre, first, dstep, dtaps, drate = call(
        carry_kernel,
        slots,
        [
            (pc, each), (taps, None), (rate, None), (act, each), (dy, each), (r_local, each), (pos, each), (lac, each),
            (dtc, each), (g_end, each), (s_in, each), (s_local, turned), (vec, None),
        ],
        [
            ((slots, seg, channels), f32, each),
            ((slots, 8, channels), f32, each),
            ((slots, seg, lanes), bf16, each),
            ((8, channels), f32, None),
            ((8, lanes), f32, None),
        ],
        "carry",
        far=True,
        rows=piece,
        **statics,
    )
    dpre, gate_step, out_step, d_shares, branch = barrier((dpre, gate_step, out_step, d_shares, branch))
    gate_sum, out_sum = halved_from(halved_end(gate_step), "seq", 8), halved_end(out_step)
    pc_later, gate_sum, out_sum, d_shares = barrier((pc, gate_sum, out_sum, d_shares))
    out_step = halved_start(out_sum, "seq", 4)
    gate_sum = traded(gate_sum, "fsdp")[None]
    dpre_share, first_share, dtaps_share = call(
        share_kernel,
        slots,
        [(pc_later, each), (taps_share.T, None)]
        + [(d, (1, lambda s, i, j=j: s ^ j)) for j, d in enumerate(d_shares)],
        [((slots, seg, lanes), f32, each), ((slots, 8, lanes), f32, each), ((share, lanes), f32, None)],
        "share",
        ids=ids,
        scratch=[pltpu.VMEM((2 * state, seg), f32)],
        **statics,
    )
    first, first_share, gate_sum = barrier((first, first_share, gate_sum))
    behind = [(i, i - 1) for i in range(1, nq)]
    after = lax.ppermute(jnp.concatenate([first, first_share], axis=2), "seq", behind)
    gate_more = swap(gate_sum, "seq", nq // 2)
    after, gate_more = barrier((after, gate_more))
    gate_sum = jnp.concatenate([gate_sum, gate_more], axis=0)
    taps_back = jnp.concatenate([taps[:, :channels], jnp.pad(taps_share, ((0, 0), (0, lanes - share)))], axis=1)
    (dconv,) = call(
        returned_kernel,
        slots,
        [(dpre, each), (dpre_share, each), (after, each), (taps_back, None), (dstep, each)],
        [((slots, seg, channels + lanes), bf16, each)],
        "returned",
        share=share,
        heads=heads,
    )

    per = channels // rows
    head_rows = jnp.stack([drate[0, :heads], drate[1, :heads], jnp.sum(dskip[0].reshape(heads, head_size), axis=1)])
    block = jnp.concatenate(
        [
            dtaps[:5].reshape(5 * per, rows),
            jnp.pad(dtaps_share[:, :5].T, ((0, 0), (0, rows - share))),
            jnp.pad(head_rows, ((0, 0), (0, rows - heads))),
        ],
        axis=0,
    )
    extra = block.shape[0]
    block = jnp.tile(block, (1, nf)).astype(bf16)
    conv_grads = [grad_of(part, main) for part in cut(dconv)]
    spare = channels + share + heads - sum(g.shape[0] for g in conv_grads[:-1])
    conv_grads[-1] = lax.dynamic_update_slice_in_dim(conv_grads[-1], block, spare, 0)

    out_unit = channels // nq
    conv_steps = [halved_start(pieces(g), "seq", 1) for g in conv_grads]
    out_sum = halved_from(halved_end(out_step, conv_grads), "seq", 8)[None]
    gate_sum = gather_step(gate_sum, "seq", nq // 4, out_sum)
    conv_sums = [halved_end(step, gate_sum) for step in conv_steps]
    late_conv = tied(dconv, conv_sums[0])
    out_sum = gather_step(out_sum, "seq", nq // 2, conv_sums)
    gate_bufs = [gathered(gate_sum, "seq", nq // 8)]
    conv_steps = [halved_start(g, "seq", 2) for g in conv_sums]
    conv_sums = [halved_end(step, out_sum) for step in conv_steps]
    out_sum = gather_step(out_sum, "seq", nq // 4, conv_sums[-1])
    conv_steps = [halved_start(g, "seq", 4) for g in conv_sums]
    conv_sums = [halved_from(halved_end(step, out_sum), "seq", 8) for step in conv_steps]
    out_parts = [gathered(out_sum, "seq", nq // 8)]
    conv_sums, gate_bufs = barrier((conv_sums, gate_bufs))
    conv_sums = [traded(g, "fsdp") for g in conv_sums]
    conv_bufs = [gather_step(g[None], "seq", nq // 2) for g in conv_sums]
    tied_bufs = conv_bufs
    conv_bufs = [gather_step(g, "seq", nq // 4) for g in conv_bufs]
    conv_bufs, out_parts = barrier((conv_bufs, out_parts))
    conv_bufs = [gathered(g, "seq", nq // 8) for g in conv_bufs]
    place_of = jnp.stack([reversed_bits(place ^ q, nq) for q in range(nq)])
    if all(buf.shape[2] % 8 == 0 for buf in gate_bufs + conv_bufs):
        g_in, tail, norm_sum = call(
            assemble_kernel,
            2 * nf + 1,
            [(buf, None) for buf in gate_bufs + conv_bufs] + [(weight, (channels, lambda s, i: s))],
            [
                (weight.shape, f32, (channels, lambda s, i: s)),
                ((nf, lanes, rows), f32, None),
                ((8, rows), f32, None),
            ],
            "assemble",
            ids=ids,
            share=share,
            heads=heads,
        )
        norm_sum = norm_sum[0]
    else:
        order = me ^ jnp.arange(nf)

        def natural(bufs):
            bufs = [buf[place_of][:, order].astype(f32).transpose(1, 0, 2, 3).reshape(nf, -1, rows) for buf in bufs]
            return jnp.concatenate(bufs, axis=1)

        gate_all, conv_all = natural(gate_bufs), natural(conv_bufs)
        tail = conv_all[:, channels:]
        joined = [gate_all.reshape(inner, rows), conv_all[:, :channels].reshape(inner, rows)]
        joined += [tail[:, :share].reshape(nf * share, rows), tail[:, share : share + heads].reshape(nf * heads, rows)]
        g_in = jnp.concatenate(joined, axis=0)
        norm_sum = jnp.sum(g_in * weight.astype(f32), axis=0)
    if out_unit % 16 == 0:
        sizes = [part.shape[-1] for part in out_parts]
        g_out, gated_sum = call(
            rows_kernel,
            nq,
            [(part, (1, lambda s, i: reversed_bits(i[0] ^ s, nq))) for part in out_parts] + [(out_weight, (out_unit, lambda s, i: s))],
            [(out_weight.shape, f32, (out_unit, lambda s, i: s)), ((channels, 1), f32, (out_unit, lambda s, i: s))],
            "rows",
            ids=ids,
            parts=[(sum(sizes[:i]), size) for i, size in enumerate(sizes)],
        )
        gated_sum = gated_sum[:, 0]
    else:
        g_out = jnp.concatenate([part[place_of].astype(f32).reshape(channels, -1) for part in out_parts], axis=1)
        gated_sum = jnp.sum(g_out * out_weight.astype(f32), axis=1)

    norm_grad = norm_sum / norm_gain.astype(f32)
    gated_grad = gated_sum / gated_gain.astype(f32)

    got = tail[:, share + heads : share + heads + extra]
    tap_grads = jnp.concatenate(
        [
            got[:, : 5 * per].reshape(nf, 5, channels).transpose(1, 0, 2).reshape(5, inner),
            got[:, 5 * per : 5 * per + 5, :share].transpose(1, 0, 2).reshape(5, 2 * state),
        ],
        axis=1,
    )
    tap_grads = lax.dynamic_slice_in_dim(tap_grads, me * conv_own, conv_own, 1)
    head_grads = lax.dynamic_index_in_dim(got, me, 0, False)[5 * per + 5 :, :heads]

    mixed = (valid * (inputs + branch)).astype(bf16)

    w_share = lax.dynamic_slice_in_dim(w_conv, channels + me * share, share, 0)
    w_last = jnp.concatenate([w_share, w_conv[cw : cw + lanes - share]], axis=0)

    def back(dz, w):
        return lax.dot_general(dz, w, (((2,), (0,)), ((), ())), preferred_element_type=f32)

    bn = back(dgate, w_gate) + back(late_conv[..., :channels], w_conv[:channels]) + back(late_conv[..., channels:], w_last)
    bn = to_owner(bn, "fsdp", turn=True, first=tied_bufs)
    (input_grad,) = call(
        input_kernel,
        1,
        [(bn, None), (norm_all, None), (tokens[0], None), (cotangent[0], None), (valid, None)],
        [((seg, width), f32, None)],
        "input",
        ids=ids,
        owners=nf,
    )
    return (
        mixed[None],
        input_grad[None],
        norm_grad,
        g_in.T,
        tap_grads[:4],
        tap_grads[4],
        head_grads[0],
        head_grads[1],
        head_grads[2],
        gated_grad,
        g_out,
    )


def solution(mesh):
    whole, rows = P("fsdp", "seq", None), P("fsdp", None)
    one, columns = P("fsdp"), P(None, "fsdp")
    return jax.shard_map(
        per_device,
        mesh=mesh,
        in_specs=(whole, one, one, rows, columns, one, one, one, one, one, rows, whole),
        out_specs=(whole, whole, one, rows, columns, one, one, one, one, one, rows),
        check_vma=False,
    )
```

```python
import functools

import jax
import jax.numpy as jnp
from jax import lax
from jax.experimental import pallas as pl
from jax.experimental.pallas import tpu as pltpu
from jax.sharding import PartitionSpec as P

epsilon = 1e-05
bf16, f32 = jnp.bfloat16, jnp.float32
best = lax.Precision.HIGHEST
halo = 16
lanes = 128
head_size = 64


def dot(a, b, ca=1, cb=0, precision=None):
    return lax.dot_general(
        a, b, (((ca,), (cb,)), ((), ())), preferred_element_type=f32, precision=precision
    )


def sigmoid(v):
    return 0.5 + 0.5 * jnp.tanh(0.5 * v)


def iota(shape, axis):
    return lax.broadcasted_iota(jnp.int32, shape, axis)


def spread(columns, pair):
    first, second = 2 * pair, 2 * pair + 1
    rows = columns.shape[0]
    return jnp.where(
        iota((rows, lanes), 1) < head_size,
        columns[:, first : first + 1],
        columns[:, second : second + 1],
    )


def per_head(total, products, pair):
    rows = products.shape[0]
    lane = iota((rows, lanes), 1)
    low = jnp.sum(jnp.where(lane < head_size, products, 0.0), axis=1, keepdims=True)
    high = jnp.sum(jnp.where(lane < head_size, 0.0, products), axis=1, keepdims=True)
    return total + jnp.where(lane == 2 * pair, low, jnp.where(lane == 2 * pair + 1, high, 0.0))


def in_heads(products, pair):
    rows = jnp.sum(products, axis=1, keepdims=True)
    low, high = jnp.sum(rows[:head_size]), jnp.sum(rows[head_size:])
    lane = iota((1, lanes), 1)
    return jnp.where(lane == 2 * pair, low, jnp.where(lane == 2 * pair + 1, high, 0.0))


def convolved(pc_ref, taps_ref, at):
    x = pc_ref[0, :, at : at + lanes].astype(f32)
    tapped = [pltpu.roll(x, 3 - k, 0)[halo:] for k in range(3)] + [x[halo:]]
    pre = taps_ref[4:5, at : at + lanes]
    for k in range(4):
        pre = pre + tapped[k] * taps_ref[k : k + 1, at : at + lanes]
    return tapped, pre


def pieces_out(out_ref, whole, rows):
    for p in range(out_ref.shape[0]):
        out_ref[p, :rows] = whole[p * rows : (p + 1) * rows]


def pieces_in(ref, rows):
    return jnp.concatenate([ref[p, :rows] for p in range(ref.shape[0])], axis=0)


def block_of(index, size):
    return pl.ds(pl.multiple_of(index * size, size), size)


def columns_of(ref, index, size):
    if size % lanes == 0:
        return ref[:, block_of(index, size)]
    value = ref[:, :size]
    for a in range(1, ref.shape[1] // size):
        value = jnp.where(index == a, ref[:, a * size : (a + 1) * size], value)
    return value


def normalize_kernel(ids_ref, main_ref, small_ref, gain_ref, out_ref, *, owners):
    size = out_ref.shape[2] // owners
    for ref, at in ((small_ref, 0), (main_ref, halo)):
        x = ref[0].astype(f32)
        inv = lax.rsqrt(jnp.mean(x * x, axis=1, keepdims=True) + epsilon)
        for j in range(owners):
            own = ids_ref[1] ^ j
            part = columns_of(ref.at[0], own, size).astype(f32) * inv * columns_of(gain_ref, own, size)
            out_ref[0, at : at + x.shape[0], j * size : (j + 1) * size] = part.astype(bf16)


def weight_kernel(ids_ref, *refs, owners, state, heads):
    rest_ref, out_ref = refs[-2:]
    size = rest_ref.shape[2]
    channels = out_ref.shape[0] - 2 * state - lanes
    n = 0
    for j in range(owners):
        own = slice(j * size, (j + 1) * size)
        if j < 2:
            out_ref[:channels, own] = refs[n][...]
            n += 1
        else:
            quarter = channels // 4
            for far_side in range(2):
                for near in range(2):
                    place = ((ids_ref[0] % 2) ^ far_side) * 2 + (((ids_ref[0] // 2) % 2) ^ near)
                    ref = refs[n] if far_side == 0 else refs[n].at[near]
                    out_ref[block_of(place, quarter), own] = ref[...]
                    n += 1 - far_side
            n += 1
        out_ref[channels : channels + 2 * state, own] = rest_ref[j, : 2 * state]
        rows = owners * heads
        pick = iota((lanes, rows), 1) == ids_ref[1] * heads + iota((lanes, rows), 0)
        pick = jnp.where(iota((lanes, rows), 0) < heads, pick.astype(f32), 0.0).astype(bf16)
        out_ref[channels + 2 * state :, own] = dot(pick, rest_ref[j, 2 * state : 2 * state + rows]).astype(bf16)


def input_kernel(ids_ref, bn_ref, gain_ref, tokens_ref, cot_ref, valid_ref, out_ref, *, owners):
    x = tokens_ref[...].astype(f32)
    width = x.shape[1]
    size = width // owners
    inv = lax.rsqrt(jnp.mean(x * x, axis=1, keepdims=True) + epsilon)
    lean = jnp.zeros_like(inv)
    for a in range(owners):
        here = slice(a * size, (a + 1) * size)
        bn = columns_of(bn_ref, ids_ref[1] ^ a, size) * gain_ref[:, here]
        lean = lean + jnp.sum(bn * x[:, here], axis=1, keepdims=True)
    lean = lean * (inv * inv * inv) * (1.0 / width)
    for a in range(owners):
        here = slice(a * size, (a + 1) * size)
        bn = columns_of(bn_ref, ids_ref[1] ^ a, size) * gain_ref[:, here]
        out_ref[:, here] = valid_ref[...] * cot_ref[:, here].astype(f32) + inv * bn - x[:, here] * lean


def of_rows(row, ids_ref, rows, count):
    head = ((ids_ref[0] % count) * rows + iota((rows, lanes), 0)) // head_size
    return jnp.sum(jnp.where(iota((rows, lanes), 1) == head, row, 0.0), axis=1, keepdims=True)


def chain_kernel(ids_ref, in_ref, out_ref, *, rows, count):
    carried = jnp.zeros((rows, lanes), f32)
    for i in range(in_ref.shape[0]):
        out_ref[i] = carried.astype(bf16)
        row = in_ref[i, rows : rows + 1].astype(f32) + in_ref[i, rows + 1 : rows + 2].astype(f32)
        carried = of_rows(row, ids_ref, rows, count) * carried + in_ref[i, :rows].astype(f32)


def back_chain_kernel(ids_ref, in_ref, decay_ref, out_ref, *, rows, count):
    carried = jnp.zeros((rows, lanes), f32)
    for i in reversed(range(in_ref.shape[0])):
        out_ref[i] = carried.astype(bf16)
        row = decay_ref[i, rows : rows + 1].astype(f32) + decay_ref[i, rows + 1 : rows + 2].astype(f32)
        carried = of_rows(row, ids_ref, rows, count) * carried + in_ref[i].astype(f32)


def states_kernel(pc_ref, taps_ref, rate_ref, act_ref, s_ref, lac_ref, dtc_ref, lar_ref, dtr_ref, *, channels, state, rows):
    width = channels + 2 * state
    for at in list(range(channels, width, lanes)) + list(range(0, channels, lanes)):
        _, pre = convolved(pc_ref, taps_ref, at)
        act_ref[0, :, at : at + lanes] = (pre * sigmoid(pre)).astype(bf16)
    seg = act_ref.shape[1]
    z = pc_ref[0, halo:, width : width + lanes].astype(f32) + rate_ref[0:1]
    dtc = jnp.maximum(z, 0.0) + jnp.log1p(jnp.exp(-jnp.abs(z)))
    lower = iota((seg, seg), 0) >= iota((seg, seg), 1)
    lac = dot(lower.astype(f32), -dtc * rate_ref[1:2], precision=best)
    tall = lar_ref.shape[1]
    lac_ref[0], dtc_ref[0], lar_ref[0], dtr_ref[0] = lac, dtc, lac.T[:tall], dtc.T[:tall]
    b_rows = act_ref[0, :, channels : channels + state]
    to_end = jnp.exp(lac[seg - 1 : seg] - lac) * dtc
    states = []
    for pair in range(channels // lanes):
        at = pair * lanes
        weighted = (spread(to_end, pair) * act_ref[0, :, at : at + lanes].astype(f32)).astype(bf16)
        states.append(dot(weighted, b_rows, 0, 0).astype(bf16))
    pieces_out(s_ref, jnp.concatenate(states, axis=0), rows)
    whole = jnp.exp(lac[seg - 1 : seg])
    high = whole.astype(bf16).astype(f32)
    row = iota((16, lanes), 0)
    tail = jnp.where(row == 0, high, jnp.where(row == 1, whole - high, 0.0)).astype(bf16)
    for p in range(s_ref.shape[0]):
        s_ref[p, rows:] = tail


def local_kernel(act_ref, lac_ref, lar_ref, dtr_ref, y_ref, *, channels, state):
    seg = act_ref.shape[1]
    lower = iota((seg, seg), 0) >= iota((seg, seg), 1)
    lac, lar, dtr = lac_ref[0], lar_ref[0], dtr_ref[0]
    both = dot(act_ref[0, :, channels + state :], act_ref[0, :, channels : channels + state], 1, 1)
    for pair in range(channels // lanes):
        at = pair * lanes
        values = act_ref[0, :, at : at + lanes]
        parts = []
        for side in range(2):
            h = 2 * pair + side
            mix = jnp.where(lower, jnp.exp(lac[:, h : h + 1] - lar[h : h + 1]), 0.0) * both * dtr[h : h + 1]
            parts.append(dot(mix.astype(bf16), values[:, side * head_size : (side + 1) * head_size]))
        y_ref[0, :, at : at + lanes] = jnp.concatenate(parts, axis=1)


def finish_kernel(y_ref, act_ref, lac_ref, sin_ref, gate_ref, bg_ref, vec_ref, y_out, stat_ref, *, channels, state):
    seg = y_ref.shape[1]
    c_rows = act_ref[0, :, channels + state : channels + 2 * state]
    decay = jnp.exp(lac_ref[0])
    first = jnp.zeros((seg, 1), f32)
    second = jnp.zeros((seg, 1), f32)
    for pair in range(channels // lanes):
        at = pair * lanes
        here = slice(at, at + lanes)
        carried = dot(c_rows, sin_ref[0, here], 1, 1)
        y = y_ref[0, :, here] + spread(decay, pair) * carried
        y_out[0, :, here] = y
        gate = gate_ref[0, :, here].astype(f32)
        heads = y + vec_ref[0:1, here] * act_ref[0, :, here].astype(f32)
        gated = heads * gate * sigmoid(gate)
        first = first + jnp.sum(gated * gated, axis=1, keepdims=True)
        second = second + jnp.sum(gated * bg_ref[0, :, here].astype(f32) * vec_ref[1:2, here], axis=1, keepdims=True)
    lane = iota((seg, lanes), 1)
    both = jnp.where(lane == 0, first, jnp.where(lane == 1, second, 0.0))
    stat_ref[0] = both.T[:8]


def norm_kernel(y_ref, act_ref, lac_ref, gate_ref, bg_ref, vec_ref, *refs, channels, state, inner, rows):
    stat_refs, (out_ref, dgate_ref, dy_ref, pos_ref, dsin_ref, dskip_ref) = refs[:-6], refs[-6:]
    seg = y_ref.shape[1]
    stats = sum(ref[0] for ref in stat_refs).T
    states = []
    inv = lax.rsqrt(stats[:, 0:1] * (1.0 / inner) + epsilon)
    lean = inv * inv * inv * (stats[:, 1:2] * (1.0 / inner))
    c_rows = act_ref[0, :, channels + state : channels + 2 * state]
    decay = jnp.exp(lac_ref[0])
    pos = jnp.zeros((seg, lanes), f32)

    @pl.when(pl.program_id(0) == 0)
    def _():
        dskip_ref[...] = jnp.zeros_like(dskip_ref)

    for pair in range(channels // lanes):
        at = pair * lanes
        here = slice(at, at + lanes)
        y = y_ref[0, :, here]
        values = act_ref[0, :, here].astype(f32)
        heads = y + vec_ref[0:1, here] * values
        gate = gate_ref[0, :, here].astype(f32)
        sg = sigmoid(gate)
        gated = heads * gate * sg
        gain = vec_ref[1:2, here]
        out_ref[0, :, here] = (gated * inv * gain).astype(bf16)
        dgated = inv * (bg_ref[0, :, here].astype(f32) * gain) - gated * lean
        dgate_ref[0, :, here] = (dgated * heads * (sg * (1.0 + gate * (1.0 - sg)))).astype(bf16)
        dy = dgated * gate * sg
        dy_ref[0, :, here] = dy
        pos = per_head(pos, dy * y, pair)
        states.append(dot((spread(decay, pair) * dy).astype(bf16), c_rows, 0, 0).astype(bf16))
        dskip_ref[0:1, here] += jnp.sum(dy * values, axis=0, keepdims=True)
    pos_ref[0] = pos
    pieces_out(dsin_ref, jnp.concatenate(states, axis=0), rows)


def backward_kernel(act_ref, dy_ref, lac_ref, lar_ref, dtr_ref, sin_ref, r_ref, dbc_ref, *, channels, state):
    seg = dy_ref.shape[1]
    b_rows = act_ref[0, :, channels : channels + state]
    c_rows = act_ref[0, :, channels + state : channels + 2 * state]
    both = dot(c_rows, b_rows, 1, 1)
    lower = iota((seg, seg), 0) >= iota((seg, seg), 1)
    lac, lar, dtr = lac_ref[0], lar_ref[0], dtr_ref[0]
    decay = jnp.exp(lac)
    dboth = jnp.zeros((seg, seg), f32)
    dc = jnp.zeros((seg, state), f32)
    for pair in range(channels // lanes):
        at = pair * lanes
        here = slice(at, at + lanes)
        values = act_ref[0, :, here]
        dy = dy_ref[0, :, here]
        dyl = dy.astype(bf16)
        parts = []
        for side in range(2):
            h = 2 * pair + side
            own = slice(side * head_size, (side + 1) * head_size)
            weights = jnp.where(lower, jnp.exp(lac[:, h : h + 1] - lar[h : h + 1]), 0.0)
            parts.append(dot((weights * both).astype(bf16), dyl[:, own], 0, 0))
            dboth = dboth + dot(dyl[:, own], values[:, own], 1, 1) * (weights * dtr[h : h + 1])
        r_ref[0, :, here] = jnp.concatenate(parts, axis=1)
        dc = dc + dot((spread(decay, pair) * dy).astype(bf16), sin_ref[0, here])
    dlow = dboth.astype(bf16)
    dbc_ref[0, :, :state] = dot(dlow, c_rows, 0, 0)
    dbc_ref[0, :, state:] = dc + dot(dlow, b_rows)


def rows_grad_kernel(ids_ref, act_ref, lac_ref, dtc_ref, g_ref, dbc_ref, *refs, channels, state):
    out_refs, hold = refs[:-1], refs[-1]
    seg = act_ref.shape[1]
    lac, dtc = lac_ref[0], dtc_ref[0]
    weights = jnp.exp(lac[seg - 1 : seg] - lac) * dtc
    db = dbc_ref[0, :, :state]
    for pair in range(channels // lanes):
        here = slice(pair * lanes, (pair + 1) * lanes)
        db = db + dot((spread(weights, pair) * act_ref[0, :, here].astype(f32)).astype(bf16), g_ref[0, here])
    hold[:state] = db.T
    hold[state:] = dbc_ref[0, :, state:].T
    share = out_refs[0].shape[1]
    for j, out_ref in enumerate(out_refs):
        out_ref[0] = hold[block_of(ids_ref[1] ^ j, share)].astype(bf16)


def share_kernel(ids_ref, pc_ref, taps_ref, *refs, channels, state):
    parts, (dpre_ref, first_ref, dtaps_ref, hold) = refs[:-4], refs[-4:]
    seg = pc_ref.shape[1] - halo
    share = parts[0].shape[1]
    own = block_of(ids_ref[1], share)
    hold[...] = pc_ref[0, :, channels : channels + 2 * state].astype(f32)[halo:].T
    x = hold[own]
    hold[:, :halo] = pc_ref[0, :halo, channels : channels + 2 * state].astype(f32).T
    edge = hold[own, :halo]
    lane = iota((share, seg), 1)
    tapped = []
    for k in range(3):
        value = pltpu.roll(x, 3 - k, 1)
        for t in range(3 - k):
            value = jnp.where(lane == t, edge[:, halo - 3 + k + t : halo - 2 + k + t], value)
        tapped.append(value)
    tapped.append(x)
    pre = taps_ref[:, 4:5] + sum(tapped[k] * taps_ref[:, k : k + 1] for k in range(4))
    sg = sigmoid(pre)
    dpre = sum(ref[0].astype(f32) for ref in parts) * (sg * (1.0 + pre * (1.0 - sg)))

    @pl.when(pl.program_id(0) == 0)
    def _():
        dtaps_ref[...] = jnp.zeros_like(dtaps_ref)

    lane = iota((share, lanes), 1)
    total = jnp.zeros((share, lanes), f32)
    for k in range(5):
        column = jnp.sum(dpre * tapped[k] if k < 4 else dpre, axis=1, keepdims=True)
        total = jnp.where(lane == k, column, total)
    dtaps_ref[...] += total
    rows = jnp.concatenate([dpre, jnp.zeros((lanes - share, seg), f32)], axis=0).T
    dpre_ref[0] = rows
    first_ref[0] = rows[:8]


def carry_kernel(pc_ref, taps_ref, rate_ref, act_ref, dy_ref, r_ref, pos_ref, lac_ref, dtc_ref, g_ref, sin_ref, s_ref, vec_ref, dpre_ref, first_ref, dstep_ref, dtaps_ref, drate_ref, *, channels, state, rows):
    seg = dy_ref.shape[1]
    width = channels + 2 * state
    b_rows = act_ref[0, :, channels : channels + state]
    lac, dtc = lac_ref[0], dtc_ref[0]
    last = lac[seg - 1 : seg]
    to_last = jnp.exp(last - lac)
    neg = jnp.zeros((seg, lanes), f32)
    through = jnp.zeros((1, lanes), f32)
    local = jnp.zeros((1, lanes), f32)
    states = pieces_in(s_ref, rows)

    @pl.when(pl.program_id(0) == 0)
    def _():
        dtaps_ref[...] = jnp.zeros_like(dtaps_ref)
        drate_ref[...] = jnp.zeros_like(drate_ref)

    for pair in range(channels // lanes):
        at = pair * lanes
        here = slice(at, at + lanes)
        grad = g_ref[0, here]
        values = act_ref[0, :, here].astype(f32)
        r = r_ref[0, :, here] + spread(to_last, pair) * dot(b_rows, grad, 1, 1)
        neg = per_head(neg, values * r, pair)
        wide = grad.astype(f32)
        through = through + in_heads(wide * sin_ref[0, here].astype(f32), pair)
        local = local + in_heads(wide * states[here].astype(f32), pair)
        tapped, pre = convolved(pc_ref, taps_ref, at)
        sg = sigmoid(pre)
        dpre = (spread(dtc, pair) * r + vec_ref[0:1, here] * dy_ref[0, :, here]) * (sg * (1.0 + pre * (1.0 - sg)))
        dpre_ref[0, :, here] = dpre
        for k in range(4):
            dtaps_ref[k : k + 1, here] += jnp.sum(dpre * tapped[k], axis=0, keepdims=True)
        dtaps_ref[4:5, here] += jnp.sum(dpre, axis=0, keepdims=True)
    first_ref[0] = dpre_ref[0, :8]
    seed = jnp.exp(last) * through + local
    upper = (iota((seg, seg), 0) <= iota((seg, seg), 1)).astype(f32)
    q = dot(upper, pos_ref[0] - dtc * neg, precision=best) + seed
    rates = rate_ref[1:2]
    z = pc_ref[0, halo:, width : width + lanes].astype(f32) + rate_ref[0:1]
    draw = (neg - rates * q) * sigmoid(z)
    dstep_ref[0] = draw.astype(bf16)
    drate_ref[0:1] += jnp.sum(draw, axis=0, keepdims=True)
    drate_ref[1:2] += jnp.sum(q * (-dtc * rates), axis=0, keepdims=True)


def returned_kernel(dpre_ref, dshare_ref, next_ref, taps_ref, dstep_ref, out_ref, *, share, heads):
    seg, width = dpre_ref.shape[1:]
    for at in range(0, width + lanes, lanes):
        here = slice(at, at + lanes)
        own = dpre_ref[0, :, here] if at < width else dshare_ref[0]
        x = jnp.concatenate([own, next_ref[0, :, here]], axis=0)
        total = x[:seg] * taps_ref[3:4, here]
        for k in range(3):
            by = 3 - k
            total = total + pltpu.roll(x, seg + 8 - by, 0)[:seg] * taps_ref[k : k + 1, here]
        if at == width:
            step = pltpu.roll(dstep_ref[0].astype(f32), share, 1)
            lane = iota((seg, lanes), 1)
            total = jnp.where(lane < share, total, jnp.where(lane < share + heads, step, 0.0))
        out_ref[0, :, here] = total.astype(bf16)


def call(kernel, grid, ins, outs, name, ids=None, flops=0, scratch=(), far=False, **statics):
    def spec(shape, index):
        if index is None:
            return pl.BlockSpec(tuple(shape), lambda s, *i: (0,) * len(shape))
        block, at = index
        return pl.BlockSpec((block,) + tuple(shape[1:]), lambda s, *i: (at(s, *i),) + (0,) * (len(shape) - 1))

    moved = sum(a.size * a.dtype.itemsize for a, _ in ins)
    for shape, dtype, _ in outs:
        size = 1
        for d in shape:
            size *= d
        moved += size * jnp.dtype(dtype).itemsize
    return pl.pallas_call(
        functools.partial(kernel, **statics),
        grid_spec=pltpu.PrefetchScalarGridSpec(
            num_scalar_prefetch=0 if ids is None else 1,
            grid=(grid,),
            in_specs=[spec(a.shape, index) for a, index in ins],
            out_specs=[spec(shape, index) for shape, _, index in outs],
            scratch_shapes=list(scratch),
        ),
        out_shape=[(pltpu.HBM if far else jax.ShapeDtypeStruct)(shape, dtype) for shape, dtype, _ in outs],
        compiler_params=pltpu.CompilerParams(vmem_limit_bytes=16 << 20),
        cost_estimate=pl.CostEstimate(flops=flops, bytes_accessed=moved, transcendentals=0),
        name=name,
    )(*([] if ids is None else [ids]), *[pltpu.with_memory_space_constraint(a, pltpu.HBM) if far else a for a, _ in ins])


each = (1, lambda s, *i: s)


def swap(value, axis, by):
    count = lax.axis_size(axis)
    return lax.ppermute(value, axis, [(i, i ^ by) for i in range(count)])


def all_slots(value, axis, first=None):
    count = lax.axis_size(axis)
    by = count // 2
    offsets = [0]
    while by:
        value = jnp.concatenate([value, swap(value, axis, by)], axis=0)
        if first is not None:
            value, first = tied(value, first), None
        offsets += [j ^ by for j in offsets]
        by //= 2
    size = value.shape[0] // count
    where = [offsets.index(j) for j in range(count)]
    return jnp.concatenate([value[i * size : (i + 1) * size] for i in where], axis=0)


def blocks_turned(value, by, owners):
    size = value.shape[-1] // owners
    return jnp.concatenate([value[..., (j ^ by) * size : ((j ^ by) + 1) * size] for j in range(owners)], axis=-1)


def to_owner(value, axis, turn=False, first=None):
    count = lax.axis_size(axis)
    by = 1
    while by < count:
        value = value.reshape((value.shape[0] // 2, 2) + value.shape[1:])
        other = swap(value[:, 1].astype(bf16), axis, by).astype(f32)
        value = value[:, 0] + (blocks_turned(other, by, count) if turn else other)
        if first is not None:
            value, first = tied(value, first), None
        by *= 2
    return value[0]


def halved_start(value, axis, by):
    value = value.reshape((value.shape[0] // 2, 2) + value.shape[1:])
    bit = (lax.axis_index(axis) // by) % 2
    keep = lax.dynamic_index_in_dim(value, bit, 1, False)
    give = lax.dynamic_index_in_dim(value, 1 - bit, 1, False)
    return keep, swap(give, axis, by)


def halved_end(pair, *others):
    keep, came = tied(pair, others) if others else pair
    return (keep.astype(f32) + came.astype(f32)).astype(bf16)


def halved_from(value, axis, by):
    while value.shape[0] > 1:
        value = halved_end(halved_start(value, axis, by))
        by *= 2
    return value[0]


def tied(value, *others):
    return lax.optimization_barrier((value, others))[0]


def gather_step(value, axis, by, *others):
    came = swap(value, axis, by)
    return jnp.concatenate([value, tied(came, others) if others else came], axis=0)


def gathered(value, axis, by):
    while by:
        value = gather_step(value, axis, by)
        by //= 2
    return value


def reversed_bits(j, count):
    out, by = 0, 1
    while by < count:
        out = out * 2 + (j // by) % 2
        by *= 2
    return out


def traded(value, axis):
    count = lax.axis_size(axis)
    size = value.shape[-1] // count
    parts = [value[:, j * size : (j + 1) * size] for j in range(count)]
    return jnp.stack([swap(part, axis, j) if j else part for j, part in enumerate(parts)])


def exchange(value, axis):
    return lax.all_to_all(value, axis, 0, 0)


def in_order(parts, index):
    stacked = jnp.stack(parts)
    return jnp.concatenate([lax.dynamic_index_in_dim(stacked, index ^ a, 0) for a in range(len(parts))])


def assemble_kernel(ids_ref, gate_ref, *refs, share, heads):
    conv_refs, (weight_ref, out_ref, tail_ref, sum_ref) = refs[:-4], refs[-4:]
    step = pl.program_id(0)
    count, owners = gate_ref.shape[:2]
    channels = out_ref.shape[0]

    def place_of(q):
        return reversed_bits(ids_ref[0] ^ q, count)

    @pl.when(step == 0)
    def _():
        sum_ref[...] = jnp.zeros_like(sum_ref)

    def put(at, value):
        size = value.shape[0]
        out_ref[at : at + size] = value
        sum_ref[0:1] += jnp.sum(value * weight_ref[at : at + size].astype(f32), axis=0, keepdims=True)

    def parts():
        at = 0
        for ref in conv_refs:
            for q in range(count):
                yield at, ref, q
                at += ref.shape[2]

    @pl.when(step < owners)
    def _():
        rows = gate_ref.shape[2]
        for q in range(count):
            put(q * rows, gate_ref[place_of(q), ids_ref[1] ^ step].astype(f32))

    @pl.when(step // owners == 1)
    def _():
        for at, ref, q in parts():
            size = min(ref.shape[2], channels - at)
            if size > 0:
                put(at, ref[place_of(q), ids_ref[1] ^ (step % owners), :size].astype(f32))

    @pl.when(step == 2 * owners)
    def _():
        for a in range(owners):
            found = []
            for at, ref, q in parts():
                skip = max(0, channels - at)
                if skip < ref.shape[2]:
                    found.append(ref[place_of(q), ids_ref[1] ^ a].astype(f32)[skip:])
            value = jnp.concatenate(found, axis=0)
            tail_ref[a] = value
            put(a * share, value[:share])
            put(owners * share + a * heads, value[share : share + heads])


def rows_kernel(ids_ref, *refs, parts):
    bufs, (weight_ref, out_ref, sum_ref) = refs[: len(parts)], refs[len(parts) :]
    total = jnp.zeros((out_ref.shape[0], 1), f32)
    for ref, (start, size) in zip(bufs, parts, strict=True):
        value = ref[0].astype(f32)
        out_ref[:, start : start + size] = value
        total = total + jnp.sum(value * weight_ref[:, start : start + size].astype(f32), axis=1, keepdims=True)
    sum_ref[...] = total


def per_device(tokens, lengths, norm_gain, in_weight, conv_weight, conv_bias, dt_bias, decay_log, skip_gain, gated_gain, out_weight, cotangent):
    nf, nq = lax.axis_size("fsdp"), lax.axis_size("seq")
    me, place = lax.axis_index("fsdp"), lax.axis_index("seq")
    _, seg, width = tokens.shape
    rows = in_weight.shape[0]
    channels = out_weight.shape[0]
    inner = channels * nf
    heads = dt_bias.shape[0]
    conv_own = conv_weight.shape[1]
    state = (conv_own * nf - inner) // 2
    share = 2 * state // nf
    slots = nf

    ids = jnp.stack([place, me]).astype(jnp.int32)
    per_slot = nq // slots
    piece = channels // per_slot

    weight = in_weight.T
    quarter, side = channels // 4, (place % 2) * 2 + (place // 2) % 2
    got, first, last = [], [], []
    for j in range(nf):
        start = inner + (me ^ j) * channels
        if j < 2:
            give = lax.dynamic_slice_in_dim(weight, start, channels, 0)
            got.append(swap(give, "fsdp", j) if j else give)
        else:
            mine = swap(lax.dynamic_slice_in_dim(weight, start + side * quarter, quarter, 0), "fsdp", j)
            near = swap(mine, "seq", 2)
            first.append(mine)
            last.append(swap(jnp.stack([mine, near]), "seq", 1))
            got += [mine, near, last[-1]]
    x_main = all_slots(tied(tokens, first), "fsdp", last)
    before = lax.ppermute(tokens[0, seg - 3 :], "seq", [(i, i + 1) for i in range(nq - 1)])

    def padded(rows_):
        return jnp.pad(rows_, ((0, 0), (0, width - rows_.shape[1])))

    small = jnp.concatenate(
        [padded(conv_weight), padded(conv_bias[None]), padded(norm_gain[None]), jnp.zeros((7, width), bf16), before], axis=0
    )
    x_small = all_slots(tied(small[None], first), "fsdp")
    listed = [x_small[j] for j in range(nf)]
    norm_all = in_order([part[5, :rows] for part in listed], me).astype(f32).reshape(1, width)
    taps_all = in_order([part[:5, :conv_own] for part in listed], me).astype(f32)
    taps_all = taps_all.reshape(nf, 5, conv_own).transpose(1, 0, 2).reshape(5, -1)
    taps_all = jnp.pad(taps_all, ((0, 3), (0, 0)))
    taps = jnp.concatenate([lax.dynamic_slice_in_dim(taps_all, me * channels, channels, 1), taps_all[:, inner:]], axis=1)
    taps_share = lax.dynamic_slice_in_dim(taps_all, inner + me * share, share, 1)
    rate = jnp.stack([dt_bias.astype(f32), jnp.exp(decay_log.astype(f32))])
    rate = jnp.pad(rate, ((0, 6), (0, lanes - heads)))
    vec = jnp.stack([jnp.repeat(skip_gain.astype(f32), head_size), gated_gain.astype(f32)])
    vec = jnp.pad(vec, ((0, 6), (0, 0)))

    rest = all_slots(weight[2 * inner :][None], "fsdp")
    cw = channels + 2 * state
    (w_conv,) = call(
        weight_kernel,
        1,
        [(part, None) for part in got] + [(rest, None)],
        [((cw + lanes, width), bf16, None)],
        "weights",
        ids=ids,
        owners=nf,
        state=state,
        heads=heads,
    )

    (normed,) = call(
        normalize_kernel,
        slots,
        [(x_main, each), (x_small, each), (norm_all, None)],
        [((slots, halo + seg, width), bf16, each)],
        "normalize",
        ids=ids,
        owners=nf,
    )
    inputs = tokens[0].astype(f32)
    valid = (place * seg + jnp.arange(seg) < lengths[0]).astype(f32)[:, None]
    upstream = valid * cotangent[0].astype(f32)

    weight_later, later = tied((weight, upstream.astype(bf16)), last)
    gives = [lax.dynamic_slice_in_dim(weight_later, (me ^ j) * channels, channels, 0) for j in range(nf)]
    w_gate = jnp.concatenate([swap(g, "fsdp", j) if j else g for j, g in enumerate(gives)], axis=1)
    back_branch = all_slots(later[None], "fsdp")

    def project(x, w):
        return lax.dot_general(x, w, (((2,), (1,)), ((), ())), preferred_element_type=f32)

    pc = project(normed, w_conv).astype(bf16)
    main = normed[:, halo:]
    tall = 16
    statics = dict(channels=channels, state=state)
    turned = (per_slot, lambda s, *i: s)
    act, s_local, lac, dtc, lar, dtr = call(
        states_kernel,
        slots,
        [(pc, each), (taps, None), (rate, None)],
        [
            ((slots, seg, cw), bf16, each),
            ((nq, piece + 16, state), bf16, turned),
            ((slots, seg, lanes), f32, each),
            ((slots, seg, lanes), f32, each),
            ((slots, tall, seg), f32, each),
            ((slots, tall, seg), f32, each),
        ],
        "states",
        rows=piece,
        **statics,
    )
    (y_local,) = call(
        local_kernel,
        slots,
        [(act, each), (lac, each), (lar, each), (dtr, each)],
        [((slots, seg, channels), f32, each)],
        "local",
        flops=2 * slots * seg * seg * channels,
        **statics,
    )
    came, y_local = lax.optimization_barrier((exchange(s_local, "seq"), y_local))
    (reached,) = call(
        chain_kernel, 1, [(came, None)], [((nq, piece, state), bf16, None)], "chain", ids=ids, rows=piece, count=per_slot
    )
    s_in = exchange(reached, "seq").reshape(slots, channels, state)

    gate = project(main, w_gate).astype(bf16)
    bg = lax.dot_general(back_branch, out_weight, (((2,), (1,)), ((), ())), preferred_element_type=f32).astype(bf16)
    y, stats = call(
        finish_kernel,
        slots,
        [(y_local, each), (act, each), (lac, each), (s_in, each), (gate, each), (bg, each), (vec, None)],
        [((slots, seg, channels), f32, each), ((slots, 8, seg), f32, each)],
        "finish",
        far=True,
        **statics,
    )
    shares = [(swap(stats, "fsdp", j) if j else stats, (1, lambda s, j=j: s ^ j)) for j in range(nf)]
    gated_out, dgate, dy, pos, dsin, dskip = call(
        norm_kernel,
        slots,
        [(y, each), (act, each), (lac, each), (gate, each), (bg, each), (vec, None)] + shares,
        [
            ((slots, seg, channels), bf16, each),
            ((slots, seg, channels), bf16, each),
            ((slots, seg, channels), f32, each),
            ((slots, seg, lanes), f32, each),
            ((nq, piece, state), bf16, turned),
            ((8, channels), f32, None),
        ],
        "norm",
        far=True,
        inner=inner,
        rows=piece,
        **statics,
    )

    def grad_of(dz, x):
        return lax.dot_general(dz, x, (((0, 1), (0, 1)), ((), ())), preferred_element_type=f32).astype(bf16)

    def cut(value):
        size = value.shape[-1] // 2
        return [value] if size // nq % 8 else [value[..., :size], value[..., size:]]

    def pieces(g):
        return g.reshape((nq, g.shape[0] // nq) + g.shape[1:])

    barrier = lax.optimization_barrier
    gate_grad, out_grad = grad_of(dgate, main), grad_of(gated_out, back_branch)
    back_came = exchange(tied(dsin, gate_grad), "seq")
    gate_step = halved_start(pieces(gate_grad), "seq", 1)
    out_step = halved_start(pieces(out_grad), "seq", 1)
    branch = lax.dot_general(gated_out, out_weight, (((2,), (0,)), ((), ())), preferred_element_type=f32)
    branch = to_owner(branch, "fsdp")
    (reached,) = call(
        back_chain_kernel,
        1,
        [(back_came, None), (came, None)],
        [((nq, piece, state), bf16, None)],
        "back_chain",
        ids=ids,
        rows=piece,
        count=per_slot,
    )
    g_end = exchange(reached, "seq").reshape(slots, channels, state)
    gate_sum = halved_end(gate_step, reached)
    dy_later, gate_sum = barrier((dy, gate_sum))
    gate_step = halved_start(gate_sum, "seq", 2)

    r_local, dbc = call(
        backward_kernel,
        slots,
        [(act, each), (dy_later, each), (lac, each), (lar, each), (dtr, each), (s_in, each)],
        [((slots, seg, channels), f32, each), ((slots, seg, 2 * state), f32, each)],
        "backward",
        far=True,
        flops=4 * slots * seg * seg * channels,
        **statics,
    )
    gate_sum = halved_end(gate_step, dbc)
    dbc, gate_sum = barrier((dbc, gate_sum))
    gate_step = halved_start(gate_sum, "seq", 4)
    d_shares = call(
        rows_grad_kernel,
        slots,
        [(act, each), (lac, each), (dtc, each), (g_end, each), (dbc, each)],
        [((slots, share, seg), bf16, each)] * nf,
        "rows_grad",
        ids=ids,
        scratch=[pltpu.VMEM((2 * state, seg), f32)],
        **statics,
    )
    out_sum = halved_end(out_step, d_shares[0])
    r_local, out_sum, own_share = barrier((r_local, out_sum, d_shares[0]))
    out_step = halved_start(out_sum, "seq", 2)
    d_shares = [own_share] + [swap(d, "fsdp", j) for j, d in enumerate(d_shares) if j]
    dpre, first, dstep, dtaps, drate = call(
        carry_kernel,
        slots,
        [
            (pc, each), (taps, None), (rate, None), (act, each), (dy, each), (r_local, each), (pos, each), (lac, each),
            (dtc, each), (g_end, each), (s_in, each), (s_local, turned), (vec, None),
        ],
        [
            ((slots, seg, channels), f32, each),
            ((slots, 8, channels), f32, each),
            ((slots, seg, lanes), bf16, each),
            ((8, channels), f32, None),
            ((8, lanes), f32, None),
        ],
        "carry",
        far=True,
        rows=piece,
        **statics,
    )
    dpre, gate_step, out_step, d_shares, branch = barrier((dpre, gate_step, out_step, d_shares, branch))
    gate_sum, out_sum = halved_from(halved_end(gate_step), "seq", 8), halved_end(out_step)
    pc_later, gate_sum, out_sum, d_shares = barrier((pc, gate_sum, out_sum, d_shares))
    out_step = halved_start(out_sum, "seq", 4)
    gate_sum = traded(gate_sum, "fsdp")[None]
    dpre_share, first_share, dtaps_share = call(
        share_kernel,
        slots,
        [(pc_later, each), (taps_share.T, None)]
        + [(d, (1, lambda s, i, j=j: s ^ j)) for j, d in enumerate(d_shares)],
        [((slots, seg, lanes), f32, each), ((slots, 8, lanes), f32, each), ((share, lanes), f32, None)],
        "share",
        ids=ids,
        scratch=[pltpu.VMEM((2 * state, seg), f32)],
        **statics,
    )
    first, first_share, gate_sum = barrier((first, first_share, gate_sum))
    behind = [(i, i - 1) for i in range(1, nq)]
    after = lax.ppermute(jnp.concatenate([first, first_share], axis=2), "seq", behind)
    gate_more = swap(gate_sum, "seq", nq // 2)
    after, gate_more = barrier((after, gate_more))
    gate_sum = jnp.concatenate([gate_sum, gate_more], axis=0)
    taps_back = jnp.concatenate([taps[:, :channels], jnp.pad(taps_share, ((0, 0), (0, lanes - share)))], axis=1)
    (dconv,) = call(
        returned_kernel,
        slots,
        [(dpre, each), (dpre_share, each), (after, each), (taps_back, None), (dstep, each)],
        [((slots, seg, channels + lanes), bf16, each)],
        "returned",
        share=share,
        heads=heads,
    )

    per = channels // rows
    head_rows = jnp.stack([drate[0, :heads], drate[1, :heads], jnp.sum(dskip[0].reshape(heads, head_size), axis=1)])
    block = jnp.concatenate(
        [
            dtaps[:5].reshape(5 * per, rows),
            jnp.pad(dtaps_share[:, :5].T, ((0, 0), (0, rows - share))),
            jnp.pad(head_rows, ((0, 0), (0, rows - heads))),
        ],
        axis=0,
    )
    extra = block.shape[0]
    block = jnp.tile(block, (1, nf)).astype(bf16)
    conv_grads = [grad_of(part, main) for part in cut(dconv)]
    spare = channels + share + heads - sum(g.shape[0] for g in conv_grads[:-1])
    conv_grads[-1] = lax.dynamic_update_slice_in_dim(conv_grads[-1], block, spare, 0)

    out_unit = channels // nq
    conv_steps = [halved_start(pieces(g), "seq", 1) for g in conv_grads]
    out_sum = halved_from(halved_end(out_step, conv_grads), "seq", 8)[None]
    gate_sum = gather_step(gate_sum, "seq", nq // 4, out_sum)
    conv_sums = [halved_end(step, gate_sum) for step in conv_steps]
    late_conv = tied(dconv, conv_sums[0])
    out_sum = gather_step(out_sum, "seq", nq // 2, conv_sums)
    gate_bufs = [gathered(gate_sum, "seq", nq // 8)]
    conv_steps = [halved_start(g, "seq", 2) for g in conv_sums]
    conv_sums = [halved_end(step) for step in conv_steps]
    conv_steps = [halved_start(g, "seq", 4) for g in conv_sums]
    out_sum = gather_step(tied(out_sum, conv_sums), "seq", nq // 4, *[step[1] for step in conv_steps])
    conv_sums = [halved_from(halved_end(step), "seq", 8) for step in conv_steps]
    out_parts = [gathered(out_sum, "seq", nq // 8)]
    conv_sums, gate_bufs = barrier((conv_sums, gate_bufs))
    conv_sums = [traded(g, "fsdp") for g in conv_sums]
    conv_bufs = [gather_step(g[None], "seq", nq // 2) for g in conv_sums]
    tied_bufs = conv_bufs
    conv_bufs = [gather_step(g, "seq", nq // 4) for g in conv_bufs]
    conv_bufs, out_parts = barrier((conv_bufs, out_parts))
    conv_bufs = [gathered(g, "seq", nq // 8) for g in conv_bufs]
    place_of = jnp.stack([reversed_bits(place ^ q, nq) for q in range(nq)])
    if all(buf.shape[2] % 8 == 0 for buf in gate_bufs + conv_bufs):
        g_in, tail, norm_sum = call(
            assemble_kernel,
            2 * nf + 1,
            [(buf, None) for buf in gate_bufs + conv_bufs] + [(weight, (channels, lambda s, i: s))],
            [
                (weight.shape, f32, (channels, lambda s, i: s)),
                ((nf, lanes, rows), f32, None),
                ((8, rows), f32, None),
            ],
            "assemble",
            ids=ids,
            share=share,
            heads=heads,
        )
        norm_sum = norm_sum[0]
    else:
        order = me ^ jnp.arange(nf)

        def natural(bufs):
            bufs = [buf[place_of][:, order].astype(f32).transpose(1, 0, 2, 3).reshape(nf, -1, rows) for buf in bufs]
            return jnp.concatenate(bufs, axis=1)

        gate_all, conv_all = natural(gate_bufs), natural(conv_bufs)
        tail = conv_all[:, channels:]
        joined = [gate_all.reshape(inner, rows), conv_all[:, :channels].reshape(inner, rows)]
        joined += [tail[:, :share].reshape(nf * share, rows), tail[:, share : share + heads].reshape(nf * heads, rows)]
        g_in = jnp.concatenate(joined, axis=0)
        norm_sum = jnp.sum(g_in * weight.astype(f32), axis=0)
    if out_unit % 16 == 0:
        sizes = [part.shape[-1] for part in out_parts]
        g_out, gated_sum = call(
            rows_kernel,
            nq,
            [(part, (1, lambda s, i: reversed_bits(i[0] ^ s, nq))) for part in out_parts] + [(out_weight, (out_unit, lambda s, i: s))],
            [(out_weight.shape, f32, (out_unit, lambda s, i: s)), ((channels, 1), f32, (out_unit, lambda s, i: s))],
            "rows",
            ids=ids,
            parts=[(sum(sizes[:i]), size) for i, size in enumerate(sizes)],
        )
        gated_sum = gated_sum[:, 0]
    else:
        g_out = jnp.concatenate([part[place_of].astype(f32).reshape(channels, -1) for part in out_parts], axis=1)
        gated_sum = jnp.sum(g_out * out_weight.astype(f32), axis=1)

    norm_grad = norm_sum / norm_gain.astype(f32)
    gated_grad = gated_sum / gated_gain.astype(f32)

    got = tail[:, share + heads : share + heads + extra]
    tap_grads = jnp.concatenate(
        [
            got[:, : 5 * per].reshape(nf, 5, channels).transpose(1, 0, 2).reshape(5, inner),
            got[:, 5 * per : 5 * per + 5, :share].transpose(1, 0, 2).reshape(5, 2 * state),
        ],
        axis=1,
    )
    tap_grads = lax.dynamic_slice_in_dim(tap_grads, me * conv_own, conv_own, 1)
    head_grads = lax.dynamic_index_in_dim(got, me, 0, False)[5 * per + 5 :, :heads]

    mixed = (valid * (inputs + branch)).astype(bf16)

    w_share = lax.dynamic_slice_in_dim(w_conv, channels + me * share, share, 0)
    w_last = jnp.concatenate([w_share, w_conv[cw : cw + lanes - share]], axis=0)

    def back(dz, w):
        return lax.dot_general(dz, w, (((2,), (0,)), ((), ())), preferred_element_type=f32)

    bn = back(dgate, w_gate) + back(late_conv[..., :channels], w_conv[:channels]) + back(late_conv[..., channels:], w_last)
    bn = to_owner(bn, "fsdp", turn=True, first=tied_bufs)
    (input_grad,) = call(
        input_kernel,
        1,
        [(bn, None), (norm_all, None), (tokens[0], None), (cotangent[0], None), (valid, None)],
        [((seg, width), f32, None)],
        "input",
        ids=ids,
        owners=nf,
    )
    return (
        mixed[None],
        input_grad[None],
        norm_grad,
        g_in.T,
        tap_grads[:4],
        tap_grads[4],
        head_grads[0],
        head_grads[1],
        head_grads[2],
        gated_grad,
        g_out,
    )


def solution(mesh):
    whole, rows = P("fsdp", "seq", None), P("fsdp", None)
    one, columns = P("fsdp"), P(None, "fsdp")
    return jax.shard_map(
        per_device,
        mesh=mesh,
        in_specs=(whole, one, one, rows, columns, one, one, one, one, one, rows, whole),
        out_specs=(whole, whole, one, rows, columns, one, one, one, one, one, rows),
        check_vma=False,
    )
```

```python
import functools

import jax
import jax.numpy as jnp
from jax import lax
from jax.experimental import pallas as pl
from jax.experimental.pallas import tpu as pltpu
from jax.sharding import PartitionSpec as P

epsilon = 1e-05
bf16, f32 = jnp.bfloat16, jnp.float32
best = lax.Precision.HIGHEST
halo = 16
lanes = 128
head_size = 64


def dot(a, b, ca=1, cb=0, precision=None):
    return lax.dot_general(
        a, b, (((ca,), (cb,)), ((), ())), preferred_element_type=f32, precision=precision
    )


def sigmoid(v):
    return 0.5 + 0.5 * jnp.tanh(0.5 * v)


def iota(shape, axis):
    return lax.broadcasted_iota(jnp.int32, shape, axis)


def spread(columns, pair):
    first, second = 2 * pair, 2 * pair + 1
    rows = columns.shape[0]
    return jnp.where(
        iota((rows, lanes), 1) < head_size,
        columns[:, first : first + 1],
        columns[:, second : second + 1],
    )


def per_head(total, products, pair):
    rows = products.shape[0]
    lane = iota((rows, lanes), 1)
    low = jnp.sum(jnp.where(lane < head_size, products, 0.0), axis=1, keepdims=True)
    high = jnp.sum(jnp.where(lane < head_size, 0.0, products), axis=1, keepdims=True)
    return total + jnp.where(lane == 2 * pair, low, jnp.where(lane == 2 * pair + 1, high, 0.0))


def in_heads(products, pair):
    rows = jnp.sum(products, axis=1, keepdims=True)
    low, high = jnp.sum(rows[:head_size]), jnp.sum(rows[head_size:])
    lane = iota((1, lanes), 1)
    return jnp.where(lane == 2 * pair, low, jnp.where(lane == 2 * pair + 1, high, 0.0))


def convolved(pc_ref, taps_ref, at):
    x = pc_ref[0, :, at : at + lanes].astype(f32)
    tapped = [pltpu.roll(x, 3 - k, 0)[halo:] for k in range(3)] + [x[halo:]]
    pre = taps_ref[4:5, at : at + lanes]
    for k in range(4):
        pre = pre + tapped[k] * taps_ref[k : k + 1, at : at + lanes]
    return tapped, pre


def pieces_out(out_ref, whole, rows):
    for p in range(out_ref.shape[0]):
        out_ref[p, :rows] = whole[p * rows : (p + 1) * rows]


def pieces_in(ref, rows):
    return jnp.concatenate([ref[p, :rows] for p in range(ref.shape[0])], axis=0)


def block_of(index, size):
    return pl.ds(pl.multiple_of(index * size, size), size)


def columns_of(ref, index, size):
    if size % lanes == 0:
        return ref[:, block_of(index, size)]
    value = ref[:, :size]
    for a in range(1, ref.shape[1] // size):
        value = jnp.where(index == a, ref[:, a * size : (a + 1) * size], value)
    return value


def normalize_kernel(ids_ref, main_ref, small_ref, gain_ref, out_ref, *, owners):
    size = out_ref.shape[2] // owners
    for ref, at in ((small_ref, 0), (main_ref, halo)):
        x = ref[0].astype(f32)
        inv = lax.rsqrt(jnp.mean(x * x, axis=1, keepdims=True) + epsilon)
        for j in range(owners):
            own = ids_ref[1] ^ j
            part = columns_of(ref.at[0], own, size).astype(f32) * inv * columns_of(gain_ref, own, size)
            out_ref[0, at : at + x.shape[0], j * size : (j + 1) * size] = part.astype(bf16)


def weight_kernel(ids_ref, *refs, owners, state, heads):
    rest_ref, out_ref = refs[-2:]
    size = rest_ref.shape[2]
    channels = out_ref.shape[0] - 2 * state - lanes
    n = 0
    for j in range(owners):
        own = slice(j * size, (j + 1) * size)
        if j < 2:
            out_ref[:channels, own] = refs[n][...]
            n += 1
        else:
            quarter = channels // 4
            for far_side in range(2):
                for near in range(2):
                    place = ((ids_ref[0] % 2) ^ far_side) * 2 + (((ids_ref[0] // 2) % 2) ^ near)
                    ref = refs[n] if far_side == 0 else refs[n].at[near]
                    out_ref[block_of(place, quarter), own] = ref[...]
                    n += 1 - far_side
            n += 1
        out_ref[channels : channels + 2 * state, own] = rest_ref[j, : 2 * state]
        rows = owners * heads
        pick = iota((lanes, rows), 1) == ids_ref[1] * heads + iota((lanes, rows), 0)
        pick = jnp.where(iota((lanes, rows), 0) < heads, pick.astype(f32), 0.0).astype(bf16)
        out_ref[channels + 2 * state :, own] = dot(pick, rest_ref[j, 2 * state : 2 * state + rows]).astype(bf16)


def input_kernel(ids_ref, bn_ref, gain_ref, tokens_ref, cot_ref, valid_ref, out_ref, *, owners):
    x = tokens_ref[...].astype(f32)
    width = x.shape[1]
    size = width // owners
    inv = lax.rsqrt(jnp.mean(x * x, axis=1, keepdims=True) + epsilon)
    lean = jnp.zeros_like(inv)
    for a in range(owners):
        here = slice(a * size, (a + 1) * size)
        bn = columns_of(bn_ref, ids_ref[1] ^ a, size) * gain_ref[:, here]
        lean = lean + jnp.sum(bn * x[:, here], axis=1, keepdims=True)
    lean = lean * (inv * inv * inv) * (1.0 / width)
    for a in range(owners):
        here = slice(a * size, (a + 1) * size)
        bn = columns_of(bn_ref, ids_ref[1] ^ a, size) * gain_ref[:, here]
        out_ref[:, here] = valid_ref[...] * cot_ref[:, here].astype(f32) + inv * bn - x[:, here] * lean


def of_rows(row, ids_ref, rows, count):
    head = ((ids_ref[0] % count) * rows + iota((rows, lanes), 0)) // head_size
    return jnp.sum(jnp.where(iota((rows, lanes), 1) == head, row, 0.0), axis=1, keepdims=True)


def chain_kernel(ids_ref, in_ref, out_ref, *, rows, count):
    carried = jnp.zeros((rows, lanes), f32)
    for i in range(in_ref.shape[0]):
        out_ref[i] = carried.astype(bf16)
        row = in_ref[i, rows : rows + 1].astype(f32) + in_ref[i, rows + 1 : rows + 2].astype(f32)
        carried = of_rows(row, ids_ref, rows, count) * carried + in_ref[i, :rows].astype(f32)


def back_chain_kernel(ids_ref, in_ref, decay_ref, out_ref, *, rows, count):
    carried = jnp.zeros((rows, lanes), f32)
    for i in reversed(range(in_ref.shape[0])):
        out_ref[i] = carried.astype(bf16)
        row = decay_ref[i, rows : rows + 1].astype(f32) + decay_ref[i, rows + 1 : rows + 2].astype(f32)
        carried = of_rows(row, ids_ref, rows, count) * carried + in_ref[i].astype(f32)


def states_kernel(pc_ref, taps_ref, rate_ref, act_ref, s_ref, lac_ref, dtc_ref, lar_ref, dtr_ref, *, channels, state, rows):
    width = channels + 2 * state
    for at in list(range(channels, width, lanes)) + list(range(0, channels, lanes)):
        _, pre = convolved(pc_ref, taps_ref, at)
        act_ref[0, :, at : at + lanes] = (pre * sigmoid(pre)).astype(bf16)
    seg = act_ref.shape[1]
    z = pc_ref[0, halo:, width : width + lanes].astype(f32) + rate_ref[0:1]
    dtc = jnp.maximum(z, 0.0) + jnp.log1p(jnp.exp(-jnp.abs(z)))
    lower = iota((seg, seg), 0) >= iota((seg, seg), 1)
    lac = dot(lower.astype(f32), -dtc * rate_ref[1:2], precision=best)
    tall = lar_ref.shape[1]
    lac_ref[0], dtc_ref[0], lar_ref[0], dtr_ref[0] = lac, dtc, lac.T[:tall], dtc.T[:tall]
    b_rows = act_ref[0, :, channels : channels + state]
    to_end = jnp.exp(lac[seg - 1 : seg] - lac) * dtc
    states = []
    for pair in range(channels // lanes):
        at = pair * lanes
        weighted = (spread(to_end, pair) * act_ref[0, :, at : at + lanes].astype(f32)).astype(bf16)
        states.append(dot(weighted, b_rows, 0, 0).astype(bf16))
    pieces_out(s_ref, jnp.concatenate(states, axis=0), rows)
    whole = jnp.exp(lac[seg - 1 : seg])
    high = whole.astype(bf16).astype(f32)
    row = iota((16, lanes), 0)
    tail = jnp.where(row == 0, high, jnp.where(row == 1, whole - high, 0.0)).astype(bf16)
    for p in range(s_ref.shape[0]):
        s_ref[p, rows:] = tail


def local_kernel(act_ref, lac_ref, lar_ref, dtr_ref, y_ref, *, channels, state):
    seg = act_ref.shape[1]
    lower = iota((seg, seg), 0) >= iota((seg, seg), 1)
    lac, lar, dtr = lac_ref[0], lar_ref[0], dtr_ref[0]
    both = dot(act_ref[0, :, channels + state :], act_ref[0, :, channels : channels + state], 1, 1)
    for pair in range(channels // lanes):
        at = pair * lanes
        values = act_ref[0, :, at : at + lanes]
        parts = []
        for side in range(2):
            h = 2 * pair + side
            mix = jnp.where(lower, jnp.exp(lac[:, h : h + 1] - lar[h : h + 1]), 0.0) * both * dtr[h : h + 1]
            parts.append(dot(mix.astype(bf16), values[:, side * head_size : (side + 1) * head_size]))
        y_ref[0, :, at : at + lanes] = jnp.concatenate(parts, axis=1)


def finish_kernel(y_ref, act_ref, lac_ref, sin_ref, gate_ref, bg_ref, vec_ref, y_out, stat_ref, *, channels, state):
    seg = y_ref.shape[1]
    c_rows = act_ref[0, :, channels + state : channels + 2 * state]
    decay = jnp.exp(lac_ref[0])
    first = jnp.zeros((seg, 1), f32)
    second = jnp.zeros((seg, 1), f32)
    for pair in range(channels // lanes):
        at = pair * lanes
        here = slice(at, at + lanes)
        carried = dot(c_rows, sin_ref[0, here], 1, 1)
        y = y_ref[0, :, here] + spread(decay, pair) * carried
        y_out[0, :, here] = y
        gate = gate_ref[0, :, here].astype(f32)
        heads = y + vec_ref[0:1, here] * act_ref[0, :, here].astype(f32)
        gated = heads * gate * sigmoid(gate)
        first = first + jnp.sum(gated * gated, axis=1, keepdims=True)
        second = second + jnp.sum(gated * bg_ref[0, :, here].astype(f32) * vec_ref[1:2, here], axis=1, keepdims=True)
    lane = iota((seg, lanes), 1)
    both = jnp.where(lane == 0, first, jnp.where(lane == 1, second, 0.0))
    stat_ref[0] = both.T[:8]


def norm_kernel(y_ref, act_ref, lac_ref, gate_ref, bg_ref, vec_ref, *refs, channels, state, inner, rows):
    stat_refs, (out_ref, dgate_ref, dy_ref, pos_ref, dsin_ref, dskip_ref) = refs[:-6], refs[-6:]
    seg = y_ref.shape[1]
    stats = sum(ref[0] for ref in stat_refs).T
    states = []
    inv = lax.rsqrt(stats[:, 0:1] * (1.0 / inner) + epsilon)
    lean = inv * inv * inv * (stats[:, 1:2] * (1.0 / inner))
    c_rows = act_ref[0, :, channels + state : channels + 2 * state]
    decay = jnp.exp(lac_ref[0])
    pos = jnp.zeros((seg, lanes), f32)

    @pl.when(pl.program_id(0) == 0)
    def _():
        dskip_ref[...] = jnp.zeros_like(dskip_ref)

    for pair in range(channels // lanes):
        at = pair * lanes
        here = slice(at, at + lanes)
        y = y_ref[0, :, here]
        values = act_ref[0, :, here].astype(f32)
        heads = y + vec_ref[0:1, here] * values
        gate = gate_ref[0, :, here].astype(f32)
        sg = sigmoid(gate)
        gated = heads * gate * sg
        gain = vec_ref[1:2, here]
        out_ref[0, :, here] = (gated * inv * gain).astype(bf16)
        dgated = inv * (bg_ref[0, :, here].astype(f32) * gain) - gated * lean
        dgate_ref[0, :, here] = (dgated * heads * (sg * (1.0 + gate * (1.0 - sg)))).astype(bf16)
        dy = dgated * gate * sg
        dy_ref[0, :, here] = dy
        pos = per_head(pos, dy * y, pair)
        states.append(dot((spread(decay, pair) * dy).astype(bf16), c_rows, 0, 0).astype(bf16))
        dskip_ref[0:1, here] += jnp.sum(dy * values, axis=0, keepdims=True)
    pos_ref[0] = pos
    pieces_out(dsin_ref, jnp.concatenate(states, axis=0), rows)


def backward_kernel(act_ref, dy_ref, lac_ref, lar_ref, dtr_ref, sin_ref, r_ref, dbc_ref, *, channels, state):
    seg = dy_ref.shape[1]
    b_rows = act_ref[0, :, channels : channels + state]
    c_rows = act_ref[0, :, channels + state : channels + 2 * state]
    both = dot(c_rows, b_rows, 1, 1)
    lower = iota((seg, seg), 0) >= iota((seg, seg), 1)
    lac, lar, dtr = lac_ref[0], lar_ref[0], dtr_ref[0]
    decay = jnp.exp(lac)
    dboth = jnp.zeros((seg, seg), f32)
    dc = jnp.zeros((seg, state), f32)
    for pair in range(channels // lanes):
        at = pair * lanes
        here = slice(at, at + lanes)
        values = act_ref[0, :, here]
        dy = dy_ref[0, :, here]
        dyl = dy.astype(bf16)
        parts = []
        for side in range(2):
            h = 2 * pair + side
            own = slice(side * head_size, (side + 1) * head_size)
            weights = jnp.where(lower, jnp.exp(lac[:, h : h + 1] - lar[h : h + 1]), 0.0)
            parts.append(dot((weights * both).astype(bf16), dyl[:, own], 0, 0))
            dboth = dboth + dot(dyl[:, own], values[:, own], 1, 1) * (weights * dtr[h : h + 1])
        r_ref[0, :, here] = jnp.concatenate(parts, axis=1)
        dc = dc + dot((spread(decay, pair) * dy).astype(bf16), sin_ref[0, here])
    dlow = dboth.astype(bf16)
    dbc_ref[0, :, :state] = dot(dlow, c_rows, 0, 0)
    dbc_ref[0, :, state:] = dc + dot(dlow, b_rows)


def rows_grad_kernel(ids_ref, act_ref, lac_ref, dtc_ref, g_ref, dbc_ref, *refs, channels, state):
    out_refs, hold = refs[:-1], refs[-1]
    seg = act_ref.shape[1]
    lac, dtc = lac_ref[0], dtc_ref[0]
    weights = jnp.exp(lac[seg - 1 : seg] - lac) * dtc
    db = dbc_ref[0, :, :state]
    for pair in range(channels // lanes):
        here = slice(pair * lanes, (pair + 1) * lanes)
        db = db + dot((spread(weights, pair) * act_ref[0, :, here].astype(f32)).astype(bf16), g_ref[0, here])
    hold[:state] = db.T
    hold[state:] = dbc_ref[0, :, state:].T
    share = out_refs[0].shape[1]
    for j, out_ref in enumerate(out_refs):
        out_ref[0] = hold[block_of(ids_ref[1] ^ j, share)].astype(bf16)


def share_kernel(ids_ref, pc_ref, taps_ref, *refs, channels, state):
    parts, (dpre_ref, first_ref, dtaps_ref, hold) = refs[:-4], refs[-4:]
    seg = pc_ref.shape[1] - halo
    share = parts[0].shape[1]
    own = block_of(ids_ref[1], share)
    hold[...] = pc_ref[0, :, channels : channels + 2 * state].astype(f32)[halo:].T
    x = hold[own]
    hold[:, :halo] = pc_ref[0, :halo, channels : channels + 2 * state].astype(f32).T
    edge = hold[own, :halo]
    lane = iota((share, seg), 1)
    tapped = []
    for k in range(3):
        value = pltpu.roll(x, 3 - k, 1)
        for t in range(3 - k):
            value = jnp.where(lane == t, edge[:, halo - 3 + k + t : halo - 2 + k + t], value)
        tapped.append(value)
    tapped.append(x)
    pre = taps_ref[:, 4:5] + sum(tapped[k] * taps_ref[:, k : k + 1] for k in range(4))
    sg = sigmoid(pre)
    dpre = sum(ref[0].astype(f32) for ref in parts) * (sg * (1.0 + pre * (1.0 - sg)))

    @pl.when(pl.program_id(0) == 0)
    def _():
        dtaps_ref[...] = jnp.zeros_like(dtaps_ref)

    lane = iota((share, lanes), 1)
    total = jnp.zeros((share, lanes), f32)
    for k in range(5):
        column = jnp.sum(dpre * tapped[k] if k < 4 else dpre, axis=1, keepdims=True)
        total = jnp.where(lane == k, column, total)
    dtaps_ref[...] += total
    rows = jnp.concatenate([dpre, jnp.zeros((lanes - share, seg), f32)], axis=0).T
    dpre_ref[0] = rows
    first_ref[0] = rows[:8]


def carry_kernel(pc_ref, taps_ref, rate_ref, act_ref, dy_ref, r_ref, pos_ref, lac_ref, dtc_ref, g_ref, sin_ref, s_ref, vec_ref, dpre_ref, first_ref, dstep_ref, dtaps_ref, drate_ref, *, channels, state, rows):
    seg = dy_ref.shape[1]
    width = channels + 2 * state
    b_rows = act_ref[0, :, channels : channels + state]
    lac, dtc = lac_ref[0], dtc_ref[0]
    last = lac[seg - 1 : seg]
    to_last = jnp.exp(last - lac)
    neg = jnp.zeros((seg, lanes), f32)
    through = jnp.zeros((1, lanes), f32)
    local = jnp.zeros((1, lanes), f32)
    states = pieces_in(s_ref, rows)

    @pl.when(pl.program_id(0) == 0)
    def _():
        dtaps_ref[...] = jnp.zeros_like(dtaps_ref)
        drate_ref[...] = jnp.zeros_like(drate_ref)

    for pair in range(channels // lanes):
        at = pair * lanes
        here = slice(at, at + lanes)
        grad = g_ref[0, here]
        values = act_ref[0, :, here].astype(f32)
        r = r_ref[0, :, here] + spread(to_last, pair) * dot(b_rows, grad, 1, 1)
        neg = per_head(neg, values * r, pair)
        wide = grad.astype(f32)
        through = through + in_heads(wide * sin_ref[0, here].astype(f32), pair)
        local = local + in_heads(wide * states[here].astype(f32), pair)
        tapped, pre = convolved(pc_ref, taps_ref, at)
        sg = sigmoid(pre)
        dpre = (spread(dtc, pair) * r + vec_ref[0:1, here] * dy_ref[0, :, here]) * (sg * (1.0 + pre * (1.0 - sg)))
        dpre_ref[0, :, here] = dpre
        for k in range(4):
            dtaps_ref[k : k + 1, here] += jnp.sum(dpre * tapped[k], axis=0, keepdims=True)
        dtaps_ref[4:5, here] += jnp.sum(dpre, axis=0, keepdims=True)
    first_ref[0] = dpre_ref[0, :8]
    seed = jnp.exp(last) * through + local
    upper = (iota((seg, seg), 0) <= iota((seg, seg), 1)).astype(f32)
    q = dot(upper, pos_ref[0] - dtc * neg, precision=best) + seed
    rates = rate_ref[1:2]
    z = pc_ref[0, halo:, width : width + lanes].astype(f32) + rate_ref[0:1]
    draw = (neg - rates * q) * sigmoid(z)
    dstep_ref[0] = draw.astype(bf16)
    drate_ref[0:1] += jnp.sum(draw, axis=0, keepdims=True)
    drate_ref[1:2] += jnp.sum(q * (-dtc * rates), axis=0, keepdims=True)


def returned_kernel(dpre_ref, dshare_ref, next_ref, taps_ref, dstep_ref, out_ref, *, share, heads):
    seg, width = dpre_ref.shape[1:]
    for at in range(0, width + lanes, lanes):
        here = slice(at, at + lanes)
        own = dpre_ref[0, :, here] if at < width else dshare_ref[0]
        x = jnp.concatenate([own, next_ref[0, :, here]], axis=0)
        total = x[:seg] * taps_ref[3:4, here]
        for k in range(3):
            by = 3 - k
            total = total + pltpu.roll(x, seg + 8 - by, 0)[:seg] * taps_ref[k : k + 1, here]
        if at == width:
            step = pltpu.roll(dstep_ref[0].astype(f32), share, 1)
            lane = iota((seg, lanes), 1)
            total = jnp.where(lane < share, total, jnp.where(lane < share + heads, step, 0.0))
        out_ref[0, :, here] = total.astype(bf16)


def call(kernel, grid, ins, outs, name, ids=None, flops=0, scratch=(), far=False, **statics):
    def spec(shape, index):
        if index is None:
            return pl.BlockSpec(tuple(shape), lambda s, *i: (0,) * len(shape))
        block, at = index
        return pl.BlockSpec((block,) + tuple(shape[1:]), lambda s, *i: (at(s, *i),) + (0,) * (len(shape) - 1))

    moved = sum(a.size * a.dtype.itemsize for a, _ in ins)
    for shape, dtype, _ in outs:
        size = 1
        for d in shape:
            size *= d
        moved += size * jnp.dtype(dtype).itemsize
    return pl.pallas_call(
        functools.partial(kernel, **statics),
        grid_spec=pltpu.PrefetchScalarGridSpec(
            num_scalar_prefetch=0 if ids is None else 1,
            grid=(grid,),
            in_specs=[spec(a.shape, index) for a, index in ins],
            out_specs=[spec(shape, index) for shape, _, index in outs],
            scratch_shapes=list(scratch),
        ),
        out_shape=[(pltpu.HBM if far else jax.ShapeDtypeStruct)(shape, dtype) for shape, dtype, _ in outs],
        compiler_params=pltpu.CompilerParams(vmem_limit_bytes=16 << 20),
        cost_estimate=pl.CostEstimate(flops=flops, bytes_accessed=moved, transcendentals=0),
        name=name,
    )(*([] if ids is None else [ids]), *[pltpu.with_memory_space_constraint(a, pltpu.HBM) if far else a for a, _ in ins])


each = (1, lambda s, *i: s)


def swap(value, axis, by):
    count = lax.axis_size(axis)
    return lax.ppermute(value, axis, [(i, i ^ by) for i in range(count)])


def all_slots(value, axis, first=None):
    count = lax.axis_size(axis)
    by = count // 2
    offsets = [0]
    while by:
        value = jnp.concatenate([value, swap(value, axis, by)], axis=0)
        if first is not None:
            value, first = tied(value, first), None
        offsets += [j ^ by for j in offsets]
        by //= 2
    size = value.shape[0] // count
    where = [offsets.index(j) for j in range(count)]
    return jnp.concatenate([value[i * size : (i + 1) * size] for i in where], axis=0)


def blocks_turned(value, by, owners):
    size = value.shape[-1] // owners
    return jnp.concatenate([value[..., (j ^ by) * size : ((j ^ by) + 1) * size] for j in range(owners)], axis=-1)


def to_owner(value, axis, turn=False, first=None):
    count = lax.axis_size(axis)
    by = 1
    while by < count:
        value = value.reshape((value.shape[0] // 2, 2) + value.shape[1:])
        other = swap(value[:, 1].astype(bf16), axis, by).astype(f32)
        value = value[:, 0] + (blocks_turned(other, by, count) if turn else other)
        if first is not None:
            value, first = tied(value, first), None
        by *= 2
    return value[0]


def halved_start(value, axis, by):
    value = value.reshape((value.shape[0] // 2, 2) + value.shape[1:])
    bit = (lax.axis_index(axis) // by) % 2
    keep = lax.dynamic_index_in_dim(value, bit, 1, False)
    give = lax.dynamic_index_in_dim(value, 1 - bit, 1, False)
    return keep, swap(give, axis, by)


def halved_end(pair, *others):
    keep, came = tied(pair, others) if others else pair
    return (keep.astype(f32) + came.astype(f32)).astype(bf16)


def halved_from(value, axis, by):
    while value.shape[0] > 1:
        value = halved_end(halved_start(value, axis, by))
        by *= 2
    return value[0]


def tied(value, *others):
    return lax.optimization_barrier((value, others))[0]


def gather_step(value, axis, by, *others):
    came = swap(value, axis, by)
    return jnp.concatenate([value, tied(came, others) if others else came], axis=0)


def gathered(value, axis, by):
    while by:
        value = gather_step(value, axis, by)
        by //= 2
    return value


def reversed_bits(j, count):
    out, by = 0, 1
    while by < count:
        out = out * 2 + (j // by) % 2
        by *= 2
    return out


def traded(value, axis):
    count = lax.axis_size(axis)
    size = value.shape[-1] // count
    parts = [value[:, j * size : (j + 1) * size] for j in range(count)]
    return jnp.stack([swap(part, axis, j) if j else part for j, part in enumerate(parts)])


def exchange(value, axis):
    return lax.all_to_all(value, axis, 0, 0)


def in_order(parts, index):
    stacked = jnp.stack(parts)
    return jnp.concatenate([lax.dynamic_index_in_dim(stacked, index ^ a, 0) for a in range(len(parts))])


def assemble_kernel(ids_ref, gate_ref, *refs, share, heads):
    conv_refs, (weight_ref, out_ref, tail_ref, sum_ref) = refs[:-4], refs[-4:]
    step = pl.program_id(0)
    count, owners = gate_ref.shape[:2]
    channels = out_ref.shape[0]

    def place_of(q):
        return reversed_bits(ids_ref[0] ^ q, count)

    @pl.when(step == 0)
    def _():
        sum_ref[...] = jnp.zeros_like(sum_ref)

    def put(at, value):
        size = value.shape[0]
        out_ref[at : at + size] = value
        sum_ref[0:1] += jnp.sum(value * weight_ref[at : at + size].astype(f32), axis=0, keepdims=True)

    def parts():
        at = 0
        for ref in conv_refs:
            for q in range(count):
                yield at, ref, q
                at += ref.shape[2]

    @pl.when(step < owners)
    def _():
        rows = gate_ref.shape[2]
        for q in range(count):
            put(q * rows, gate_ref[place_of(q), ids_ref[1] ^ step].astype(f32))

    @pl.when(step // owners == 1)
    def _():
        for at, ref, q in parts():
            size = min(ref.shape[2], channels - at)
            if size > 0:
                put(at, ref[place_of(q), ids_ref[1] ^ (step % owners), :size].astype(f32))

    @pl.when(step == 2 * owners)
    def _():
        for a in range(owners):
            found = []
            for at, ref, q in parts():
                skip = max(0, channels - at)
                if skip < ref.shape[2]:
                    found.append(ref[place_of(q), ids_ref[1] ^ a].astype(f32)[skip:])
            value = jnp.concatenate(found, axis=0)
            tail_ref[a] = value
            put(a * share, value[:share])
            put(owners * share + a * heads, value[share : share + heads])


def rows_kernel(ids_ref, *refs, parts):
    bufs, (weight_ref, out_ref, sum_ref) = refs[: len(parts)], refs[len(parts) :]
    total = jnp.zeros((out_ref.shape[0], 1), f32)
    for ref, (start, size) in zip(bufs, parts, strict=True):
        value = ref[0].astype(f32)
        out_ref[:, start : start + size] = value
        total = total + jnp.sum(value * weight_ref[:, start : start + size].astype(f32), axis=1, keepdims=True)
    sum_ref[...] = total


def per_device(tokens, lengths, norm_gain, in_weight, conv_weight, conv_bias, dt_bias, decay_log, skip_gain, gated_gain, out_weight, cotangent):
    nf, nq = lax.axis_size("fsdp"), lax.axis_size("seq")
    me, place = lax.axis_index("fsdp"), lax.axis_index("seq")
    _, seg, width = tokens.shape
    rows = in_weight.shape[0]
    channels = out_weight.shape[0]
    inner = channels * nf
    heads = dt_bias.shape[0]
    conv_own = conv_weight.shape[1]
    state = (conv_own * nf - inner) // 2
    share = 2 * state // nf
    slots = nf

    ids = jnp.stack([place, me]).astype(jnp.int32)
    per_slot = nq // slots
    piece = channels // per_slot

    weight = in_weight.T
    quarter, side = channels // 4, (place % 2) * 2 + (place // 2) % 2
    got, first, last = [], [], []
    for j in range(nf):
        start = inner + (me ^ j) * channels
        if j < 2:
            give = lax.dynamic_slice_in_dim(weight, start, channels, 0)
            got.append(swap(give, "fsdp", j) if j else give)
        else:
            mine = swap(lax.dynamic_slice_in_dim(weight, start + side * quarter, quarter, 0), "fsdp", j)
            near = swap(mine, "seq", 2)
            first.append(mine)
            last.append(swap(jnp.stack([mine, near]), "seq", 1))
            got += [mine, near, last[-1]]
    x_main = all_slots(tied(tokens, first), "fsdp", last)
    before = lax.ppermute(tokens[0, seg - 3 :], "seq", [(i, i + 1) for i in range(nq - 1)])

    def padded(rows_):
        return jnp.pad(rows_, ((0, 0), (0, width - rows_.shape[1])))

    small = jnp.concatenate(
        [padded(conv_weight), padded(conv_bias[None]), padded(norm_gain[None]), jnp.zeros((7, width), bf16), before], axis=0
    )
    x_small = all_slots(tied(small[None], first), "fsdp")
    listed = [x_small[j] for j in range(nf)]
    norm_all = in_order([part[5, :rows] for part in listed], me).astype(f32).reshape(1, width)
    taps_all = in_order([part[:5, :conv_own] for part in listed], me).astype(f32)
    taps_all = taps_all.reshape(nf, 5, conv_own).transpose(1, 0, 2).reshape(5, -1)
    taps_all = jnp.pad(taps_all, ((0, 3), (0, 0)))
    taps = jnp.concatenate([lax.dynamic_slice_in_dim(taps_all, me * channels, channels, 1), taps_all[:, inner:]], axis=1)
    taps_share = lax.dynamic_slice_in_dim(taps_all, inner + me * share, share, 1)
    rate = jnp.stack([dt_bias.astype(f32), jnp.exp(decay_log.astype(f32))])
    rate = jnp.pad(rate, ((0, 6), (0, lanes - heads)))
    vec = jnp.stack([jnp.repeat(skip_gain.astype(f32), head_size), gated_gain.astype(f32)])
    vec = jnp.pad(vec, ((0, 6), (0, 0)))

    rest = all_slots(weight[2 * inner :][None], "fsdp")
    cw = channels + 2 * state
    (w_conv,) = call(
        weight_kernel,
        1,
        [(part, None) for part in got] + [(rest, None)],
        [((cw + lanes, width), bf16, None)],
        "weights",
        ids=ids,
        owners=nf,
        state=state,
        heads=heads,
    )

    (normed,) = call(
        normalize_kernel,
        slots,
        [(x_main, each), (x_small, each), (norm_all, None)],
        [((slots, halo + seg, width), bf16, each)],
        "normalize",
        ids=ids,
        owners=nf,
    )
    inputs = tokens[0].astype(f32)
    valid = (place * seg + jnp.arange(seg) < lengths[0]).astype(f32)[:, None]
    upstream = valid * cotangent[0].astype(f32)

    weight_later, later = tied((weight, upstream.astype(bf16)), last)
    gives = [lax.dynamic_slice_in_dim(weight_later, (me ^ j) * channels, channels, 0) for j in range(nf)]
    w_gate = jnp.concatenate([swap(g, "fsdp", j) if j else g for j, g in enumerate(gives)], axis=1)
    back_branch = all_slots(later[None], "fsdp")

    def project(x, w):
        return lax.dot_general(x, w, (((2,), (1,)), ((), ())), preferred_element_type=f32)

    pc = project(normed, w_conv).astype(bf16)
    main = normed[:, halo:]
    tall = 16
    statics = dict(channels=channels, state=state)
    turned = (per_slot, lambda s, *i: s)
    act, s_local, lac, dtc, lar, dtr = call(
        states_kernel,
        slots,
        [(pc, each), (taps, None), (rate, None)],
        [
            ((slots, seg, cw), bf16, each),
            ((nq, piece + 16, state), bf16, turned),
            ((slots, seg, lanes), f32, each),
            ((slots, seg, lanes), f32, each),
            ((slots, tall, seg), f32, each),
            ((slots, tall, seg), f32, each),
        ],
        "states",
        far=True,
        rows=piece,
        **statics,
    )
    (y_local,) = call(
        local_kernel,
        slots,
        [(act, each), (lac, each), (lar, each), (dtr, each)],
        [((slots, seg, channels), f32, each)],
        "local",
        flops=2 * slots * seg * seg * channels,
        **statics,
    )
    came, y_local = lax.optimization_barrier((exchange(s_local, "seq"), y_local))
    (reached,) = call(
        chain_kernel, 1, [(came, None)], [((nq, piece, state), bf16, None)], "chain", ids=ids, rows=piece, count=per_slot
    )
    s_in = exchange(reached, "seq").reshape(slots, channels, state)

    gate = project(main, w_gate).astype(bf16)
    bg = lax.dot_general(back_branch, out_weight, (((2,), (1,)), ((), ())), preferred_element_type=f32).astype(bf16)
    y, stats = call(
        finish_kernel,
        slots,
        [(y_local, each), (act, each), (lac, each), (s_in, each), (gate, each), (bg, each), (vec, None)],
        [((slots, seg, channels), f32, each), ((slots, 8, seg), f32, each)],
        "finish",
        far=True,
        **statics,
    )
    shares = [(swap(stats, "fsdp", j) if j else stats, (1, lambda s, j=j: s ^ j)) for j in range(nf)]
    gated_out, dgate, dy, pos, dsin, dskip = call(
        norm_kernel,
        slots,
        [(y, each), (act, each), (lac, each), (gate, each), (bg, each), (vec, None)] + shares,
        [
            ((slots, seg, channels), bf16, each),
            ((slots, seg, channels), bf16, each),
            ((slots, seg, channels), f32, each),
            ((slots, seg, lanes), f32, each),
            ((nq, piece, state), bf16, turned),
            ((8, channels), f32, None),
        ],
        "norm",
        far=True,
        inner=inner,
        rows=piece,
        **statics,
    )

    def grad_of(dz, x):
        return lax.dot_general(dz, x, (((0, 1), (0, 1)), ((), ())), preferred_element_type=f32).astype(bf16)

    def cut(value):
        size = value.shape[-1] // 2
        return [value] if size // nq % 8 else [value[..., :size], value[..., size:]]

    def pieces(g):
        return g.reshape((nq, g.shape[0] // nq) + g.shape[1:])

    barrier = lax.optimization_barrier
    gate_grad, out_grad = grad_of(dgate, main), grad_of(gated_out, back_branch)
    back_came = exchange(dsin, "seq")
    gate_step = halved_start(pieces(gate_grad), "seq", 1)
    out_step = halved_start(pieces(out_grad), "seq", 1)
    branch = lax.dot_general(gated_out, out_weight, (((2,), (0,)), ((), ())), preferred_element_type=f32)
    branch = to_owner(branch, "fsdp")
    (reached,) = call(
        back_chain_kernel,
        1,
        [(back_came, None), (came, None)],
        [((nq, piece, state), bf16, None)],
        "back_chain",
        ids=ids,
        rows=piece,
        count=per_slot,
    )
    g_end = exchange(reached, "seq").reshape(slots, channels, state)
    gate_sum = halved_end(gate_step, reached)
    dy_later, gate_sum = barrier((dy, gate_sum))
    gate_step = halved_start(gate_sum, "seq", 2)

    r_local, dbc = call(
        backward_kernel,
        slots,
        [(act, each), (dy_later, each), (lac, each), (lar, each), (dtr, each), (s_in, each)],
        [((slots, seg, channels), f32, each), ((slots, seg, 2 * state), f32, each)],
        "backward",
        far=True,
        flops=4 * slots * seg * seg * channels,
        **statics,
    )
    gate_sum = halved_end(gate_step, dbc)
    dbc, gate_sum = barrier((dbc, gate_sum))
    gate_step = halved_start(gate_sum, "seq", 4)
    d_shares = call(
        rows_grad_kernel,
        slots,
        [(act, each), (lac, each), (dtc, each), (g_end, each), (dbc, each)],
        [((slots, share, seg), bf16, each)] * nf,
        "rows_grad",
        ids=ids,
        scratch=[pltpu.VMEM((2 * state, seg), f32)],
        **statics,
    )
    out_sum = halved_end(out_step, d_shares[0])
    r_local, out_sum, own_share = barrier((r_local, out_sum, d_shares[0]))
    out_step = halved_start(out_sum, "seq", 2)
    d_shares = [own_share] + [swap(d, "fsdp", j) for j, d in enumerate(d_shares) if j]
    dpre, first, dstep, dtaps, drate = call(
        carry_kernel,
        slots,
        [
            (pc, each), (taps, None), (rate, None), (act, each), (dy, each), (r_local, each), (pos, each), (lac, each),
            (dtc, each), (g_end, each), (s_in, each), (s_local, turned), (vec, None),
        ],
        [
            ((slots, seg, channels), f32, each),
            ((slots, 8, channels), f32, each),
            ((slots, seg, lanes), bf16, each),
            ((8, channels), f32, None),
            ((8, lanes), f32, None),
        ],
        "carry",
        far=True,
        rows=piece,
        **statics,
    )
    dpre, gate_step, out_step, d_shares, branch = barrier((dpre, gate_step, out_step, d_shares, branch))
    gate_sum, out_sum = halved_from(halved_end(gate_step), "seq", 8), halved_end(out_step)
    pc_later, gate_sum, out_sum, d_shares = barrier((pc, gate_sum, out_sum, d_shares))
    out_step = halved_start(out_sum, "seq", 4)
    gate_sum = traded(gate_sum, "fsdp")[None]
    dpre_share, first_share, dtaps_share = call(
        share_kernel,
        slots,
        [(pc_later, each), (taps_share.T, None)]
        + [(d, (1, lambda s, i, j=j: s ^ j)) for j, d in enumerate(d_shares)],
        [((slots, seg, lanes), f32, each), ((slots, 8, lanes), f32, each), ((share, lanes), f32, None)],
        "share",
        ids=ids,
        scratch=[pltpu.VMEM((2 * state, seg), f32)],
        **statics,
    )
    first, first_share, gate_sum = barrier((first, first_share, gate_sum))
    behind = [(i, i - 1) for i in range(1, nq)]
    after = lax.ppermute(jnp.concatenate([first, first_share], axis=2), "seq", behind)
    gate_more = swap(gate_sum, "seq", nq // 2)
    after, gate_more = barrier((after, gate_more))
    gate_sum = jnp.concatenate([gate_sum, gate_more], axis=0)
    taps_back = jnp.concatenate([taps[:, :channels], jnp.pad(taps_share, ((0, 0), (0, lanes - share)))], axis=1)
    (dconv,) = call(
        returned_kernel,
        slots,
        [(dpre, each), (dpre_share, each), (after, each), (taps_back, None), (dstep, each)],
        [((slots, seg, channels + lanes), bf16, each)],
        "returned",
        share=share,
        heads=heads,
    )

    dtaps, drate, dskip, dtaps_share = tied((dtaps, drate, dskip, dtaps_share), dconv)

    per = channels // rows
    head_rows = jnp.stack([drate[0, :heads], drate[1, :heads], jnp.sum(dskip[0].reshape(heads, head_size), axis=1)])
    block = jnp.concatenate(
        [
            dtaps[:5].reshape(5 * per, rows),
            jnp.pad(dtaps_share[:, :5].T, ((0, 0), (0, rows - share))),
            jnp.pad(head_rows, ((0, 0), (0, rows - heads))),
        ],
        axis=0,
    )
    extra = block.shape[0]
    block = jnp.tile(block, (1, nf)).astype(bf16)
    conv_grads = [grad_of(part, main) for part in cut(dconv)]
    spare = channels + share + heads - sum(g.shape[0] for g in conv_grads[:-1])
    conv_grads[-1] = lax.dynamic_update_slice_in_dim(conv_grads[-1], block, spare, 0)

    out_unit = channels // nq
    conv_steps = [halved_start(pieces(g), "seq", 1) for g in conv_grads]
    out_sum = halved_from(halved_end(out_step, conv_grads), "seq", 8)[None]
    gate_sum = gather_step(gate_sum, "seq", nq // 4, out_sum)
    conv_sums = [halved_end(step, gate_sum) for step in conv_steps]
    late_conv = tied(dconv, conv_sums[0])
    out_sum = gather_step(out_sum, "seq", nq // 2, conv_sums)
    gate_bufs = [gathered(gate_sum, "seq", nq // 8)]
    conv_steps = [halved_start(g, "seq", 2) for g in conv_sums]
    conv_sums = [halved_end(step) for step in conv_steps]
    conv_steps = [halved_start(g, "seq", 4) for g in conv_sums]
    out_sum = gather_step(tied(out_sum, conv_sums), "seq", nq // 4, *[step[1] for step in conv_steps])
    conv_sums = [halved_from(halved_end(step), "seq", 8) for step in conv_steps]
    out_parts = [gathered(out_sum, "seq", nq // 8)]
    conv_sums, gate_bufs = barrier((conv_sums, gate_bufs))
    conv_sums = [traded(g, "fsdp") for g in conv_sums]
    conv_bufs = [gather_step(g[None], "seq", nq // 2) for g in conv_sums]
    tied_bufs = conv_bufs
    conv_bufs = [gather_step(g, "seq", nq // 4) for g in conv_bufs]
    conv_bufs, out_parts = barrier((conv_bufs, out_parts))
    conv_bufs = [gathered(g, "seq", nq // 8) for g in conv_bufs]
    place_of = jnp.stack([reversed_bits(place ^ q, nq) for q in range(nq)])
    if all(buf.shape[2] % 8 == 0 for buf in gate_bufs + conv_bufs):
        g_in, tail, norm_sum = call(
            assemble_kernel,
            2 * nf + 1,
            [(buf, None) for buf in gate_bufs + conv_bufs] + [(weight, (channels, lambda s, i: s))],
            [
                (weight.shape, f32, (channels, lambda s, i: s)),
                ((nf, lanes, rows), f32, None),
                ((8, rows), f32, None),
            ],
            "assemble",
            ids=ids,
            share=share,
            heads=heads,
        )
        norm_sum = norm_sum[0]
    else:
        order = me ^ jnp.arange(nf)

        def natural(bufs):
            bufs = [buf[place_of][:, order].astype(f32).transpose(1, 0, 2, 3).reshape(nf, -1, rows) for buf in bufs]
            return jnp.concatenate(bufs, axis=1)

        gate_all, conv_all = natural(gate_bufs), natural(conv_bufs)
        tail = conv_all[:, channels:]
        joined = [gate_all.reshape(inner, rows), conv_all[:, :channels].reshape(inner, rows)]
        joined += [tail[:, :share].reshape(nf * share, rows), tail[:, share : share + heads].reshape(nf * heads, rows)]
        g_in = jnp.concatenate(joined, axis=0)
        norm_sum = jnp.sum(g_in * weight.astype(f32), axis=0)
    if out_unit % 16 == 0:
        sizes = [part.shape[-1] for part in out_parts]
        g_out, gated_sum = call(
            rows_kernel,
            nq,
            [(part, (1, lambda s, i: reversed_bits(i[0] ^ s, nq))) for part in out_parts] + [(out_weight, (out_unit, lambda s, i: s))],
            [(out_weight.shape, f32, (out_unit, lambda s, i: s)), ((channels, 1), f32, (out_unit, lambda s, i: s))],
            "rows",
            ids=ids,
            parts=[(sum(sizes[:i]), size) for i, size in enumerate(sizes)],
        )
        gated_sum = gated_sum[:, 0]
    else:
        g_out = jnp.concatenate([part[place_of].astype(f32).reshape(channels, -1) for part in out_parts], axis=1)
        gated_sum = jnp.sum(g_out * out_weight.astype(f32), axis=1)

    norm_grad = norm_sum / norm_gain.astype(f32)
    gated_grad = gated_sum / gated_gain.astype(f32)

    got = tail[:, share + heads : share + heads + extra]
    tap_grads = jnp.concatenate(
        [
            got[:, : 5 * per].reshape(nf, 5, channels).transpose(1, 0, 2).reshape(5, inner),
            got[:, 5 * per : 5 * per + 5, :share].transpose(1, 0, 2).reshape(5, 2 * state),
        ],
        axis=1,
    )
    tap_grads = lax.dynamic_slice_in_dim(tap_grads, me * conv_own, conv_own, 1)
    head_grads = lax.dynamic_index_in_dim(got, me, 0, False)[5 * per + 5 :, :heads]

    mixed = (valid * (inputs + branch)).astype(bf16)

    w_share = lax.dynamic_slice_in_dim(w_conv, channels + me * share, share, 0)
    w_last = jnp.concatenate([w_share, w_conv[cw : cw + lanes - share]], axis=0)

    def back(dz, w):
        return lax.dot_general(dz, w, (((2,), (0,)), ((), ())), preferred_element_type=f32)

    bn = back(dgate, w_gate) + back(late_conv[..., :channels], w_conv[:channels]) + back(late_conv[..., channels:], w_last)
    bn = to_owner(bn, "fsdp", turn=True, first=tied_bufs)
    (input_grad,) = call(
        input_kernel,
        1,
        [(bn, None), (norm_all, None), (tokens[0], None), (cotangent[0], None), (valid, None)],
        [((seg, width), f32, None)],
        "input",
        ids=ids,
        owners=nf,
    )
    return (
        mixed[None],
        input_grad[None],
        norm_grad,
        g_in.T,
        tap_grads[:4],
        tap_grads[4],
        head_grads[0],
        head_grads[1],
        head_grads[2],
        gated_grad,
        g_out,
    )


def solution(mesh):
    whole, rows = P("fsdp", "seq", None), P("fsdp", None)
    one, columns = P("fsdp"), P(None, "fsdp")
    return jax.shard_map(
        per_device,
        mesh=mesh,
        in_specs=(whole, one, one, rows, columns, one, one, one, one, one, rows, whole),
        out_specs=(whole, whole, one, rows, columns, one, one, one, one, one, rows),
        check_vma=False,
    )
```

```python
import functools

import jax
import jax.numpy as jnp
from jax import lax
from jax.experimental import pallas as pl
from jax.experimental.pallas import tpu as pltpu
from jax.sharding import PartitionSpec as P

epsilon = 1e-05
bf16, f32 = jnp.bfloat16, jnp.float32
best = lax.Precision.HIGHEST
halo = 16
lanes = 128
head_size = 64


def dot(a, b, ca=1, cb=0, precision=None):
    return lax.dot_general(
        a, b, (((ca,), (cb,)), ((), ())), preferred_element_type=f32, precision=precision
    )


def sigmoid(v):
    return 0.5 + 0.5 * jnp.tanh(0.5 * v)


def iota(shape, axis):
    return lax.broadcasted_iota(jnp.int32, shape, axis)


def spread(columns, pair):
    first, second = 2 * pair, 2 * pair + 1
    rows = columns.shape[0]
    return jnp.where(
        iota((rows, lanes), 1) < head_size,
        columns[:, first : first + 1],
        columns[:, second : second + 1],
    )


def per_head(total, products, pair):
    rows = products.shape[0]
    lane = iota((rows, lanes), 1)
    low = jnp.sum(jnp.where(lane < head_size, products, 0.0), axis=1, keepdims=True)
    high = jnp.sum(jnp.where(lane < head_size, 0.0, products), axis=1, keepdims=True)
    return total + jnp.where(lane == 2 * pair, low, jnp.where(lane == 2 * pair + 1, high, 0.0))


def in_heads(products, pair):
    rows = jnp.sum(products, axis=1, keepdims=True)
    low, high = jnp.sum(rows[:head_size]), jnp.sum(rows[head_size:])
    lane = iota((1, lanes), 1)
    return jnp.where(lane == 2 * pair, low, jnp.where(lane == 2 * pair + 1, high, 0.0))


def convolved(pc_ref, taps_ref, at):
    x = pc_ref[0, :, at : at + lanes].astype(f32)
    tapped = [pltpu.roll(x, 3 - k, 0)[halo:] for k in range(3)] + [x[halo:]]
    pre = taps_ref[4:5, at : at + lanes]
    for k in range(4):
        pre = pre + tapped[k] * taps_ref[k : k + 1, at : at + lanes]
    return tapped, pre


def pieces_out(out_ref, whole, rows):
    for p in range(out_ref.shape[0]):
        out_ref[p, :rows] = whole[p * rows : (p + 1) * rows]


def pieces_in(ref, rows):
    return jnp.concatenate([ref[p, :rows] for p in range(ref.shape[0])], axis=0)


def block_of(index, size):
    return pl.ds(pl.multiple_of(index * size, size), size)


def columns_of(ref, index, size):
    if size % lanes == 0:
        return ref[:, block_of(index, size)]
    value = ref[:, :size]
    for a in range(1, ref.shape[1] // size):
        value = jnp.where(index == a, ref[:, a * size : (a + 1) * size], value)
    return value


def normalize_kernel(ids_ref, main_ref, small_ref, gain_ref, out_ref, *, owners):
    size = out_ref.shape[2] // owners
    for ref, at in ((small_ref, 0), (main_ref, halo)):
        x = ref[0].astype(f32)
        inv = lax.rsqrt(jnp.mean(x * x, axis=1, keepdims=True) + epsilon)
        for j in range(owners):
            own = ids_ref[1] ^ j
            part = columns_of(ref.at[0], own, size).astype(f32) * inv * columns_of(gain_ref, own, size)
            out_ref[0, at : at + x.shape[0], j * size : (j + 1) * size] = part.astype(bf16)


def weight_kernel(ids_ref, *refs, owners, state, heads):
    rest_ref, out_ref = refs[-2:]
    size = rest_ref.shape[2]
    channels = out_ref.shape[0] - 2 * state - lanes
    n = 0
    for j in range(owners):
        own = slice(j * size, (j + 1) * size)
        if j < 2:
            out_ref[:channels, own] = refs[n][...]
            n += 1
        else:
            quarter = channels // 4
            for far_side in range(2):
                for near in range(2):
                    place = ((ids_ref[0] % 2) ^ far_side) * 2 + (((ids_ref[0] // 2) % 2) ^ near)
                    ref = refs[n] if far_side == 0 else refs[n].at[near]
                    out_ref[block_of(place, quarter), own] = ref[...]
                    n += 1 - far_side
            n += 1
        out_ref[channels : channels + 2 * state, own] = rest_ref[j, : 2 * state]
        rows = owners * heads
        pick = iota((lanes, rows), 1) == ids_ref[1] * heads + iota((lanes, rows), 0)
        pick = jnp.where(iota((lanes, rows), 0) < heads, pick.astype(f32), 0.0).astype(bf16)
        out_ref[channels + 2 * state :, own] = dot(pick, rest_ref[j, 2 * state : 2 * state + rows]).astype(bf16)


def input_kernel(ids_ref, bn_ref, gain_ref, tokens_ref, cot_ref, valid_ref, out_ref, *, owners):
    x = tokens_ref[...].astype(f32)
    width = x.shape[1]
    size = width // owners
    inv = lax.rsqrt(jnp.mean(x * x, axis=1, keepdims=True) + epsilon)
    lean = jnp.zeros_like(inv)
    for a in range(owners):
        here = slice(a * size, (a + 1) * size)
        bn = columns_of(bn_ref, ids_ref[1] ^ a, size) * gain_ref[:, here]
        lean = lean + jnp.sum(bn * x[:, here], axis=1, keepdims=True)
    lean = lean * (inv * inv * inv) * (1.0 / width)
    for a in range(owners):
        here = slice(a * size, (a + 1) * size)
        bn = columns_of(bn_ref, ids_ref[1] ^ a, size) * gain_ref[:, here]
        out_ref[:, here] = valid_ref[...] * cot_ref[:, here].astype(f32) + inv * bn - x[:, here] * lean


def of_rows(row, ids_ref, rows, count):
    head = ((ids_ref[0] % count) * rows + iota((rows, lanes), 0)) // head_size
    return jnp.sum(jnp.where(iota((rows, lanes), 1) == head, row, 0.0), axis=1, keepdims=True)


def chain_kernel(ids_ref, in_ref, out_ref, *, rows, count):
    carried = jnp.zeros((rows, lanes), f32)
    for i in range(in_ref.shape[0]):
        out_ref[i] = carried.astype(bf16)
        row = in_ref[i, rows : rows + 1].astype(f32) + in_ref[i, rows + 1 : rows + 2].astype(f32)
        carried = of_rows(row, ids_ref, rows, count) * carried + in_ref[i, :rows].astype(f32)


def back_chain_kernel(ids_ref, in_ref, decay_ref, out_ref, *, rows, count):
    carried = jnp.zeros((rows, lanes), f32)
    for i in reversed(range(in_ref.shape[0])):
        out_ref[i] = carried.astype(bf16)
        row = decay_ref[i, rows : rows + 1].astype(f32) + decay_ref[i, rows + 1 : rows + 2].astype(f32)
        carried = of_rows(row, ids_ref, rows, count) * carried + in_ref[i].astype(f32)


def states_kernel(pc_ref, taps_ref, rate_ref, act_ref, s_ref, lac_ref, dtc_ref, lar_ref, dtr_ref, *, channels, state, rows):
    width = channels + 2 * state
    for at in list(range(channels, width, lanes)) + list(range(0, channels, lanes)):
        _, pre = convolved(pc_ref, taps_ref, at)
        act_ref[0, :, at : at + lanes] = (pre * sigmoid(pre)).astype(bf16)
    seg = act_ref.shape[1]
    z = pc_ref[0, halo:, width : width + lanes].astype(f32) + rate_ref[0:1]
    dtc = jnp.maximum(z, 0.0) + jnp.log1p(jnp.exp(-jnp.abs(z)))
    lower = iota((seg, seg), 0) >= iota((seg, seg), 1)
    lac = dot(lower.astype(f32), -dtc * rate_ref[1:2], precision=best)
    tall = lar_ref.shape[1]
    lac_ref[0], dtc_ref[0], lar_ref[0], dtr_ref[0] = lac, dtc, lac.T[:tall], dtc.T[:tall]
    b_rows = act_ref[0, :, channels : channels + state]
    to_end = jnp.exp(lac[seg - 1 : seg] - lac) * dtc
    states = []
    for pair in range(channels // lanes):
        at = pair * lanes
        weighted = (spread(to_end, pair) * act_ref[0, :, at : at + lanes].astype(f32)).astype(bf16)
        states.append(dot(weighted, b_rows, 0, 0).astype(bf16))
    pieces_out(s_ref, jnp.concatenate(states, axis=0), rows)
    whole = jnp.exp(lac[seg - 1 : seg])
    high = whole.astype(bf16).astype(f32)
    row = iota((16, lanes), 0)
    tail = jnp.where(row == 0, high, jnp.where(row == 1, whole - high, 0.0)).astype(bf16)
    for p in range(s_ref.shape[0]):
        s_ref[p, rows:] = tail


def local_kernel(act_ref, lac_ref, lar_ref, dtr_ref, y_ref, *, channels, state):
    seg = act_ref.shape[1]
    lower = iota((seg, seg), 0) >= iota((seg, seg), 1)
    lac, lar, dtr = lac_ref[0], lar_ref[0], dtr_ref[0]
    both = dot(act_ref[0, :, channels + state :], act_ref[0, :, channels : channels + state], 1, 1)
    for pair in range(channels // lanes):
        at = pair * lanes
        values = act_ref[0, :, at : at + lanes]
        parts = []
        for side in range(2):
            h = 2 * pair + side
            mix = jnp.where(lower, jnp.exp(lac[:, h : h + 1] - lar[h : h + 1]), 0.0) * both * dtr[h : h + 1]
            parts.append(dot(mix.astype(bf16), values[:, side * head_size : (side + 1) * head_size]))
        y_ref[0, :, at : at + lanes] = jnp.concatenate(parts, axis=1)


def finish_kernel(y_ref, act_ref, lac_ref, sin_ref, gate_ref, bg_ref, vec_ref, y_out, stat_ref, *, channels, state):
    seg = y_ref.shape[1]
    c_rows = act_ref[0, :, channels + state : channels + 2 * state]
    decay = jnp.exp(lac_ref[0])
    first = jnp.zeros((seg, 1), f32)
    second = jnp.zeros((seg, 1), f32)
    for pair in range(channels // lanes):
        at = pair * lanes
        here = slice(at, at + lanes)
        carried = dot(c_rows, sin_ref[0, here], 1, 1)
        y = y_ref[0, :, here] + spread(decay, pair) * carried
        y_out[0, :, here] = y
        gate = gate_ref[0, :, here].astype(f32)
        heads = y + vec_ref[0:1, here] * act_ref[0, :, here].astype(f32)
        gated = heads * gate * sigmoid(gate)
        first = first + jnp.sum(gated * gated, axis=1, keepdims=True)
        second = second + jnp.sum(gated * bg_ref[0, :, here].astype(f32) * vec_ref[1:2, here], axis=1, keepdims=True)
    lane = iota((seg, lanes), 1)
    both = jnp.where(lane == 0, first, jnp.where(lane == 1, second, 0.0))
    stat_ref[0] = both.T[:8]


def norm_kernel(y_ref, act_ref, lac_ref, gate_ref, bg_ref, vec_ref, *refs, channels, state, inner, rows):
    stat_refs, (out_ref, dgate_ref, dy_ref, pos_ref, dsin_ref, dskip_ref) = refs[:-6], refs[-6:]
    seg = y_ref.shape[1]
    stats = sum(ref[0] for ref in stat_refs).T
    states = []
    inv = lax.rsqrt(stats[:, 0:1] * (1.0 / inner) + epsilon)
    lean = inv * inv * inv * (stats[:, 1:2] * (1.0 / inner))
    c_rows = act_ref[0, :, channels + state : channels + 2 * state]
    decay = jnp.exp(lac_ref[0])
    pos = jnp.zeros((seg, lanes), f32)

    @pl.when(pl.program_id(0) == 0)
    def _():
        dskip_ref[...] = jnp.zeros_like(dskip_ref)

    for pair in range(channels // lanes):
        at = pair * lanes
        here = slice(at, at + lanes)
        y = y_ref[0, :, here]
        values = act_ref[0, :, here].astype(f32)
        heads = y + vec_ref[0:1, here] * values
        gate = gate_ref[0, :, here].astype(f32)
        sg = sigmoid(gate)
        gated = heads * gate * sg
        gain = vec_ref[1:2, here]
        out_ref[0, :, here] = (gated * inv * gain).astype(bf16)
        dgated = inv * (bg_ref[0, :, here].astype(f32) * gain) - gated * lean
        dgate_ref[0, :, here] = (dgated * heads * (sg * (1.0 + gate * (1.0 - sg)))).astype(bf16)
        dy = dgated * gate * sg
        dy_ref[0, :, here] = dy.astype(bf16)
        pos = per_head(pos, dy * y, pair)
        states.append(dot((spread(decay, pair) * dy).astype(bf16), c_rows, 0, 0).astype(bf16))
        dskip_ref[0:1, here] += jnp.sum(dy * values, axis=0, keepdims=True)
    pos_ref[0] = pos
    pieces_out(dsin_ref, jnp.concatenate(states, axis=0), rows)


def backward_kernel(act_ref, dy_ref, lac_ref, lar_ref, dtr_ref, sin_ref, r_ref, dbc_ref, *, channels, state):
    seg = dy_ref.shape[1]
    b_rows = act_ref[0, :, channels : channels + state]
    c_rows = act_ref[0, :, channels + state : channels + 2 * state]
    both = dot(c_rows, b_rows, 1, 1)
    lower = iota((seg, seg), 0) >= iota((seg, seg), 1)
    lac, lar, dtr = lac_ref[0], lar_ref[0], dtr_ref[0]
    decay = jnp.exp(lac)
    dboth = jnp.zeros((seg, seg), f32)
    dc = jnp.zeros((seg, state), f32)
    for pair in range(channels // lanes):
        at = pair * lanes
        here = slice(at, at + lanes)
        values = act_ref[0, :, here]
        dy = dy_ref[0, :, here]
        dyl = dy
        parts = []
        for side in range(2):
            h = 2 * pair + side
            own = slice(side * head_size, (side + 1) * head_size)
            weights = jnp.where(lower, jnp.exp(lac[:, h : h + 1] - lar[h : h + 1]), 0.0)
            parts.append(dot((weights * both).astype(bf16), dyl[:, own], 0, 0))
            dboth = dboth + dot(dyl[:, own], values[:, own], 1, 1) * (weights * dtr[h : h + 1])
        r_ref[0, :, here] = jnp.concatenate(parts, axis=1).astype(bf16)
        dc = dc + dot((spread(decay, pair) * dy.astype(f32)).astype(bf16), sin_ref[0, here])
    dlow = dboth.astype(bf16)
    dbc_ref[0, :, :state] = dot(dlow, c_rows, 0, 0)
    dbc_ref[0, :, state:] = dc + dot(dlow, b_rows)


def rows_grad_kernel(ids_ref, act_ref, lac_ref, dtc_ref, g_ref, dbc_ref, *refs, channels, state):
    out_refs, hold = refs[:-1], refs[-1]
    seg = act_ref.shape[1]
    lac, dtc = lac_ref[0], dtc_ref[0]
    weights = jnp.exp(lac[seg - 1 : seg] - lac) * dtc
    db = dbc_ref[0, :, :state]
    for pair in range(channels // lanes):
        here = slice(pair * lanes, (pair + 1) * lanes)
        db = db + dot((spread(weights, pair) * act_ref[0, :, here].astype(f32)).astype(bf16), g_ref[0, here])
    hold[:state] = db.T
    hold[state:] = dbc_ref[0, :, state:].T
    share = out_refs[0].shape[1]
    for j, out_ref in enumerate(out_refs):
        out_ref[0] = hold[block_of(ids_ref[1] ^ j, share)].astype(bf16)


def share_kernel(ids_ref, pc_ref, taps_ref, *refs, channels, state):
    parts, (dpre_ref, first_ref, dtaps_ref, hold) = refs[:-4], refs[-4:]
    seg = pc_ref.shape[1] - halo
    share = parts[0].shape[1]
    own = block_of(ids_ref[1], share)
    hold[...] = pc_ref[0, :, channels : channels + 2 * state].astype(f32)[halo:].T
    x = hold[own]
    hold[:, :halo] = pc_ref[0, :halo, channels : channels + 2 * state].astype(f32).T
    edge = hold[own, :halo]
    lane = iota((share, seg), 1)
    tapped = []
    for k in range(3):
        value = pltpu.roll(x, 3 - k, 1)
        for t in range(3 - k):
            value = jnp.where(lane == t, edge[:, halo - 3 + k + t : halo - 2 + k + t], value)
        tapped.append(value)
    tapped.append(x)
    pre = taps_ref[:, 4:5] + sum(tapped[k] * taps_ref[:, k : k + 1] for k in range(4))
    sg = sigmoid(pre)
    dpre = sum(ref[0].astype(f32) for ref in parts) * (sg * (1.0 + pre * (1.0 - sg)))

    @pl.when(pl.program_id(0) == 0)
    def _():
        dtaps_ref[...] = jnp.zeros_like(dtaps_ref)

    lane = iota((share, lanes), 1)
    total = jnp.zeros((share, lanes), f32)
    for k in range(5):
        column = jnp.sum(dpre * tapped[k] if k < 4 else dpre, axis=1, keepdims=True)
        total = jnp.where(lane == k, column, total)
    dtaps_ref[...] += total
    rows = jnp.concatenate([dpre, jnp.zeros((lanes - share, seg), f32)], axis=0).T
    dpre_ref[0] = rows
    first_ref[0] = rows[:8]


def carry_kernel(pc_ref, taps_ref, rate_ref, act_ref, dy_ref, r_ref, pos_ref, lac_ref, dtc_ref, g_ref, sin_ref, s_ref, vec_ref, dpre_ref, first_ref, dstep_ref, dtaps_ref, drate_ref, *, channels, state, rows):
    seg = dy_ref.shape[1]
    width = channels + 2 * state
    b_rows = act_ref[0, :, channels : channels + state]
    lac, dtc = lac_ref[0], dtc_ref[0]
    last = lac[seg - 1 : seg]
    to_last = jnp.exp(last - lac)
    neg = jnp.zeros((seg, lanes), f32)
    through = jnp.zeros((1, lanes), f32)
    local = jnp.zeros((1, lanes), f32)
    states = pieces_in(s_ref, rows)

    @pl.when(pl.program_id(0) == 0)
    def _():
        dtaps_ref[...] = jnp.zeros_like(dtaps_ref)
        drate_ref[...] = jnp.zeros_like(drate_ref)

    for pair in range(channels // lanes):
        at = pair * lanes
        here = slice(at, at + lanes)
        grad = g_ref[0, here]
        values = act_ref[0, :, here].astype(f32)
        r = r_ref[0, :, here].astype(f32) + spread(to_last, pair) * dot(b_rows, grad, 1, 1)
        neg = per_head(neg, values * r, pair)
        wide = grad.astype(f32)
        through = through + in_heads(wide * sin_ref[0, here].astype(f32), pair)
        local = local + in_heads(wide * states[here].astype(f32), pair)
        tapped, pre = convolved(pc_ref, taps_ref, at)
        sg = sigmoid(pre)
        dpre = (spread(dtc, pair) * r + vec_ref[0:1, here] * dy_ref[0, :, here].astype(f32)) * (sg * (1.0 + pre * (1.0 - sg)))
        dpre_ref[0, :, here] = dpre.astype(bf16)
        first_ref[0, :, here] = dpre[:8]
        for k in range(4):
            dtaps_ref[k : k + 1, here] += jnp.sum(dpre * tapped[k], axis=0, keepdims=True)
        dtaps_ref[4:5, here] += jnp.sum(dpre, axis=0, keepdims=True)
    seed = jnp.exp(last) * through + local
    upper = (iota((seg, seg), 0) <= iota((seg, seg), 1)).astype(f32)
    q = dot(upper, pos_ref[0] - dtc * neg, precision=best) + seed
    rates = rate_ref[1:2]
    z = pc_ref[0, halo:, width : width + lanes].astype(f32) + rate_ref[0:1]
    draw = (neg - rates * q) * sigmoid(z)
    dstep_ref[0] = draw.astype(bf16)
    drate_ref[0:1] += jnp.sum(draw, axis=0, keepdims=True)
    drate_ref[1:2] += jnp.sum(q * (-dtc * rates), axis=0, keepdims=True)


def returned_kernel(dpre_ref, dshare_ref, next_ref, taps_ref, dstep_ref, out_ref, *, share, heads):
    seg, width = dpre_ref.shape[1:]
    for at in range(0, width + lanes, lanes):
        here = slice(at, at + lanes)
        own = dpre_ref[0, :, here].astype(f32) if at < width else dshare_ref[0]
        x = jnp.concatenate([own, next_ref[0, :, here]], axis=0)
        total = x[:seg] * taps_ref[3:4, here]
        for k in range(3):
            by = 3 - k
            total = total + pltpu.roll(x, seg + 8 - by, 0)[:seg] * taps_ref[k : k + 1, here]
        if at == width:
            step = pltpu.roll(dstep_ref[0].astype(f32), share, 1)
            lane = iota((seg, lanes), 1)
            total = jnp.where(lane < share, total, jnp.where(lane < share + heads, step, 0.0))
        out_ref[0, :, here] = total.astype(bf16)


def call(kernel, grid, ins, outs, name, ids=None, flops=0, scratch=(), far=False, **statics):
    def spec(shape, index):
        if index is None:
            return pl.BlockSpec(tuple(shape), lambda s, *i: (0,) * len(shape))
        block, at = index
        return pl.BlockSpec((block,) + tuple(shape[1:]), lambda s, *i: (at(s, *i),) + (0,) * (len(shape) - 1))

    moved = sum(a.size * a.dtype.itemsize for a, _ in ins)
    for shape, dtype, _ in outs:
        size = 1
        for d in shape:
            size *= d
        moved += size * jnp.dtype(dtype).itemsize
    return pl.pallas_call(
        functools.partial(kernel, **statics),
        grid_spec=pltpu.PrefetchScalarGridSpec(
            num_scalar_prefetch=0 if ids is None else 1,
            grid=(grid,),
            in_specs=[spec(a.shape, index) for a, index in ins],
            out_specs=[spec(shape, index) for shape, _, index in outs],
            scratch_shapes=list(scratch),
        ),
        out_shape=[(pltpu.HBM if far else jax.ShapeDtypeStruct)(shape, dtype) for shape, dtype, _ in outs],
        compiler_params=pltpu.CompilerParams(vmem_limit_bytes=16 << 20),
        cost_estimate=pl.CostEstimate(flops=flops, bytes_accessed=moved, transcendentals=0),
        name=name,
    )(*([] if ids is None else [ids]), *[pltpu.with_memory_space_constraint(a, pltpu.HBM) if far else a for a, _ in ins])


each = (1, lambda s, *i: s)


def swap(value, axis, by):
    count = lax.axis_size(axis)
    return lax.ppermute(value, axis, [(i, i ^ by) for i in range(count)])


def all_slots(value, axis, first=None):
    count = lax.axis_size(axis)
    by = count // 2
    offsets = [0]
    while by:
        value = jnp.concatenate([value, swap(value, axis, by)], axis=0)
        if first is not None:
            value, first = tied(value, first), None
        offsets += [j ^ by for j in offsets]
        by //= 2
    size = value.shape[0] // count
    where = [offsets.index(j) for j in range(count)]
    return jnp.concatenate([value[i * size : (i + 1) * size] for i in where], axis=0)


def blocks_turned(value, by, owners):
    size = value.shape[-1] // owners
    return jnp.concatenate([value[..., (j ^ by) * size : ((j ^ by) + 1) * size] for j in range(owners)], axis=-1)


def to_owner(value, axis, turn=False, first=None):
    count = lax.axis_size(axis)
    by = 1
    while by < count:
        value = value.reshape((value.shape[0] // 2, 2) + value.shape[1:])
        other = swap(value[:, 1].astype(bf16), axis, by).astype(f32)
        value = value[:, 0] + (blocks_turned(other, by, count) if turn else other)
        if first is not None:
            value, first = tied(value, first), None
        by *= 2
    return value[0]


def halved_start(value, axis, by):
    value = value.reshape((value.shape[0] // 2, 2) + value.shape[1:])
    bit = (lax.axis_index(axis) // by) % 2
    keep = lax.dynamic_index_in_dim(value, bit, 1, False)
    give = lax.dynamic_index_in_dim(value, 1 - bit, 1, False)
    return keep, swap(give, axis, by)


def halved_end(pair, *others):
    keep, came = tied(pair, others) if others else pair
    return (keep.astype(f32) + came.astype(f32)).astype(bf16)


def halved_from(value, axis, by):
    while value.shape[0] > 1:
        value = halved_end(halved_start(value, axis, by))
        by *= 2
    return value[0]


def tied(value, *others):
    return lax.optimization_barrier((value, others))[0]


def gather_step(value, axis, by, *others):
    came = swap(value, axis, by)
    return jnp.concatenate([value, tied(came, others) if others else came], axis=0)


def gathered(value, axis, by):
    while by:
        value = gather_step(value, axis, by)
        by //= 2
    return value


def reversed_bits(j, count):
    out, by = 0, 1
    while by < count:
        out = out * 2 + (j // by) % 2
        by *= 2
    return out


def traded(value, axis):
    count = lax.axis_size(axis)
    size = value.shape[-1] // count
    parts = [value[:, j * size : (j + 1) * size] for j in range(count)]
    return jnp.stack([swap(part, axis, j) if j else part for j, part in enumerate(parts)])


def exchange(value, axis):
    return lax.all_to_all(value, axis, 0, 0)


def in_order(parts, index):
    stacked = jnp.stack(parts)
    return jnp.concatenate([lax.dynamic_index_in_dim(stacked, index ^ a, 0) for a in range(len(parts))])


def assemble_kernel(ids_ref, gate_ref, *refs, share, heads):
    conv_refs, (weight_ref, out_ref, tail_ref, sum_ref) = refs[:-4], refs[-4:]
    step = pl.program_id(0)
    count, owners = gate_ref.shape[:2]
    channels = out_ref.shape[0]

    def place_of(q):
        return reversed_bits(ids_ref[0] ^ q, count)

    @pl.when(step == 0)
    def _():
        sum_ref[...] = jnp.zeros_like(sum_ref)

    def put(at, value):
        size = value.shape[0]
        out_ref[at : at + size] = value
        sum_ref[0:1] += jnp.sum(value * weight_ref[at : at + size].astype(f32), axis=0, keepdims=True)

    def parts():
        at = 0
        for ref in conv_refs:
            for q in range(count):
                yield at, ref, q
                at += ref.shape[2]

    @pl.when(step < owners)
    def _():
        rows = gate_ref.shape[2]
        for q in range(count):
            put(q * rows, gate_ref[place_of(q), ids_ref[1] ^ step].astype(f32))

    @pl.when(step // owners == 1)
    def _():
        for at, ref, q in parts():
            size = min(ref.shape[2], channels - at)
            if size > 0:
                put(at, ref[place_of(q), ids_ref[1] ^ (step % owners), :size].astype(f32))

    @pl.when(step == 2 * owners)
    def _():
        for a in range(owners):
            found = []
            for at, ref, q in parts():
                skip = max(0, channels - at)
                if skip < ref.shape[2]:
                    found.append(ref[place_of(q), ids_ref[1] ^ a].astype(f32)[skip:])
            value = jnp.concatenate(found, axis=0)
            tail_ref[a] = value
            put(a * share, value[:share])
            put(owners * share + a * heads, value[share : share + heads])


def rows_kernel(ids_ref, *refs, parts):
    bufs, (weight_ref, out_ref, sum_ref) = refs[: len(parts)], refs[len(parts) :]
    total = jnp.zeros((out_ref.shape[0], 1), f32)
    for ref, (start, size) in zip(bufs, parts, strict=True):
        value = ref[0].astype(f32)
        out_ref[:, start : start + size] = value
        total = total + jnp.sum(value * weight_ref[:, start : start + size].astype(f32), axis=1, keepdims=True)
    sum_ref[...] = total


def per_device(tokens, lengths, norm_gain, in_weight, conv_weight, conv_bias, dt_bias, decay_log, skip_gain, gated_gain, out_weight, cotangent):
    nf, nq = lax.axis_size("fsdp"), lax.axis_size("seq")
    me, place = lax.axis_index("fsdp"), lax.axis_index("seq")
    _, seg, width = tokens.shape
    rows = in_weight.shape[0]
    channels = out_weight.shape[0]
    inner = channels * nf
    heads = dt_bias.shape[0]
    conv_own = conv_weight.shape[1]
    state = (conv_own * nf - inner) // 2
    share = 2 * state // nf
    slots = nf

    ids = jnp.stack([place, me]).astype(jnp.int32)
    per_slot = nq // slots
    piece = channels // per_slot

    weight = in_weight.T
    quarter, side = channels // 4, (place % 2) * 2 + (place // 2) % 2
    got, first, last = [], [], []
    for j in range(nf):
        start = inner + (me ^ j) * channels
        if j < 2:
            give = lax.dynamic_slice_in_dim(weight, start, channels, 0)
            got.append(swap(give, "fsdp", j) if j else give)
        else:
            mine = swap(lax.dynamic_slice_in_dim(weight, start + side * quarter, quarter, 0), "fsdp", j)
            near = swap(mine, "seq", 2)
            first.append(mine)
            last.append(swap(jnp.stack([mine, near]), "seq", 1))
            got += [mine, near, last[-1]]
    x_main = all_slots(tied(tokens, first), "fsdp", last)
    before = lax.ppermute(tokens[0, seg - 3 :], "seq", [(i, i + 1) for i in range(nq - 1)])

    def padded(rows_):
        return jnp.pad(rows_, ((0, 0), (0, width - rows_.shape[1])))

    small = jnp.concatenate(
        [padded(conv_weight), padded(conv_bias[None]), padded(norm_gain[None]), jnp.zeros((7, width), bf16), before], axis=0
    )
    x_small = all_slots(tied(small[None], first), "fsdp")
    listed = [x_small[j] for j in range(nf)]
    norm_all = in_order([part[5, :rows] for part in listed], me).astype(f32).reshape(1, width)
    taps_all = in_order([part[:5, :conv_own] for part in listed], me).astype(f32)
    taps_all = taps_all.reshape(nf, 5, conv_own).transpose(1, 0, 2).reshape(5, -1)
    taps_all = jnp.pad(taps_all, ((0, 3), (0, 0)))
    taps = jnp.concatenate([lax.dynamic_slice_in_dim(taps_all, me * channels, channels, 1), taps_all[:, inner:]], axis=1)
    taps_share = lax.dynamic_slice_in_dim(taps_all, inner + me * share, share, 1)
    rate = jnp.stack([dt_bias.astype(f32), jnp.exp(decay_log.astype(f32))])
    rate = jnp.pad(rate, ((0, 6), (0, lanes - heads)))
    vec = jnp.stack([jnp.repeat(skip_gain.astype(f32), head_size), gated_gain.astype(f32)])
    vec = jnp.pad(vec, ((0, 6), (0, 0)))

    rest = all_slots(weight[2 * inner :][None], "fsdp")
    cw = channels + 2 * state
    (w_conv,) = call(
        weight_kernel,
        1,
        [(part, None) for part in got] + [(rest, None)],
        [((cw + lanes, width), bf16, None)],
        "weights",
        ids=ids,
        owners=nf,
        state=state,
        heads=heads,
    )

    (normed,) = call(
        normalize_kernel,
        slots,
        [(x_main, each), (x_small, each), (norm_all, None)],
        [((slots, halo + seg, width), bf16, each)],
        "normalize",
        ids=ids,
        owners=nf,
    )
    inputs = tokens[0].astype(f32)
    valid = (place * seg + jnp.arange(seg) < lengths[0]).astype(f32)[:, None]
    upstream = valid * cotangent[0].astype(f32)

    weight_later, later = tied((weight, upstream.astype(bf16)), last)
    gives = [lax.dynamic_slice_in_dim(weight_later, (me ^ j) * channels, channels, 0) for j in range(nf)]
    w_gate = jnp.concatenate([swap(g, "fsdp", j) if j else g for j, g in enumerate(gives)], axis=1)
    back_branch = all_slots(later[None], "fsdp")

    def project(x, w):
        return lax.dot_general(x, w, (((2,), (1,)), ((), ())), preferred_element_type=f32)

    pc = project(normed, w_conv).astype(bf16)
    main = normed[:, halo:]
    tall = 16
    statics = dict(channels=channels, state=state)
    turned = (per_slot, lambda s, *i: s)
    act, s_local, lac, dtc, lar, dtr = call(
        states_kernel,
        slots,
        [(pc, each), (taps, None), (rate, None)],
        [
            ((slots, seg, cw), bf16, each),
            ((nq, piece + 16, state), bf16, turned),
            ((slots, seg, lanes), f32, each),
            ((slots, seg, lanes), f32, each),
            ((slots, tall, seg), f32, each),
            ((slots, tall, seg), f32, each),
        ],
        "states",
        far=True,
        rows=piece,
        **statics,
    )
    (y_local,) = call(
        local_kernel,
        slots,
        [(act, each), (lac, each), (lar, each), (dtr, each)],
        [((slots, seg, channels), f32, each)],
        "local",
        flops=2 * slots * seg * seg * channels,
        **statics,
    )
    came, y_local = lax.optimization_barrier((exchange(s_local, "seq"), y_local))
    (reached,) = call(
        chain_kernel, 1, [(came, None)], [((nq, piece, state), bf16, None)], "chain", ids=ids, rows=piece, count=per_slot
    )
    s_in = exchange(reached, "seq").reshape(slots, channels, state)

    gate = project(main, w_gate).astype(bf16)
    bg = lax.dot_general(back_branch, out_weight, (((2,), (1,)), ((), ())), preferred_element_type=f32).astype(bf16)
    y, stats = call(
        finish_kernel,
        slots,
        [(y_local, each), (act, each), (lac, each), (s_in, each), (gate, each), (bg, each), (vec, None)],
        [((slots, seg, channels), f32, each), ((slots, 8, seg), f32, each)],
        "finish",
        far=True,
        **statics,
    )
    shares = [(swap(stats, "fsdp", j) if j else stats, (1, lambda s, j=j: s ^ j)) for j in range(nf)]
    gated_out, dgate, dy, pos, dsin, dskip = call(
        norm_kernel,
        slots,
        [(y, each), (act, each), (lac, each), (gate, each), (bg, each), (vec, None)] + shares,
        [
            ((slots, seg, channels), bf16, each),
            ((slots, seg, channels), bf16, each),
            ((slots, seg, channels), bf16, each),
            ((slots, seg, lanes), f32, each),
            ((nq, piece, state), bf16, turned),
            ((8, channels), f32, None),
        ],
        "norm",
        far=True,
        inner=inner,
        rows=piece,
        **statics,
    )

    def grad_of(dz, x):
        return lax.dot_general(dz, x, (((0, 1), (0, 1)), ((), ())), preferred_element_type=f32).astype(bf16)

    def cut(value):
        size = value.shape[-1] // 2
        return [value] if size // nq % 8 else [value[..., :size], value[..., size:]]

    def pieces(g):
        return g.reshape((nq, g.shape[0] // nq) + g.shape[1:])

    barrier = lax.optimization_barrier
    gate_grad, out_grad = grad_of(dgate, main), grad_of(gated_out, back_branch)
    back_came = exchange(dsin, "seq")
    gate_step = halved_start(pieces(gate_grad), "seq", 1)
    out_step = halved_start(pieces(out_grad), "seq", 1)
    branch = lax.dot_general(gated_out, out_weight, (((2,), (0,)), ((), ())), preferred_element_type=f32)
    branch = to_owner(branch, "fsdp")
    (reached,) = call(
        back_chain_kernel,
        1,
        [(back_came, None), (came, None)],
        [((nq, piece, state), bf16, None)],
        "back_chain",
        ids=ids,
        rows=piece,
        count=per_slot,
    )
    g_end = exchange(reached, "seq").reshape(slots, channels, state)
    gate_sum = halved_end(gate_step, reached)
    dy_later, gate_sum = barrier((dy, gate_sum))
    gate_step = halved_start(gate_sum, "seq", 2)

    r_local, dbc = call(
        backward_kernel,
        slots,
        [(act, each), (dy_later, each), (lac, each), (lar, each), (dtr, each), (s_in, each)],
        [((slots, seg, channels), bf16, each), ((slots, seg, 2 * state), f32, each)],
        "backward",
        far=True,
        flops=4 * slots * seg * seg * channels,
        **statics,
    )
    gate_sum = halved_end(gate_step, dbc)
    dbc, gate_sum = barrier((dbc, gate_sum))
    gate_step = halved_start(gate_sum, "seq", 4)
    d_shares = call(
        rows_grad_kernel,
        slots,
        [(act, each), (lac, each), (dtc, each), (g_end, each), (dbc, each)],
        [((slots, share, seg), bf16, each)] * nf,
        "rows_grad",
        ids=ids,
        scratch=[pltpu.VMEM((2 * state, seg), f32)],
        **statics,
    )
    out_sum = halved_end(out_step, d_shares[0])
    r_local, out_sum, own_share = barrier((r_local, out_sum, d_shares[0]))
    out_step = halved_start(out_sum, "seq", 2)
    d_shares = [own_share] + [swap(d, "fsdp", j) for j, d in enumerate(d_shares) if j]
    dpre, first, dstep, dtaps, drate = call(
        carry_kernel,
        slots,
        [
            (pc, each), (taps, None), (rate, None), (act, each), (dy, each), (r_local, each), (pos, each), (lac, each),
            (dtc, each), (g_end, each), (s_in, each), (s_local, turned), (vec, None),
        ],
        [
            ((slots, seg, channels), bf16, each),
            ((slots, 8, channels), f32, each),
            ((slots, seg, lanes), bf16, each),
            ((8, channels), f32, None),
            ((8, lanes), f32, None),
        ],
        "carry",
        far=True,
        rows=piece,
        **statics,
    )
    dpre, gate_step, out_step, d_shares, branch = barrier((dpre, gate_step, out_step, d_shares, branch))
    gate_sum, out_sum = halved_from(halved_end(gate_step), "seq", 8), halved_end(out_step)
    pc_later, gate_sum, out_sum, d_shares = barrier((pc, gate_sum, out_sum, d_shares))
    out_step = halved_start(out_sum, "seq", 4)
    gate_sum = traded(gate_sum, "fsdp")[None]
    dpre_share, first_share, dtaps_share = call(
        share_kernel,
        slots,
        [(pc_later, each), (taps_share.T, None)]
        + [(d, (1, lambda s, i, j=j: s ^ j)) for j, d in enumerate(d_shares)],
        [((slots, seg, lanes), f32, each), ((slots, 8, lanes), f32, each), ((share, lanes), f32, None)],
        "share",
        ids=ids,
        scratch=[pltpu.VMEM((2 * state, seg), f32)],
        **statics,
    )
    first, first_share, gate_sum = barrier((first, first_share, gate_sum))
    behind = [(i, i - 1) for i in range(1, nq)]
    after = lax.ppermute(jnp.concatenate([first, first_share], axis=2), "seq", behind)
    gate_more = swap(gate_sum, "seq", nq // 2)
    after, gate_more = barrier((after, gate_more))
    gate_sum = jnp.concatenate([gate_sum, gate_more], axis=0)
    taps_back = jnp.concatenate([taps[:, :channels], jnp.pad(taps_share, ((0, 0), (0, lanes - share)))], axis=1)
    (dconv,) = call(
        returned_kernel,
        slots,
        [(dpre, each), (dpre_share, each), (after, each), (taps_back, None), (dstep, each)],
        [((slots, seg, channels + lanes), bf16, each)],
        "returned",
        share=share,
        heads=heads,
    )

    dtaps, drate, dskip, dtaps_share = tied((dtaps, drate, dskip, dtaps_share), dconv)

    per = channels // rows
    head_rows = jnp.stack([drate[0, :heads], drate[1, :heads], jnp.sum(dskip[0].reshape(heads, head_size), axis=1)])
    block = jnp.concatenate(
        [
            dtaps[:5].reshape(5 * per, rows),
            jnp.pad(dtaps_share[:, :5].T, ((0, 0), (0, rows - share))),
            jnp.pad(head_rows, ((0, 0), (0, rows - heads))),
        ],
        axis=0,
    )
    extra = block.shape[0]
    block = jnp.tile(block, (1, nf)).astype(bf16)
    conv_grads = [grad_of(part, main) for part in cut(dconv)]
    spare = channels + share + heads - sum(g.shape[0] for g in conv_grads[:-1])
    conv_grads[-1] = lax.dynamic_update_slice_in_dim(conv_grads[-1], block, spare, 0)

    out_unit = channels // nq
    conv_steps = [halved_start(pieces(g), "seq", 1) for g in conv_grads]
    out_sum = halved_from(halved_end(out_step, conv_grads), "seq", 8)[None]
    gate_sum = gather_step(gate_sum, "seq", nq // 4, out_sum)
    conv_sums = [halved_end(step, gate_sum) for step in conv_steps]
    late_conv = tied(dconv, conv_sums[0])
    out_sum = gather_step(out_sum, "seq", nq // 2, conv_sums)
    gate_bufs = [gathered(gate_sum, "seq", nq // 8)]
    conv_steps = [halved_start(g, "seq", 2) for g in conv_sums]
    conv_sums = [halved_end(step) for step in conv_steps]
    conv_steps = [halved_start(g, "seq", 4) for g in conv_sums]
    out_sum = gather_step(tied(out_sum, conv_sums), "seq", nq // 4, *[step[1] for step in conv_steps])
    conv_sums = [halved_from(halved_end(step), "seq", 8) for step in conv_steps]
    out_parts = [gathered(out_sum, "seq", nq // 8)]
    conv_sums, gate_bufs = barrier((conv_sums, gate_bufs))
    conv_sums = [traded(g, "fsdp") for g in conv_sums]
    conv_bufs = [gather_step(g[None], "seq", nq // 2) for g in conv_sums]
    tied_bufs = conv_bufs
    conv_bufs = [gather_step(g, "seq", nq // 4) for g in conv_bufs]
    conv_bufs, out_parts = barrier((conv_bufs, out_parts))
    conv_bufs = [gathered(g, "seq", nq // 8) for g in conv_bufs]
    place_of = jnp.stack([reversed_bits(place ^ q, nq) for q in range(nq)])
    if all(buf.shape[2] % 8 == 0 for buf in gate_bufs + conv_bufs):
        g_in, tail, norm_sum = call(
            assemble_kernel,
            2 * nf + 1,
            [(buf, None) for buf in gate_bufs + conv_bufs] + [(weight, (channels, lambda s, i: s))],
            [
                (weight.shape, f32, (channels, lambda s, i: s)),
                ((nf, lanes, rows), f32, None),
                ((8, rows), f32, None),
            ],
            "assemble",
            ids=ids,
            share=share,
            heads=heads,
        )
        norm_sum = norm_sum[0]
    else:
        order = me ^ jnp.arange(nf)

        def natural(bufs):
            bufs = [buf[place_of][:, order].astype(f32).transpose(1, 0, 2, 3).reshape(nf, -1, rows) for buf in bufs]
            return jnp.concatenate(bufs, axis=1)

        gate_all, conv_all = natural(gate_bufs), natural(conv_bufs)
        tail = conv_all[:, channels:]
        joined = [gate_all.reshape(inner, rows), conv_all[:, :channels].reshape(inner, rows)]
        joined += [tail[:, :share].reshape(nf * share, rows), tail[:, share : share + heads].reshape(nf * heads, rows)]
        g_in = jnp.concatenate(joined, axis=0)
        norm_sum = jnp.sum(g_in * weight.astype(f32), axis=0)
    if out_unit % 16 == 0:
        sizes = [part.shape[-1] for part in out_parts]
        g_out, gated_sum = call(
            rows_kernel,
            nq,
            [(part, (1, lambda s, i: reversed_bits(i[0] ^ s, nq))) for part in out_parts] + [(out_weight, (out_unit, lambda s, i: s))],
            [(out_weight.shape, f32, (out_unit, lambda s, i: s)), ((channels, 1), f32, (out_unit, lambda s, i: s))],
            "rows",
            ids=ids,
            parts=[(sum(sizes[:i]), size) for i, size in enumerate(sizes)],
        )
        gated_sum = gated_sum[:, 0]
    else:
        g_out = jnp.concatenate([part[place_of].astype(f32).reshape(channels, -1) for part in out_parts], axis=1)
        gated_sum = jnp.sum(g_out * out_weight.astype(f32), axis=1)

    norm_grad = norm_sum / norm_gain.astype(f32)
    gated_grad = gated_sum / gated_gain.astype(f32)

    got = tail[:, share + heads : share + heads + extra]
    tap_grads = jnp.concatenate(
        [
            got[:, : 5 * per].reshape(nf, 5, channels).transpose(1, 0, 2).reshape(5, inner),
            got[:, 5 * per : 5 * per + 5, :share].transpose(1, 0, 2).reshape(5, 2 * state),
        ],
        axis=1,
    )
    tap_grads = lax.dynamic_slice_in_dim(tap_grads, me * conv_own, conv_own, 1)
    head_grads = lax.dynamic_index_in_dim(got, me, 0, False)[5 * per + 5 :, :heads]

    mixed = (valid * (inputs + branch)).astype(bf16)

    w_share = lax.dynamic_slice_in_dim(w_conv, channels + me * share, share, 0)
    w_last = jnp.concatenate([w_share, w_conv[cw : cw + lanes - share]], axis=0)

    def back(dz, w):
        return lax.dot_general(dz, w, (((2,), (0,)), ((), ())), preferred_element_type=f32)

    bn = back(dgate, w_gate) + back(late_conv[..., :channels], w_conv[:channels]) + back(late_conv[..., channels:], w_last)
    bn = to_owner(bn, "fsdp", turn=True, first=tied_bufs)
    (input_grad,) = call(
        input_kernel,
        1,
        [(bn, None), (norm_all, None), (tokens[0], None), (cotangent[0], None), (valid, None)],
        [((seg, width), f32, None)],
        "input",
        ids=ids,
        owners=nf,
    )
    return (
        mixed[None],
        input_grad[None],
        norm_grad,
        g_in.T,
        tap_grads[:4],
        tap_grads[4],
        head_grads[0],
        head_grads[1],
        head_grads[2],
        gated_grad,
        g_out,
    )


def solution(mesh):
    whole, rows = P("fsdp", "seq", None), P("fsdp", None)
    one, columns = P("fsdp"), P(None, "fsdp")
    return jax.shard_map(
        per_device,
        mesh=mesh,
        in_specs=(whole, one, one, rows, columns, one, one, one, one, one, rows, whole),
        out_specs=(whole, whole, one, rows, columns, one, one, one, one, one, rows),
        check_vma=False,
    )
```
